32 devices in a mesh: group: 2 (over x), replica: 16 (over z, y, core).
Axes of the slice: x: 2, y: 2, z: 4, core: 2. Of those that a mesh axis runs over, the one named last changes fastest.
Arguments:
- tokens: bfloat16 [32, 1024, 768], P(('group', 'replica')), may hold values from -6 to 6
- lengths: int32 [32], P(('group', 'replica')), may hold values from 256 to 1024, as said below
- w_qkv: bfloat16 [768, 2304], P('group'), may hold values from -0.21875 to 0.21875
- w_out: bfloat16 [768, 768], P('group'), may hold values from -4 to 4
- gain_one: bfloat16 [768], P('group'), may hold values from 0.25 to 1.75
- w_in: bfloat16 [768, 2304], P('group'), may hold values from -0.21875 to 0.21875
- w_down: bfloat16 [1152, 768], P('group'), may hold values from -0.1875 to 0.1875
- gain_two: bfloat16 [768], P('group'), may hold values from 0.25 to 1.75
- cotangent: bfloat16 [32, 1024, 768], P(('group', 'replica')), may hold values from -6 to 6
Outputs:
- output: bfloat16 [32, 1024, 768], P(('group', 'replica'))
- grad_tokens: float32 [32, 1024, 768], P(('group', 'replica'))
- grad_qkv: float32 [768, 2304], P('group')
- grad_out: float32 [768, 768], P('group')
- grad_gain_one: float32 [768], P('group')
- grad_in: float32 [768, 2304], P('group')
- grad_down: float32 [1152, 768], P('group')
- grad_gain_two: float32 [768], P('group')
The draws below stay inside these ranges and needn't reach their ends.
Inputs may be any that keep to these rules, and one draw needn't show every extreme that they name: Slots 0 to lengths - 1 of a sequence hold tokens, the rest are padding; some sequence has exactly 1024 valid slots and some exactly 256.
All inputs are finite; a program needn't handle non-finite values.
Results may differ from the reference program's by a relative error of at most 0.018.
Values may be sent and summed in bfloat16 or wider, within the bound.
No kernel may reach another device: no remote copies, remote signals or barrier semaphores. Data moves between devices by JAX's collectives and lax.ppermute only.
A program may use at most 192 MiB of HBM per device.

```python
import math
import jax
import jax.numpy as jnp
from jax import lax

HEADS = 12
HEAD_DIM = 64
D = 768
FF = 1152
SEQ = 1024
BATCH = 32


def draw_lengths(key, part):
    first, second, third = jax.random.split(key, 3)
    base = jax.random.randint(first, (BATCH,), SEQ // 4, SEQ + 1)
    longest = jax.random.randint(second, (), 0, BATCH)
    shortest = (longest + 1 + jax.random.randint(third, (), 0, BATCH - 1)) % BATCH
    places = jnp.arange(BATCH)
    base = jnp.where(places == longest, SEQ, base)
    base = jnp.where(places == shortest, SEQ // 4, base)
    return base.astype(jnp.int32)


def steps_of(rng, dims, cuts, low, top_value):
    level = 1.0
    for dim, blocks in cuts:
        heights = jax.random.uniform(jax.random.fold_in(jax.random.fold_in(rng, 6), dim), (blocks,), jnp.float32, low / len(cuts), top_value / len(cuts))
        level = level * jnp.repeat(jnp.exp(heights), dims[dim] // blocks).reshape((-1,) + (1,) * (len(dims) - 1 - dim))
    return level


def normal_values(own_key, shape, deviation, limit, pieces=(), kind=jnp.bfloat16):
    loudness = steps_of(own_key, shape, pieces, -0.22, 0.18) if pieces else 1.0
    array = jax.random.normal(own_key, shape, jnp.float32) * deviation * loudness
    return jnp.minimum(jnp.maximum(array, -limit), limit).astype(kind)


def setup_inputs(seed: int = 0) -> dict:
    streams_of = jax.random.split(jax.random.key(seed), 10)
    tokens = normal_values(streams_of[0], (BATCH, SEQ, D), 1.0, 6.0, ((0, 32),))
    lengths = draw_lengths(jax.random.fold_in(streams_of[9], 71), 0)
    w_qkv = normal_values(streams_of[2], (D, 3 * D), D ** -0.5, 0.21875, ((0, 2),))
    w_out = normal_values(streams_of[3], (D, D), 2 ** -0.5, 4.0, ((0, 2),))
    gain_one = jnp.clip(1.0 + 0.15 * jax.random.normal(streams_of[4], (D,), jnp.float32), 0.25, 1.75).astype(jnp.bfloat16)
    w_in = normal_values(streams_of[5], (D, 2 * FF), D ** -0.5, 0.21875, ((0, 2),))
    w_down = normal_values(streams_of[6], (FF, D), FF ** -0.5, 0.1875, ((0, 2),))
    gain_two = jnp.clip(1.0 + 0.15 * jax.random.normal(streams_of[7], (D,), jnp.float32), 0.25, 1.75).astype(jnp.bfloat16)
    cotangent = normal_values(streams_of[8], (BATCH, SEQ, D), 1.0, 6.0, ((0, 32),))
    return {"tokens": tokens, "lengths": lengths, "w_qkv": w_qkv, "w_out": w_out, "gain_one": gain_one, "w_in": w_in, "w_down": w_down, "gain_two": gain_two, "cotangent": cotangent}


@jax.custom_vjp
def low(v):
    return lax.optimization_barrier(v.astype(jnp.bfloat16)).astype(jnp.float32)

@jax.custom_vjp
def low_back(v):
    return v

def low_keep(v):
    return (low(v), None)

def low_pass(kept, grad):
    return (grad,)

def back_keep(v):
    return (v, None)

def back_low(kept, grad):
    return (low(grad),)
low.defvjp(low_keep, low_pass)
low_back.defvjp(back_keep, back_low)
theta_base = 160000.0
norm_eps = 1e-05

def matmul(left, right):
    return jnp.dot(left, right, precision=lax.Precision.HIGHEST, preferred_element_type=jnp.float32)

def normed(field, gain):
    center = field - lax.optimization_barrier(jnp.mean(field, axis=-1, keepdims=True))
    spread = lax.optimization_barrier(jnp.mean(center * center, axis=-1, keepdims=True))
    return center * lax.rsqrt(spread + norm_eps) * gain

def rotary(field):
    half = HEAD_DIM // 2
    freq = jnp.exp(-math.log(theta_base) * 2.0 * jnp.arange(half, dtype=jnp.float32) / HEAD_DIM)
    angle = jnp.arange(SEQ, dtype=jnp.float32)[:, None] * freq[None, :]
    cosine = jnp.cos(angle)
    sine = jnp.sin(angle)
    first = field[..., :half]
    second = field[..., half:]
    return jnp.concatenate([first * cosine - second * sine, second * cosine + first * sine], axis=-1)

def attend(query, key_rows, values, valid):
    scale = 1.0 / math.sqrt(HEAD_DIM)
    scores = jnp.einsum('qd,kd->qk', query, key_rows, precision=lax.Precision.HIGHEST) * scale
    scores = low_back(scores)
    scores = jnp.where(valid[None, :], scores, -1e+30)
    top = lax.optimization_barrier(jnp.max(scores, axis=1, keepdims=True))
    weights = jnp.exp(scores - top)
    weights = weights / lax.optimization_barrier(jnp.sum(weights, axis=1, keepdims=True))
    return matmul(low(weights), values)

def layer(field, w_qkv, w_out, gain_one, w_in, w_down, gain_two, valid):
    first_in = low(normed(field, gain_one))
    merged = low_back(matmul(first_in, w_qkv))
    parts = merged.reshape(SEQ, 3, HEADS, HEAD_DIM).transpose(1, 2, 0, 3)
    query = low(rotary(parts[0]))
    key_rows = low(rotary(parts[1]))
    values = low(parts[2])

    def one_head(item):
        return attend(item[0], item[1], item[2], valid)
    heads = lax.map(jax.checkpoint(one_head), (query, key_rows, values))
    mixed = low(low_back(heads.transpose(1, 0, 2).reshape(SEQ, D)))
    middle = field + low_back(matmul(mixed, w_out))
    second_in = low(normed(middle, gain_two))
    upward = low_back(matmul(second_in, w_in))
    activ = low(jax.nn.gelu(upward[:, :FF], approximate=False) * upward[:, FF:])
    result = middle + matmul(activ, w_down)
    return jnp.where(valid[:, None], result, 0.0)

def reference(tokens, lengths, w_qkv, w_out, gain_one, w_in, w_down, gain_two, cotangent):
    weights = tuple((w.astype(jnp.float32) for w in (w_qkv, w_out, gain_one, w_in, w_down, gain_two)))
    start = tuple((jnp.zeros(w.shape, jnp.float32) for w in weights))

    def per_sequence(carry, item):
        field, length, cot = item
        valid = jnp.arange(SEQ, dtype=jnp.int32) < length

        def forward(inputs, *params):
            return layer(inputs, *params, valid)
        result, pull = jax.vjp(forward, field.astype(jnp.float32), *weights)
        grads = pull(cot.astype(jnp.float32))
        carry = tuple((c + g for c, g in zip(carry, grads[1:])))
        return (carry, (result.astype(jnp.bfloat16), grads[0]))
    sums, (output, grad_tokens) = lax.scan(per_sequence, start, (tokens, lengths, cotangent))
    return (output, grad_tokens, sums[0], sums[1], sums[2], sums[3], sums[4], sums[5])
```

```python
import math

import jax
import jax.numpy as jnp
from jax import lax
from jax.sharding import PartitionSpec as P

HEADS = 12
HEAD_DIM = 64


theta_base = 160000.0
norm_eps = 1e-05


def normed(field, gain):
    center = field - jnp.mean(field, axis=-1, keepdims=True)
    spread = jnp.mean(center * center, axis=-1, keepdims=True)
    return center * lax.rsqrt(spread + norm_eps) * gain


def rotary(field):
    half = HEAD_DIM // 2
    length = field.shape[1]
    freq = jnp.exp(-math.log(theta_base) * 2.0 * jnp.arange(half, dtype=jnp.float32) / HEAD_DIM)
    angle = jnp.arange(length, dtype=jnp.float32)[:, None] * freq[None, :]
    cosine = jnp.cos(angle)
    sine = jnp.sin(angle)
    first = field[..., :half]
    second = field[..., half:]
    return jnp.concatenate(
        [first * cosine - second * sine, second * cosine + first * sine], axis=-1
    )


def rotate_both(query, key_rows):
    return (rotary(query), rotary(key_rows))


def geglu(upward):
    half = upward.shape[1] // 2
    return jax.nn.gelu(upward[:, :half], approximate=False) * upward[:, half:]


def inner(left, right):
    return lax.dot_general(
        left, right, (((0,), (0,)), ((), ())), preferred_element_type=jnp.float32
    )


def outer(left, right):
    return lax.dot_general(
        left, right, (((1,), (1,)), ((), ())), preferred_element_type=jnp.float32
    )


def swap_replica(field, bit):
    count = lax.axis_size("replica")
    return lax.ppermute(field, "replica", [(i, i ^ bit) for i in range(count)])


def swap_group(field):
    return lax.ppermute(field, "group", [(0, 1), (1, 0)])


def pick(field, index, axis):
    size = field.shape[axis] // 2
    return lax.dynamic_slice_in_dim(field, index * size, size, axis)


def in_order(mine, other, index, axis):
    return jnp.where(
        index == 0,
        jnp.concatenate([mine, other], axis=axis),
        jnp.concatenate([other, mine], axis=axis),
    )


def add_low(left, right):
    return (left.astype(jnp.float32) + right.astype(jnp.float32)).astype(jnp.bfloat16)


def other_rows(send, core):
    fetched = swap_group(send)
    return fetched, swap_replica(fetched, 1)


def reduce_unit(send, keep, group, replica):
    count = lax.axis_size("replica")
    total = add_low(keep, swap_replica(send, 1))
    total = add_low(pick(total, group, 0), swap_group(pick(total, 1 - group, 0)))[0]
    split = []
    bit = 2
    while bit < count:
        at = (replica // bit) % 2
        if total.shape[0] % 32 == 0:
            total = add_low(pick(total, at, 0), swap_replica(pick(total, 1 - at, 0), bit))
            split.append((bit, at))
        else:
            total = add_low(total, swap_replica(total, bit))
        bit *= 2
    for bit, at in reversed(split):
        total = in_order(total, swap_replica(total, bit), at, 0)
    return total, swap_replica(total, 1)


def on_device(tokens, lengths, w_qkv, w_out, gain_one, w_in, w_down, gain_two, cotangent):
    field = tokens[0].astype(jnp.float32)
    length = field.shape[0]
    width = field.shape[1]
    scale = 1.0 / math.sqrt(HEAD_DIM)
    valid = jnp.arange(length, dtype=jnp.int32) < lengths[0]
    group = lax.axis_index("group")
    replica = lax.axis_index("replica")
    core = replica % 2
    gain_rows = jnp.zeros((16, w_qkv.shape[1] // 2), jnp.bfloat16)
    gain_rows = lax.dynamic_update_slice(gain_rows, gain_one[None], (0, 0))
    qkv_send = jnp.concatenate([pick(w_qkv, core, 1), gain_rows], axis=0)
    rest_rows = jnp.zeros((16, w_out.shape[1] // 2), jnp.bfloat16)
    rest_rows = lax.dynamic_update_slice(rest_rows, gain_two[None], (0, 0))
    wide = w_out.shape[1] // 2
    in_half = pick(w_in, core, 1)
    rest_send = jnp.concatenate(
        [pick(w_out, core, 1), pick(w_down, core, 1)]
        + [in_half[:, i * wide : (i + 1) * wide] for i in range(3)]
        + [rest_rows],
        axis=0,
    )
    qkv_parts = other_rows(qkv_send, core)
    rest_parts = other_rows(rest_send, core)
    n_own = w_qkv.shape[0]
    n_down = w_down.shape[0]
    cut = [0, n_own, n_own + n_down, 2 * n_own + n_down, 3 * n_own + n_down, 4 * n_own + n_down]

    def whole(own, parts):
        return in_order(own, in_order(parts[0], parts[1], core, 1), group, 0)

    qkv_full = whole(w_qkv, [part[:n_own] for part in qkv_parts])
    gain_first = in_order(gain_one, qkv_parts[0][n_own, :n_own], group, 0)
    out_full = whole(w_out, [part[: cut[1]] for part in rest_parts])
    down_full = whole(w_down, [part[cut[1] : cut[2]] for part in rest_parts])
    in_full = whole(
        w_in,
        [
            jnp.concatenate([part[cut[i] : cut[i + 1]] for i in (2, 3, 4)], axis=1)
            for part in rest_parts
        ],
    )
    gain_second = in_order(gain_two, rest_parts[0][cut[5], :n_own], group, 0)
    first_f, first_pull = jax.vjp(normed, field, gain_first.astype(jnp.float32))
    first_in = first_f.astype(jnp.bfloat16)
    merged = jnp.dot(first_in, qkv_full, preferred_element_type=jnp.float32)
    parts = merged.reshape(length, 3, HEADS, HEAD_DIM).transpose(1, 2, 0, 3)
    (query_f, key_f), rotate_pull = jax.vjp(rotate_both, parts[0], parts[1])
    query = query_f.astype(jnp.bfloat16)
    key_rows = key_f.astype(jnp.bfloat16)
    values = parts[2].astype(jnp.bfloat16)

    def masked_scores(head_query, head_keys):
        scores = (
            jnp.einsum("qd,kd->qk", head_query, head_keys, preferred_element_type=jnp.float32)
            * scale
        )
        return jnp.where(valid[None, :], scores, -1e30)

    def forward_head(item):
        head_query, head_keys, head_values = item
        scores = masked_scores(head_query, head_keys)
        top = jnp.max(scores, axis=1, keepdims=True)
        weights = jnp.exp(scores - top)
        total = jnp.sum(weights, axis=1, keepdims=True)
        weights = weights / total
        result = jnp.einsum(
            "qk,kd->qd",
            weights.astype(jnp.bfloat16),
            head_values,
            preferred_element_type=jnp.float32,
        )
        return (result, top[:, 0] + jnp.log(total[:, 0]))

    heads, log_totals = lax.map(forward_head, (query, key_rows, values))
    mixed = heads.transpose(1, 0, 2).reshape(length, width).astype(jnp.bfloat16)
    middle = field + jnp.dot(mixed, out_full, preferred_element_type=jnp.float32)
    second_f, second_pull = jax.vjp(normed, middle, gain_second.astype(jnp.float32))
    second_in = second_f.astype(jnp.bfloat16)
    upward = jnp.dot(second_in, in_full, preferred_element_type=jnp.float32)
    activ_f, activ_pull = jax.vjp(geglu, upward)
    activ = activ_f.astype(jnp.bfloat16)
    result = middle + jnp.dot(activ, down_full, preferred_element_type=jnp.float32)
    output = jnp.where(valid[:, None], result, 0.0).astype(jnp.bfloat16)[None]
    d_out = jnp.where(valid[:, None], cotangent[0], jnp.zeros((), jnp.bfloat16))
    grad_down = inner(activ, d_out)
    d_activ = outer(d_out, down_full)
    (d_up,) = activ_pull(d_activ)
    d_up = d_up.astype(jnp.bfloat16)
    grad_in = inner(second_in, d_up)
    d_second = outer(d_up, in_full)
    d_middle_norm, grad_gain_two = second_pull(d_second)
    d_middle = d_out.astype(jnp.float32) + d_middle_norm
    d_middle_low = d_middle.astype(jnp.bfloat16)
    grad_out = inner(mixed, d_middle_low)
    d_mixed = outer(d_middle_low, out_full).astype(jnp.bfloat16)
    d_heads = d_mixed.reshape(length, HEADS, HEAD_DIM).transpose(1, 0, 2)

    def backward_head(item):
        head_query, head_keys, head_values, head_grad, log_total = item
        scores = masked_scores(head_query, head_keys)
        weights = jnp.where(valid[None, :], jnp.exp(scores - log_total[:, None]), 0.0)
        d_values = jnp.einsum(
            "qk,qd->kd", weights.astype(jnp.bfloat16), head_grad, preferred_element_type=jnp.float32
        )
        d_weights = jnp.einsum(
            "qd,kd->qk", head_grad, head_values, preferred_element_type=jnp.float32
        )
        d_scores = weights * (d_weights - jnp.sum(weights * d_weights, axis=1, keepdims=True))
        d_scores = d_scores.astype(jnp.bfloat16)
        d_query = (
            jnp.einsum("qk,kd->qd", d_scores, head_keys, preferred_element_type=jnp.float32) * scale
        )
        d_keys = (
            jnp.einsum("qk,qd->kd", d_scores, head_query, preferred_element_type=jnp.float32)
            * scale
        )
        return (d_query, d_keys, d_values)

    d_query_r, d_keys_r, d_values = lax.map(
        backward_head, (query, key_rows, values, d_heads, log_totals)
    )
    d_query, d_keys = rotate_pull((d_query_r, d_keys_r))
    d_merged = (
        jnp.stack([d_query, d_keys, d_values]).transpose(2, 0, 1, 3).reshape(length, 3 * width)
    )
    d_merged = d_merged.astype(jnp.bfloat16)
    grad_qkv = inner(first_in, d_merged)
    d_first = outer(d_merged, qkv_full)
    d_field_norm, grad_gain_one = first_pull(d_first)
    grad_tokens = (d_middle + d_field_norm)[None]
    def unit_of(fields):
        halves = []
        for half in (1 - core, core):
            parts = []
            for field in fields:
                part = pick(field.astype(jnp.bfloat16), half, 1)
                rows = part.shape[0] // 2
                for i in range(part.shape[1] // wide):
                    parts.append(part[:, i * wide : (i + 1) * wide].reshape(2, rows, wide))
            used = sum(part.shape[1] for part in parts)
            filled = -(-used // 128) * 128
            if filled > used:
                parts.append(jnp.zeros((2, filled - used, wide), jnp.bfloat16))
            halves.append(jnp.concatenate(parts, axis=1))
        return halves

    def gain_unit(field):
        return jnp.zeros((2 * n_own, 2 * wide), jnp.float32).at[:2, :n_own].set(field.reshape(2, n_own))

    def spread(result, fields):
        outs = []
        at = 0
        for field in fields:
            rows = field.shape[0] // 2
            count = field.shape[1] // 2 // wide
            sides = []
            for side in result:
                sides.append(
                    jnp.concatenate(
                        [side[at + i * rows : at + (i + 1) * rows] for i in range(count)], axis=1
                    )
                )
            outs.append(in_order(sides[0], sides[1], core, 1).astype(jnp.float32))
            at += rows * count
        return outs

    early = [grad_down, grad_in, grad_out]
    early_sum = reduce_unit(*unit_of(early), group, replica)
    late = [grad_qkv]
    late_sum = reduce_unit(*unit_of(late), group, replica)
    grad_down, grad_in, grad_out = spread(early_sum, early)
    (grad_qkv,) = spread(late_sum, late)
    gains = jnp.stack([grad_gain_one, grad_gain_two])
    gains = lax.psum(gains, ("group", "replica"))
    gains = lax.dynamic_slice_in_dim(gains, group * n_own, n_own, 1)
    return (
        output,
        grad_tokens,
        grad_qkv,
        grad_out,
        gains[0],
        grad_in,
        grad_down,
        gains[1],
    )


def solution(mesh):
    in_specs = (
        P(("group", "replica"), None, None),
        P(("group", "replica")),
        P("group", None),
        P("group", None),
        P("group"),
        P("group", None),
        P("group", None),
        P("group"),
        P(("group", "replica"), None, None),
    )
    out_specs = (
        P(("group", "replica"), None, None),
        P(("group", "replica"), None, None),
        P("group", None),
        P("group", None),
        P("group"),
        P("group", None),
        P("group", None),
        P("group"),
    )
    return jax.shard_map(
        on_device, mesh=mesh, in_specs=in_specs, out_specs=out_specs, check_vma=False
    )
```

```python
import functools
import math

import jax
import jax.numpy as jnp
import numpy as np
from jax import lax
from jax.experimental import pallas as pl
from jax.experimental.pallas import tpu as pltpu
from jax.sharding import PartitionSpec as P

HEADS = 12
HEAD_DIM = 64
theta_base = 160000.0
norm_eps = 1e-05
LOG2E = 1.4426950408889634
LN2 = 0.6931471805599453
F32 = jnp.float32
BF16 = jnp.bfloat16
PAIR = 2 * HEAD_DIM
GROUP_HEADS = 4
SPAN = GROUP_HEADS * HEAD_DIM
NEG = -1e30
LOCAL = pl.BlockSpec(memory_space=pltpu.VMEM)
SCALAR = pl.BlockSpec(memory_space=pltpu.SMEM)
FAR = pl.BlockSpec(memory_space=pl.ANY)


def dot_nn(a, b):
    return lax.dot_general(a, b, (((1,), (0,)), ((), ())), preferred_element_type=F32)


def dot_nt(a, b):
    return lax.dot_general(a, b, (((1,), (1,)), ((), ())), preferred_element_type=F32)


def dot_tn(a, b):
    return lax.dot_general(a, b, (((0,), (0,)), ((), ())), preferred_element_type=F32)


def angle_tables(length):
    half = HEAD_DIM // 2
    freq = np.exp(-math.log(theta_base) * 2.0 * np.arange(half, dtype=np.float64) / HEAD_DIM)
    angle = np.arange(length, dtype=np.float64)[:, None] * freq.astype(np.float32).astype(np.float64)[None]
    cosine = np.cos(angle)
    sine = np.sin(angle)
    cos_rows = np.concatenate([cosine] * 4, axis=1).astype(np.float32)
    sin_rows = np.concatenate([-sine, sine, -sine, sine], axis=1).astype(np.float32)
    return cos_rows, sin_rows


def swap_halves(field):
    half = HEAD_DIM // 2
    lane = lax.broadcasted_iota(jnp.int32, field.shape, 1)
    return jnp.where(
        (lane // half) % 2 == 0, pltpu.roll(field, PAIR - half, 1), pltpu.roll(field, half, 1)
    )


def erf_exp(u):
    return lax.erf(u * (1.0 / math.sqrt(2.0))), jnp.exp(-0.5 * u * u)


LIMITS = {"attend": 12, "middle": 24, "early_in": 8, "early_rest": 8, "pull": 12, "late": 6, "last": 12, "spread": 12}
LENGTHS = {"attend": 17, "middle": 28, "early_in": 3, "early_rest": 3, "pull": 15, "late": 2, "last": 8, "spread": 3, "halves": 1}


def cost(name):
    return pl.CostEstimate(flops=LENGTHS[name] * 1_000_000_000, transcendentals=0, bytes_accessed=0)


def start_all(copies):
    for copy in copies:
        copy.start()


def attend_kernel(*refs, chunk, first, step):
    if first:
        (info_ref, tok_ref, gain_ref, w_ref, mine_ref, other_ref, cos_ref, sin_ref,
         qkv_ref, mixed_ref, lse_ref, full_ref, h_ref, vt_ref, qa_ref, ka_ref, row_ref, sems) = refs
    else:
        (info_ref, h_ref, w_ref, mine_ref, other_ref, cos_ref, sin_ref,
         qkv_ref, mixed_ref, lse_ref, full_ref, vt_ref, qa_ref, ka_ref, sems) = refs
    rows_all = h_ref.shape[0]
    own = w_ref.shape[0]
    valid = info_ref[0]
    group = info_ref[1]
    core = info_ref[2]
    width = 3 * SPAN // 2
    there = pl.ds(pl.multiple_of(group * own, own), own)
    away = pl.ds(pl.multiple_of((1 - group) * own, own), own)
    copies = []
    for i in range(3):
        copies.append(
            pltpu.make_async_copy(
                w_ref.at[:, pl.ds(i * HEADS * HEAD_DIM + chunk * SPAN, SPAN)],
                full_ref.at[there, pl.ds(i * SPAN, SPAN)],
                sems.at[i],
            )
        )
    for i, (part, side) in enumerate(((mine_ref, core), (other_ref, 1 - core))):
        copies.append(
            pltpu.make_async_copy(
                part.at[pl.ds(0, own)],
                full_ref.at[away, pl.ds(pl.multiple_of(side * width, width), width)],
                sems.at[3 + i],
            )
        )
    if first:
        copies.append(pltpu.make_async_copy(mine_ref.at[pl.ds(own, 16)], row_ref, sems.at[5]))
    start_all(copies)
    if first:
        copies[-1].wait()
        copies = copies[:-1]
        gain_own = gain_ref[...].astype(F32)
        gain_away = row_ref[0:1, :].astype(F32)
        gain = jnp.where(
            group == 0,
            jnp.concatenate([gain_own, gain_away], axis=1),
            jnp.concatenate([gain_away, gain_own], axis=1),
        )
        for at in range(0, rows_all, step):
            field = tok_ref[at : at + step, :].astype(F32)
            center = field - jnp.mean(field, axis=1, keepdims=True)
            spread = jnp.mean(center * center, axis=1, keepdims=True)
            h_ref[at : at + step, :] = (center * lax.rsqrt(spread + norm_eps) * gain).astype(BF16)
    for copy in copies:
        copy.wait()
    lane = lax.broadcasted_iota(jnp.int32, (step, PAIR), 1)
    for at in range(0, rows_all, step):
        rows = pl.ds(at, step)
        merged = dot_nn(h_ref[rows, :], full_ref[...])
        cosine = cos_ref[rows, :]
        sine = sin_ref[rows, :]
        row = lax.broadcasted_iota(jnp.int32, (step, PAIR), 0) + at
        bias = jnp.where(row < valid, 0.0, NEG)
        for pair in range(SPAN // PAIR):
            left = pair * PAIR
            q = merged[:, left : left + PAIR]
            k = merged[:, SPAN + left : SPAN + left + PAIR]
            v = merged[:, 2 * SPAN + left : 2 * SPAN + left + PAIR].astype(BF16)
            q = (q * cosine + swap_halves(q) * sine) * (LOG2E / math.sqrt(HEAD_DIM))
            k = k * cosine + swap_halves(k) * sine
            qkv_ref[rows, left : left + PAIR] = q.astype(BF16)
            qkv_ref[rows, SPAN + left : SPAN + left + PAIR] = k.astype(BF16)
            qkv_ref[rows, 2 * SPAN + left : 2 * SPAN + left + PAIR] = v
            vt_ref[pair, :, rows] = v.T
            for side in range(2):
                mine = (lane // HEAD_DIM) == side
                spare = lane == (1 - side) * HEAD_DIM
                qa_ref[2 * pair + side, rows, :] = jnp.where(
                    mine, q, jnp.where(spare, 1.0, 0.0)
                ).astype(BF16)
                ka_ref[2 * pair + side, rows, :] = jnp.where(
                    mine, k, jnp.where(spare, bias, 0.0)
                ).astype(BF16)
    ones = jnp.ones((16, rows_all), BF16)

    def body(block, _):
        rows = pl.ds(pl.multiple_of(block * step, step), step)
        for pair in range(SPAN // PAIR):
            outs = []
            for side in range(2):
                head = 2 * pair + side
                scores = dot_nt(ka_ref[head], qa_ref[head, rows, :])
                top = jnp.max(scores, axis=0, keepdims=True)
                weights = jnp.exp2(scores - top).astype(BF16)
                values = jnp.concatenate(
                    [vt_ref[pair, side * HEAD_DIM : (side + 1) * HEAD_DIM, :], ones], axis=0
                )
                result = dot_nn(values, weights)
                total = result[HEAD_DIM : HEAD_DIM + 1, :]
                outs.append(result[:HEAD_DIM, :] / total)
                lse_ref[head : head + 1, rows] = top + jnp.log2(total)
            mixed_ref[rows, pair * PAIR : (pair + 1) * PAIR] = (
                jnp.concatenate(outs, axis=0).T.astype(BF16)
            )
        return 0

    lax.fori_loop(0, rows_all // step, body, 0)


def attend(info, source, gain, w, parts, cosine, sine, chunk, step=256):
    rows = source.shape[0]
    width = 2 * w.shape[0]
    first = gain is not None
    out_shape = [
        jax.ShapeDtypeStruct((rows, 3 * SPAN), BF16),
        jax.ShapeDtypeStruct((rows, SPAN), BF16),
        jax.ShapeDtypeStruct((8, rows), F32),
        jax.ShapeDtypeStruct((width, 3 * SPAN), BF16),
    ]
    scratch = [
        pltpu.VMEM((SPAN // PAIR, PAIR, rows), BF16),
        pltpu.VMEM((GROUP_HEADS, rows, PAIR), BF16),
        pltpu.VMEM((GROUP_HEADS, rows, PAIR), BF16),
    ]
    inputs = [info, source]
    specs = [SCALAR, LOCAL]
    if first:
        out_shape.append(jax.ShapeDtypeStruct((rows, width), BF16))
        scratch.append(pltpu.VMEM((16, 3 * SPAN // 2), BF16))
        inputs.append(gain)
        specs.append(LOCAL)
    inputs += [w, *parts, cosine, sine]
    specs += [FAR, FAR, FAR, LOCAL, LOCAL]
    scratch.append(pltpu.SemaphoreType.DMA((6,)))
    return pl.pallas_call(
        functools.partial(attend_kernel, chunk=chunk, first=first, step=step),
        out_shape=tuple(out_shape),
        in_specs=specs,
        out_specs=tuple([LOCAL] * len(out_shape)),
        scratch_shapes=scratch,
        compiler_params=pltpu.CompilerParams(vmem_limit_bytes=LIMITS["attend"] << 20),
        cost_estimate=cost("attend"),
        name=f"attend_{chunk}",
    )(*inputs)


def middle_kernel(
    info_ref, tok_ref, mix0_ref, mix1_ref, mix2_ref, cot_ref, gain_ref,
    wo_ref, wi_ref, wd_ref, mine_ref, other_ref,
    out_ref, dx_ref, dxl_ref, dm_ref, h_ref, act_ref, du_ref,
    fo_ref, fi_ref, fd_ref, row_ref, sems, *, step,
):
    rows_all, width = tok_ref.shape
    own = wo_ref.shape[0]
    down = wd_ref.shape[0]
    half = width // 2
    hidden = fd_ref.shape[0]
    valid = info_ref[0]
    group = info_ref[1]
    core = info_ref[2]

    def at(start, size):
        return pl.ds(pl.multiple_of(start, size), size)

    copies = [
        pltpu.make_async_copy(wo_ref, fo_ref.at[at(group * own, own)], sems.at[0]),
        pltpu.make_async_copy(wi_ref, fi_ref.at[at(group * own, own)], sems.at[1]),
        pltpu.make_async_copy(wd_ref, fd_ref.at[at(group * down, down)], sems.at[2]),
        pltpu.make_async_copy(mine_ref.at[pl.ds(4 * own + down, 16)], row_ref, sems.at[3]),
    ]
    for i, (part, side) in enumerate(((mine_ref, core), (other_ref, 1 - core))):
        base = 4 + 5 * i
        copies.append(
            pltpu.make_async_copy(
                part.at[pl.ds(0, own)],
                fo_ref.at[at((1 - group) * own, own), at(side * half, half)],
                sems.at[base],
            )
        )
        copies.append(
            pltpu.make_async_copy(
                part.at[pl.ds(own, down)],
                fd_ref.at[at((1 - group) * down, down), at(side * half, half)],
                sems.at[base + 1],
            )
        )
        for j in range(3):
            copies.append(
                pltpu.make_async_copy(
                    part.at[pl.ds(own + down + j * own, own)],
                    fi_ref.at[at((1 - group) * own, own), at(side * 3 * half + j * half, half)],
                    sems.at[base + 2 + j],
                )
            )
    start_all(copies)
    for copy in copies:
        copy.wait()
    gain_own = gain_ref[...].astype(F32)
    gain_away = row_ref[0:1, :].astype(F32)
    gain = jnp.where(
        group == 0,
        jnp.concatenate([gain_own, gain_away], axis=1),
        jnp.concatenate([gain_away, gain_own], axis=1),
    )

    def body(block, _):
        rows = pl.ds(pl.multiple_of(block * step, step), step)
        mixed = jnp.concatenate([mix0_ref[rows, :], mix1_ref[rows, :], mix2_ref[rows, :]], axis=1)
        x1 = tok_ref[rows, :].astype(F32) + dot_nn(mixed, fo_ref[...])
        center = x1 - jnp.mean(x1, axis=1, keepdims=True)
        rate = lax.rsqrt(jnp.mean(center * center, axis=1, keepdims=True) + norm_eps)
        unit = center * rate
        h2 = (unit * gain).astype(BF16)
        h_ref[rows, :] = h2
        row = lax.broadcasted_iota(jnp.int32, (step, 1), 0) + block * step
        keep = row < valid
        up = dot_nn(h2, fi_ref[...])
        turned = up[:, :hidden]
        gate = up[:, hidden:]
        curve, bell = erf_exp(turned)
        share = 0.5 * (1.0 + curve)
        bent = turned * share
        act = (bent * gate).astype(BF16)
        act_ref[rows, :] = jnp.where(keep, act, jnp.zeros((), BF16))
        result = x1 + dot_nn(act, fd_ref[...])
        out_ref[rows, :] = jnp.where(keep, result, 0.0).astype(BF16)
        dy = jnp.where(keep, cot_ref[rows, :], jnp.zeros((), BF16))
        d_act = dot_nt(dy, fd_ref[...])
        slope = share + turned * bell * (1.0 / math.sqrt(2.0 * math.pi))
        d_up = jnp.concatenate([d_act * gate * slope, d_act * bent], axis=1).astype(BF16)
        du_ref[rows, :] = d_up
        e = dot_nt(d_up, fi_ref[...]) * gain
        d_x1 = dy.astype(F32) + rate * (
            e
            - jnp.mean(e, axis=1, keepdims=True)
            - unit * jnp.mean(e * unit, axis=1, keepdims=True)
        )
        dx_ref[rows, :] = d_x1
        low = d_x1.astype(BF16)
        dxl_ref[rows, :] = low
        dm_ref[rows, :] = dot_nt(low, fo_ref[...]).astype(BF16)
        return 0

    lax.fori_loop(0, rows_all // step, body, 0)


def middle(info, tokens, mixed, cotangent, gain, w_out, w_in, w_down, parts, step=256):
    rows, width = tokens.shape
    hidden = 2 * w_down.shape[0]
    shapes = [
        ((rows, width), BF16),
        ((rows, width), F32),
        ((rows, width), BF16),
        ((rows, width), BF16),
        ((rows, width), BF16),
        ((rows, hidden), BF16),
        ((rows, 2 * hidden), BF16),
    ]
    return pl.pallas_call(
        functools.partial(middle_kernel, step=step),
        out_shape=tuple(jax.ShapeDtypeStruct(*s) for s in shapes),
        in_specs=[SCALAR] + [LOCAL] * 6 + [FAR] * 5,
        out_specs=tuple([LOCAL] * len(shapes)),
        scratch_shapes=[
            pltpu.VMEM((width, width), BF16),
            pltpu.VMEM((width, 2 * hidden), BF16),
            pltpu.VMEM((hidden, width), BF16),
            pltpu.VMEM((16, width // 2), BF16),
            pltpu.SemaphoreType.DMA((14,)),
        ],
        compiler_params=pltpu.CompilerParams(vmem_limit_bytes=LIMITS["middle"] << 20),
        cost_estimate=cost("middle"),
        name="middle",
    )(info, tokens, *mixed, cotangent, gain, w_out, w_in, w_down, *parts)


def early_in_kernel(half_ref, h_ref, du_ref, unit_ref):
    own = h_ref.shape[1] // 2
    for group in range(2):
        left = h_ref[:, group * own : (group + 1) * own]
        for j in range(3):
            unit_ref[group, j * own : (j + 1) * own, :] = dot_tn(
                left, du_ref[:, j * own : (j + 1) * own]
            ).astype(BF16)


def early_rest_kernel(half_ref, act_ref, cot_ref, m0_ref, m1_ref, m2_ref, dx_ref, unit_ref):
    own = dx_ref.shape[1]
    down = act_ref.shape[1] // 2
    zero = jnp.zeros((unit_ref.shape[1] - own - down, own), BF16)
    mixed = [ref[...] for ref in (m0_ref, m1_ref, m2_ref)]
    grad_out = jnp.concatenate([dot_tn(m, dx_ref[...]) for m in mixed], axis=0).astype(BF16)
    grad_down = dot_tn(act_ref[...], cot_ref[...]).astype(BF16)
    for group in range(2):
        unit_ref[group, :own, :] = grad_out[group * own : (group + 1) * own]
        unit_ref[group, own : own + down, :] = grad_down[group * down : (group + 1) * down]
        unit_ref[group, own + down :, :] = zero


def same(rows, count):
    return pl.BlockSpec((rows, count), lambda i, s: (0, 0))


def side(rows, count):
    return pl.BlockSpec((rows, count), lambda i, s: (0, s[0]))


def per_half(kernel, half, inputs, specs, shape, name):
    return pl.pallas_call(
        kernel,
        out_shape=jax.ShapeDtypeStruct(shape, BF16),
        grid_spec=pltpu.PrefetchScalarGridSpec(
            num_scalar_prefetch=1,
            grid=(1,),
            in_specs=specs,
            out_specs=pl.BlockSpec(shape, lambda i, s: (0, 0, 0)),
        ),
        compiler_params=pltpu.CompilerParams(vmem_limit_bytes=LIMITS[name] << 20),
        cost_estimate=cost(name),
        name=name,
    )(half, *inputs)


def early_in(half, h2, d_up):
    rows, width = h2.shape
    own = width // 2
    return per_half(
        early_in_kernel,
        half,
        (h2, d_up),
        [same(rows, width), side(rows, 3 * own)],
        (2, 3 * own, own),
        "early_in",
    )


def early_rest(half, act, cotangent, mixed, dx_low):
    rows, hidden = act.shape
    own = dx_low.shape[1] // 2
    filled = -(-(own + hidden // 2) // 128) * 128
    return per_half(
        early_rest_kernel,
        half,
        (act, cotangent, *mixed, dx_low),
        [same(rows, hidden), side(rows, own)] + [same(rows, SPAN)] * 3 + [side(rows, own)],
        (2, filled, own),
        "early_rest",
    )


def late_kernel(half_ref, h_ref, *refs):
    own = h_ref.shape[1] // 2
    unit_ref = refs[-1]
    for group in range(2):
        left = h_ref[:, group * own : (group + 1) * own]
        for i, d_ref in enumerate(refs[:-1]):
            unit_ref[group, i * own : (i + 1) * own, :] = dot_tn(left, d_ref[...]).astype(BF16)


def late(half, h1, d_qkv):
    rows, width = h1.shape
    own = width // 2
    return per_half(
        late_kernel,
        half,
        (h1, *d_qkv),
        [same(rows, width)] + [side(rows, 3 * SPAN // 2)] * len(d_qkv),
        (2, own * len(d_qkv), 3 * SPAN // 2),
        "late",
    )


def half_of(w_ref, chunk, core):
    space = HEADS * HEAD_DIM
    half = SPAN // 2
    left = chunk * SPAN
    query = w_ref[:, left : left + SPAN]
    key = w_ref[:, space + left : space + left + SPAN]
    value = w_ref[:, 2 * space + left : 2 * space + left + SPAN]
    low = jnp.concatenate([query, key[:, :half]], axis=1)
    high = jnp.concatenate([key[:, half:], value], axis=1)
    return jnp.where(core == 0, low, high)


def pack_first_kernel(info_ref, w_ref, gain_ref, send_ref):
    own = w_ref.shape[0]
    send_ref[:own, :] = half_of(w_ref, 0, info_ref[2])
    send_ref[own:, :] = jnp.broadcast_to(gain_ref[...], (16, send_ref.shape[1]))


def pack_first(info, w_qkv, gain):
    return pl.pallas_call(
        pack_first_kernel,
        out_shape=jax.ShapeDtypeStruct((w_qkv.shape[0] + 16, 3 * SPAN // 2), BF16),
        in_specs=[SCALAR, LOCAL, LOCAL],
        out_specs=LOCAL,
        compiler_params=pltpu.CompilerParams(vmem_limit_bytes=8 << 20),
        name="pack_first",
    )(info, w_qkv, gain)


def pack_kernel(info_ref, w_ref, wo_ref, wi_ref, wd_ref, gain_ref, s1_ref, s2_ref, rest_ref):
    core = info_ref[2]
    own = wo_ref.shape[0]
    down = wd_ref.shape[0]
    half = wo_ref.shape[1] // 2
    s1_ref[...] = half_of(w_ref, 1, core)
    s2_ref[...] = half_of(w_ref, 2, core)

    def part(ref, i):
        left = i * half
        right = ref.shape[1] // 2 + i * half
        return jnp.where(core == 0, ref[:, left : left + half], ref[:, right : right + half])

    rest_ref[:own, :] = part(wo_ref, 0)
    rest_ref[own : own + down, :] = part(wd_ref, 0)
    for j in range(3):
        at = own + down + j * own
        rest_ref[at : at + own, :] = part(wi_ref, j)
    at = own + down + 3 * own
    rest_ref[at:, :] = jnp.broadcast_to(gain_ref[...], (16, half))


def pack(info, w_qkv, w_out, w_in, w_down, gain):
    own = w_qkv.shape[0]
    wide = 3 * SPAN // 2
    return pl.pallas_call(
        pack_kernel,
        out_shape=(
            jax.ShapeDtypeStruct((own, wide), BF16),
            jax.ShapeDtypeStruct((own, wide), BF16),
            jax.ShapeDtypeStruct((4 * own + w_down.shape[0] + 16, wide), BF16),
        ),
        in_specs=[SCALAR] + [LOCAL] * 5,
        out_specs=(LOCAL,) * 3,
        compiler_params=pltpu.CompilerParams(vmem_limit_bytes=12 << 20),
        name="pack",
    )(info, w_qkv, w_out, w_in, w_down, gain)


def halves_kernel(at_ref, mine_ref, in_ref, away_ref, here_ref, *, axis):
    size = here_ref.shape[axis]
    at = at_ref[0]

    def part(ref, index):
        start = pl.multiple_of(index * size, size)
        if axis == 0:
            return ref[pl.ds(start, size)].astype(F32)
        return ref[:, pl.ds(start, size)].astype(F32)

    away_ref[...] = (part(mine_ref, 1 - at) + part(in_ref, 1 - at)).astype(BF16)
    here_ref[...] = (part(mine_ref, at) + part(in_ref, at)).astype(BF16)


def halves(mine, received, at, axis):
    shape = list(mine.shape)
    shape[axis] //= 2
    out = jax.ShapeDtypeStruct(tuple(shape), BF16)
    return pl.pallas_call(
        functools.partial(halves_kernel, axis=axis),
        out_shape=(out, out),
        in_specs=[SCALAR, LOCAL, LOCAL],
        out_specs=(LOCAL, LOCAL),
        compiler_params=pltpu.CompilerParams(vmem_limit_bytes=8 << 20),
        cost_estimate=cost("halves"),
        name="halves",
    )(at.astype(jnp.int32)[None], mine, received)


def last_kernel(info_ref, tok_ref, gain_ref, away_ref, d0_ref, d1_ref, d2_ref, w0_ref, w1_ref, w2_ref, dx_ref, out_ref, *, step):
    group = info_ref[1]
    gain_own = gain_ref[...].astype(F32)
    gain_away = away_ref[0:1, :].astype(F32)
    gain = jnp.where(
        group == 0,
        jnp.concatenate([gain_own, gain_away], axis=1),
        jnp.concatenate([gain_away, gain_own], axis=1),
    )
    for at in range(0, tok_ref.shape[0], step):
        rows = slice(at, at + step)
        field = tok_ref[rows, :].astype(F32)
        center = field - jnp.mean(field, axis=1, keepdims=True)
        rate = lax.rsqrt(jnp.mean(center * center, axis=1, keepdims=True) + norm_eps)
        unit = center * rate
        e = dot_nt(d0_ref[rows, :], w0_ref[...])
        e += dot_nt(d1_ref[rows, :], w1_ref[...])
        e += dot_nt(d2_ref[rows, :], w2_ref[...])
        e *= gain
        out_ref[rows, :] = dx_ref[rows, :] + rate * (
            e
            - jnp.mean(e, axis=1, keepdims=True)
            - unit * jnp.mean(e * unit, axis=1, keepdims=True)
        )


def last(info, tokens, gain, away, d_qkv, full, d_x1, step=256):
    return pl.pallas_call(
        functools.partial(last_kernel, step=step),
        out_shape=jax.ShapeDtypeStruct(d_x1.shape, F32),
        in_specs=[SCALAR] + [LOCAL] * 10,
        out_specs=LOCAL,
        compiler_params=pltpu.CompilerParams(vmem_limit_bytes=LIMITS["last"] << 20),
        cost_estimate=cost("last"),
        name="last",
    )(info, tokens, gain, away, *d_qkv, *full, d_x1)


def row_of(column):
    return jnp.broadcast_to(column, (column.shape[0], 128)).T[0:1, :]


def spread_early_kernel(
    info_ref, ma_ref, mb_ref, oa_ref, ob_ref, w_ref, gain_ref, in_ref, out_ref, down_ref, dg_ref
):
    core = info_ref[2]
    own = out_ref.shape[0]
    down = down_ref.shape[0]
    half = out_ref.shape[1] // 2

    def part_of(i, mine_ref, other_ref, start, size):
        mine = mine_ref[start : start + size, :].astype(F32)
        other = other_ref[start : start + size, :].astype(F32)
        return jnp.where(core == i, mine, other)

    total = jnp.zeros((own, 1), F32)
    for i in range(2):
        for j in range(3):
            at = (3 * i + j) * half
            part = part_of(i, ma_ref, oa_ref, j * own, own)
            in_ref[:, at : at + half] = part
            total += jnp.sum(part * w_ref[:, at : at + half].astype(F32), axis=1, keepdims=True)
        out_ref[:, i * half : (i + 1) * half] = part_of(i, mb_ref, ob_ref, 0, own)
        down_ref[:, i * half : (i + 1) * half] = part_of(i, mb_ref, ob_ref, own, down)
    dg_ref[...] = (row_of(total) / gain_ref[...].astype(F32))[0]


def spread_early(info, mine, other, w_in, gain, down):
    own = w_in.shape[0]
    return pl.pallas_call(
        spread_early_kernel,
        out_shape=(
            jax.ShapeDtypeStruct(w_in.shape, F32),
            jax.ShapeDtypeStruct((own, 2 * own), F32),
            jax.ShapeDtypeStruct((down, 2 * own), F32),
            jax.ShapeDtypeStruct((own,), F32),
        ),
        in_specs=[SCALAR] + [LOCAL] * 6,
        out_specs=(LOCAL,) * 4,
        compiler_params=pltpu.CompilerParams(vmem_limit_bytes=LIMITS["spread"] << 20),
        cost_estimate=cost("spread"),
        name="spread_early",
    )(info, *mine, *other, w_in, gain)


def spread_late_kernel(info_ref, m01_ref, o01_ref, m2_ref, o2_ref, w_ref, gain_ref, out_ref, dg_ref):
    core = info_ref[2]
    own = w_ref.shape[0]
    total = jnp.zeros((own, 1), F32)
    for chunk in range(3):
        mine_ref, other_ref = (m2_ref, o2_ref) if chunk == 2 else (m01_ref, o01_ref)
        start = own if chunk == 1 else 0
        mine = mine_ref[start : start + own, :].astype(F32)
        other = other_ref[start : start + own, :].astype(F32)
        whole = jnp.concatenate(
            [jnp.where(core == 0, mine, other), jnp.where(core == 0, other, mine)], axis=1
        )
        for i in range(3):
            at = i * HEADS * HEAD_DIM + chunk * SPAN
            part = whole[:, i * SPAN : (i + 1) * SPAN]
            out_ref[:, at : at + SPAN] = part
            total += jnp.sum(part * w_ref[:, at : at + SPAN].astype(F32), axis=1, keepdims=True)
    dg_ref[...] = (row_of(total) / gain_ref[...].astype(F32))[0]


def spread_late(info, first, second, w_qkv, gain):
    own = w_qkv.shape[0]
    return pl.pallas_call(
        spread_late_kernel,
        out_shape=(jax.ShapeDtypeStruct(w_qkv.shape, F32), jax.ShapeDtypeStruct((own,), F32)),
        in_specs=[SCALAR] + [LOCAL] * 6,
        out_specs=(LOCAL, LOCAL),
        compiler_params=pltpu.CompilerParams(vmem_limit_bytes=LIMITS["spread"] << 20),
        cost_estimate=cost("spread"),
        name="spread_late",
    )(info, *first, *second, w_qkv, gain)


def pull_kernel(
    length_ref, qkv_ref, mixed_ref, dm_ref, lse_ref, cos_ref, sin_ref, out_ref,
    qa_ref, ka_ref, kt_ref, dv_ref, dk_ref, *, chunk, step,
):
    length = qkv_ref.shape[0]
    lane = lax.broadcasted_iota(jnp.int32, (step, PAIR), 1)
    for at in range(0, length, step):
        rows = pl.ds(at, step)
        row = lax.broadcasted_iota(jnp.int32, (step, PAIR), 0) + at
        bias = jnp.where(row < length_ref[0], 0.0, NEG).astype(BF16)
        one = jnp.ones((), BF16)
        zero = jnp.zeros((), BF16)
        for pair in range(SPAN // PAIR):
            left = pair * PAIR
            q = qkv_ref[rows, left : left + PAIR]
            k = qkv_ref[rows, SPAN + left : SPAN + left + PAIR]
            kt_ref[pair, :, rows] = k.T
            for side in range(2):
                mine = (lane // HEAD_DIM) == side
                spare = lane == (1 - side) * HEAD_DIM
                qa_ref[2 * pair + side, rows, :] = jnp.where(mine, q, jnp.where(spare, one, zero))
                ka_ref[2 * pair + side, rows, :] = jnp.where(mine, k, jnp.where(spare, bias, zero))
    dv_ref[...] = jnp.zeros_like(dv_ref)
    dk_ref[...] = jnp.zeros_like(dk_ref)
    half_rows = lax.broadcasted_iota(jnp.int32, (8, PAIR), 0)
    half_lane = lax.broadcasted_iota(jnp.int32, (8, PAIR), 1)
    chooser = jnp.where(half_lane // HEAD_DIM == half_rows, 1.0, 0.0).astype(BF16)

    def body(block, _):
        rows = pl.ds(pl.multiple_of(block * step, step), step)
        for pair in range(SPAN // PAIR):
            left = pair * PAIR
            dm = dm_ref[rows, chunk * SPAN + left : chunk * SPAN + left + PAIR]
            product = dm.astype(F32) * mixed_ref[rows, left : left + PAIR].astype(F32)
            high = product.astype(BF16)
            low = (product - high.astype(F32)).astype(BF16)
            delta = dot_nt(chooser, high) + dot_nt(chooser, low)
            q = qkv_ref[rows, left : left + PAIR]
            v = qkv_ref[:, 2 * SPAN + left : 2 * SPAN + left + PAIR]
            outs = []
            for side in range(2):
                head = 2 * pair + side
                mine = (lane // HEAD_DIM) == side
                zero = jnp.zeros((), BF16)
                dms = jnp.where(mine, dm, zero)
                qs = jnp.where(mine, q, zero)
                scores = dot_nt(ka_ref[head], qa_ref[head, rows, :])
                weights = jnp.exp2(scores - lse_ref[head : head + 1, rows])
                d_weights = dot_nt(v, dms)
                d_scores = (weights * (d_weights - delta[side : side + 1, :])).astype(BF16)
                weights = weights.astype(BF16)
                dv_ref[pair] += dot_nn(weights, dms)
                dk_ref[pair] += dot_nn(d_scores, qs)
                outs.append(dot_nn(kt_ref[pair, side * HEAD_DIM : (side + 1) * HEAD_DIM, :], d_scores))
            dq = jnp.concatenate(outs, axis=0).T * (1.0 / math.sqrt(HEAD_DIM))
            dq = dq * cos_ref[rows, :] - swap_halves(dq) * sin_ref[rows, :]
            out_ref[rows, left : left + PAIR] = dq.astype(BF16)
        return 0

    lax.fori_loop(0, length // step, body, 0)
    for at in range(0, length, step):
        rows = pl.ds(at, step)
        for pair in range(SPAN // PAIR):
            left = pair * PAIR
            dk = dk_ref[pair, rows, :] * LN2
            dk = dk * cos_ref[rows, :] - swap_halves(dk) * sin_ref[rows, :]
            out_ref[rows, SPAN + left : SPAN + left + PAIR] = dk.astype(BF16)
            out_ref[rows, 2 * SPAN + left : 2 * SPAN + left + PAIR] = dv_ref[pair, rows, :].astype(BF16)


def pull(length, qkv, mixed, d_mixed, lse, cosine, sine, chunk, step=256):
    rows = qkv.shape[0]
    return pl.pallas_call(
        functools.partial(pull_kernel, chunk=chunk, step=step),
        out_shape=jax.ShapeDtypeStruct((rows, 3 * SPAN), BF16),
        in_specs=[SCALAR] + [LOCAL] * 6,
        out_specs=LOCAL,
        scratch_shapes=[
            pltpu.VMEM((GROUP_HEADS, rows, PAIR), BF16),
            pltpu.VMEM((GROUP_HEADS, rows, PAIR), BF16),
            pltpu.VMEM((SPAN // PAIR, PAIR, rows), BF16),
            pltpu.VMEM((SPAN // PAIR, rows, PAIR), F32),
            pltpu.VMEM((SPAN // PAIR, rows, PAIR), F32),
        ],
        compiler_params=pltpu.CompilerParams(vmem_limit_bytes=LIMITS["pull"] << 20),
        cost_estimate=cost("pull"),
        name=f"pull_{chunk}",
    )(length, qkv, mixed, d_mixed, lse, cosine, sine)


def swap_replica(field, bit):
    count = lax.axis_size("replica")
    return lax.ppermute(field, "replica", [(i, i ^ bit) for i in range(count)])


def swap_group(field):
    return lax.ppermute(field, "group", [(0, 1), (1, 0)])


def pick(field, index, axis):
    size = field.shape[axis] // 2
    return lax.dynamic_slice_in_dim(field, index * size, size, axis)


def in_order(mine, other, index, axis):
    return jnp.where(
        index == 0,
        jnp.concatenate([mine, other], axis=axis),
        jnp.concatenate([other, mine], axis=axis),
    )


def add_low(left, right):
    return (left.astype(F32) + right.astype(F32)).astype(BF16)


def hold(value, *others):
    return lax.optimization_barrier((value, others))[0]


def further_bits():
    bits = []
    bit = 4
    while bit < lax.axis_size("replica"):
        bits.append(bit)
        bit *= 2
    return bits


def on_device(tokens, lengths, w_qkv, w_out, gain_one, w_in, w_down, gain_two, cotangent):
    rows = tokens.shape[1]
    group = lax.axis_index("group")
    replica = lax.axis_index("replica")
    core = replica % 2
    second = (replica // 2) % 2
    info = jnp.stack([lengths[0], group, core]).astype(jnp.int32)
    cos_rows, sin_rows = angle_tables(rows)
    cosine, sine = jnp.asarray(cos_rows), jnp.asarray(sin_rows)

    field = tokens[0]
    cot = cotangent[0]
    qkv, mixed, lse, full = [None] * 3, [None] * 3, [None] * 3, [None] * 3
    far0 = swap_group(pack_first(info, w_qkv, gain_one[None]))
    send1, send2, send_rest = pack(info, w_qkv, w_out, w_in, w_down, gain_two[None])
    send1, send_rest = hold((send1, send_rest), far0)
    far1 = swap_group(send1)
    far_rest = swap_group(send_rest)
    parts0 = (far0, swap_replica(far0, 1))
    qkv[0], mixed[0], lse[0], full[0], h1 = attend(
        info, hold(field, send1, send_rest), gain_one[None], w_qkv, parts0, cosine, sine, 0
    )
    far1, send2 = hold((far1, send2), mixed[0])
    far2 = swap_group(send2)
    parts1 = (far1, swap_replica(far1, 1))
    qkv[1], mixed[1], lse[1], full[1] = attend(
        info, hold(h1, send2), None, w_qkv, parts1, cosine, sine, 1
    )
    far2 = hold(far2, mixed[1])
    parts2 = (far2, swap_replica(far2, 1))
    qkv[2], mixed[2], lse[2], full[2] = attend(info, h1, None, w_qkv, parts2, cosine, sine, 2)
    far_rest = hold(far_rest, mixed[2])
    parts_rest = (far_rest, swap_replica(far_rest, 1))
    output, d_x1, dx_low, d_mixed, h2, act, d_up = middle(
        info, field, mixed, cot, gain_two[None], w_out, w_in, w_down, parts_rest
    )
    mine = core.astype(jnp.int32)[None]
    theirs = 1 - mine

    a_send = early_in(theirs, h2, d_up)
    a_in = swap_replica(a_send, 1)
    b_send = early_rest(theirs, act, hold(cot, a_send), mixed, dx_low)
    b_in = swap_replica(b_send, 1)
    a_mine = early_in(mine, hold(h2, b_send), d_up)
    a_in = hold(a_in, a_mine)
    a_away, a_here = halves(a_mine, a_in, group, 0)
    a_in = swap_group(a_away)
    b_mine = early_rest(mine, act, hold(cot, a_away), mixed, dx_low)
    b_in = hold(b_in, b_mine)
    b_away, b_here = halves(b_mine, b_in, second, 1)
    b_in = swap_replica(b_away, 2)

    d_qkv = [None] * 3
    d_qkv[0] = pull(info, qkv[0], mixed[0], hold(d_mixed, b_away), lse[0], cosine, sine, 0)
    a_in, b_in = hold((a_in, b_in), d_qkv[0])
    a_away, a_here = halves(a_here[0], a_in[0], second, 0)
    a_in = swap_replica(a_away, 2)
    b_away, b_here = halves(b_here, b_in, group, 0)
    b_in = swap_group(b_away)
    d_qkv[1] = pull(info, qkv[1], mixed[1], hold(d_mixed, a_away, b_away), lse[1], cosine, sine, 1)
    a_in, b_in = hold((a_in, b_in), d_qkv[1])
    early_mine = jnp.concatenate([a_here, b_here[0]], axis=0)
    early_in_sum = jnp.concatenate([a_in, b_in[0]], axis=0)
    bits = further_bits()
    at = (replica // bits[0]) % 2
    e_away, e_here = halves(early_mine, early_in_sum, at, 0)
    e_in = swap_replica(e_away, bits[0])

    l_send = late(theirs, hold(h1, e_away), d_qkv[:2])
    l_in = swap_replica(l_send, 1)
    l_mine = late(mine, hold(h1, l_send), d_qkv[:2])
    l_in = hold(l_in, l_mine)
    l_away, l_here = halves(l_mine, l_in, group, 0)
    l_in = swap_group(l_away)
    d_qkv[2] = pull(info, qkv[2], mixed[2], hold(d_mixed, l_away), lse[2], cosine, sine, 2)
    e_in, l_in = hold((e_in, l_in), d_qkv[2])
    e_sum = add_low(e_here, e_in)
    e_in = [swap_replica(e_sum, bits[1])]
    l_away, l_here = halves(l_here[0], l_in[0], second, 0)
    l_in = swap_replica(l_away, 2)

    m_send = late(theirs, hold(h1, e_sum, l_away), d_qkv[2:])
    m_in = swap_replica(m_send, 1)
    m_mine = late(mine, hold(h1, m_send), d_qkv[2:])
    m_in = hold(m_in, m_mine)
    m_away, m_here = halves(m_mine, m_in, group, 0)
    m_in = swap_group(m_away)
    grad_tokens = last(
        info, hold(field, m_away), gain_one[None], far0[w_qkv.shape[0] :], d_qkv, full, d_x1
    )

    m_in = hold(m_in, grad_tokens)

    def across(mine_, received, todo):
        total = add_low(mine_, received)
        for bit in todo:
            total = add_low(total, swap_replica(total, bit))
        return total

    e_in = e_in[0]
    e_sum = across(e_sum, e_in, bits[2:])
    l_sum = across(l_here, l_in, bits)
    m_away, m_here = halves(m_here[0], m_in[0], second, 0)
    m_sum = across(m_here, swap_replica(m_away, 2), bits)
    e_sum = in_order(e_sum, swap_replica(e_sum, bits[0]), at, 0)
    e_other = swap_replica(e_sum, 2)
    cut = a_here.shape[0]
    whole_a = in_order(e_sum[:cut], e_other[:cut], second, 0)
    whole_b = in_order(e_sum[cut:], e_other[cut:], second, 0)
    l_sum = in_order(l_sum, swap_replica(l_sum, 2), second, 0)
    m_sum = in_order(m_sum, swap_replica(m_sum, 2), second, 0)
    grad_in, grad_out, grad_down, grad_two = spread_early(
        info,
        (whole_a, whole_b),
        (swap_replica(whole_a, 1), swap_replica(whole_b, 1)),
        w_in,
        gain_two[None],
        w_down.shape[0],
    )
    grad_qkv, grad_one = spread_late(
        info, (l_sum, swap_replica(l_sum, 1)), (m_sum, swap_replica(m_sum, 1)), w_qkv, gain_one[None]
    )
    return (
        output[None],
        grad_tokens[None],
        grad_qkv,
        grad_out,
        grad_one,
        grad_in,
        grad_down,
        grad_two,
    )


def solution(mesh):
    both = P(("group", "replica"), None, None)
    rows = P("group", None)
    vector = P("group")
    return jax.shard_map(
        on_device,
        mesh=mesh,
        in_specs=(both, P(("group", "replica")), rows, rows, vector, rows, rows, vector, both),
        out_specs=(both, both, rows, rows, vector, rows, rows, vector),
        check_vma=False,
    )
```

```python
import functools
import math

import jax
import jax.numpy as jnp
import numpy as np
from jax import lax
from jax.experimental import pallas as pl
from jax.experimental.pallas import tpu as pltpu
from jax.sharding import PartitionSpec as P

HEADS = 12
HEAD_DIM = 64
theta_base = 160000.0
norm_eps = 1e-05
LOG2E = 1.4426950408889634
LN2 = 0.6931471805599453
F32 = jnp.float32
BF16 = jnp.bfloat16
PAIR = 2 * HEAD_DIM
GROUP_HEADS = 4
SPAN = GROUP_HEADS * HEAD_DIM
WIDE = 3 * PAIR
NEG = -1e30
LOCAL = pl.BlockSpec(memory_space=pltpu.VMEM)
SCALAR = pl.BlockSpec(memory_space=pltpu.SMEM)
FAR = pl.BlockSpec(memory_space=pl.ANY)
STORED = pl.BlockSpec(memory_space=pltpu.HBM)


def dot_nn(a, b):
    return lax.dot_general(a, b, (((1,), (0,)), ((), ())), preferred_element_type=F32)


def dot_nt(a, b):
    return lax.dot_general(a, b, (((1,), (1,)), ((), ())), preferred_element_type=F32)


def dot_tn(a, b):
    return lax.dot_general(a, b, (((0,), (0,)), ((), ())), preferred_element_type=F32)


def angle_tables(length):
    half = HEAD_DIM // 2
    freq = np.exp(-math.log(theta_base) * 2.0 * np.arange(half, dtype=np.float64) / HEAD_DIM)
    angle = np.arange(length, dtype=np.float64)[:, None] * freq.astype(np.float32).astype(np.float64)[None]
    cosine = np.cos(angle)
    sine = np.sin(angle)
    cos_rows = np.concatenate([cosine] * 4, axis=1).astype(np.float32)
    sin_rows = np.concatenate([-sine, sine, -sine, sine], axis=1).astype(np.float32)
    return cos_rows, sin_rows


def swap_halves(field):
    half = HEAD_DIM // 2
    lane = lax.broadcasted_iota(jnp.int32, field.shape, 1)
    return jnp.where(
        (lane // half) % 2 == 0, pltpu.roll(field, PAIR - half, 1), pltpu.roll(field, half, 1)
    )


def erf_exp(u):
    return lax.erf(u * (1.0 / math.sqrt(2.0))), jnp.exp(-0.5 * u * u)


LIMITS = {"attend": 16, "middle": 27, "early_in": 8, "early_rest": 8, "pull": 12, "late": 6, "last": 12, "spread": 12}
LENGTHS = {"attend": 3, "middle": 28, "early_in": 3, "early_rest": 3, "pull": 5, "late": 2, "last": 8, "spread": 3, "halves": 1}


def cost(name):
    return pl.CostEstimate(flops=LENGTHS[name] * 1_000_000_000, transcendentals=0, bytes_accessed=0)


def skip(kernel, at, count):
    return lambda *refs: kernel(*refs[:at], *refs[at + count :])


def start_all(copies):
    for copy in copies:
        copy.start()


def attend_kernel(*refs, chunk, first, step):
    if first:
        (info_ref, tok_ref, gain_ref, w_ref, mine_ref, other_ref, turn_ref,
         *outs_far, mixed_ref, h_ref,
         qkva_ref, qkvb_ref, full_ref, lse_ref, vt_ref, qa_ref, ka_ref, s_ref, row_ref, sems) = refs
    else:
        (info_ref, h_ref, w_ref, mine_ref, other_ref, turn_ref,
         *outs_far, mixed_ref,
         qkva_ref, qkvb_ref, full_ref, lse_ref, vt_ref, qa_ref, ka_ref, s_ref, sems) = refs
    stores = [
        pltpu.make_async_copy(near, far, sems.at[9 + i])
        for i, (near, far) in enumerate(zip((qkva_ref, qkvb_ref, full_ref, lse_ref), outs_far))
    ]
    rows_all = h_ref.shape[0]
    own = w_ref.shape[0]
    valid = info_ref[0]
    group = info_ref[1]
    core = info_ref[2]
    there = pl.ds(pl.multiple_of(group * own, own), own)
    away = pl.ds(pl.multiple_of((1 - group) * own, own), own)
    copies = []
    for pair in range(2):
        for i in range(3):
            copies.append(
                pltpu.make_async_copy(
                    w_ref.at[:, pl.ds(i * HEADS * HEAD_DIM + chunk * SPAN + pair * PAIR, PAIR)],
                    full_ref.at[there, pl.ds(pair * WIDE + i * PAIR, PAIR)],
                    sems.at[3 * pair + i],
                )
            )
    for i, (part, side) in enumerate(((mine_ref, core), (other_ref, 1 - core))):
        copies.append(
            pltpu.make_async_copy(
                part.at[pl.ds(0, own)],
                full_ref.at[away, pl.ds(pl.multiple_of(side * WIDE, WIDE), WIDE)],
                sems.at[6 + i],
            )
        )
    if first:
        copies.append(pltpu.make_async_copy(mine_ref.at[pl.ds(own, 16)], row_ref, sems.at[8]))
    start_all(copies)
    if first:
        copies[-1].wait()
        copies = copies[:-1]
        gain_own = gain_ref[...].astype(F32)
        gain_away = row_ref[0:1, :].astype(F32)
        gain = jnp.where(
            group == 0,
            jnp.concatenate([gain_own, gain_away], axis=1),
            jnp.concatenate([gain_away, gain_own], axis=1),
        )
        for at in range(0, rows_all, step):
            field = tok_ref[at : at + step, :].astype(F32)
            center = field - jnp.mean(field, axis=1, keepdims=True)
            spread = jnp.mean(center * center, axis=1, keepdims=True)
            h_ref[at : at + step, :] = (center * lax.rsqrt(spread + norm_eps) * gain).astype(BF16)
    for copy in copies:
        copy.wait()
    stores[2].start()
    lane = lax.broadcasted_iota(jnp.int32, (step, PAIR), 1)

    def project(block, _):
        rows = pl.ds(pl.multiple_of(block * step, step), step)
        merged = dot_nn(h_ref[rows, :], full_ref[...])
        cosine = turn_ref[rows, :PAIR]
        sine = turn_ref[rows, PAIR:]
        row = lax.broadcasted_iota(jnp.int32, (step, PAIR), 0) + block * step
        bias = jnp.where(row < valid, 0.0, NEG)
        for pair, qkv_ref in enumerate((qkva_ref, qkvb_ref)):
            left = pair * WIDE
            q = merged[:, left : left + PAIR]
            k = merged[:, left + PAIR : left + 2 * PAIR]
            v = merged[:, left + 2 * PAIR : left + WIDE].astype(BF16)
            q = (q * cosine + swap_halves(q) * sine) * (LOG2E / math.sqrt(HEAD_DIM))
            k = k * cosine + swap_halves(k) * sine
            qkv_ref[rows, :PAIR] = q.astype(BF16)
            qkv_ref[rows, PAIR : 2 * PAIR] = k.astype(BF16)
            qkv_ref[rows, 2 * PAIR :] = v
            vt_ref[pair, :, rows] = v.T
            for side in range(2):
                mine = (lane // HEAD_DIM) == side
                spare = lane == (1 - side) * HEAD_DIM
                qa_ref[2 * pair + side, rows, :] = jnp.where(
                    mine, q, jnp.where(spare, 1.0, 0.0)
                ).astype(BF16)
                ka_ref[2 * pair + side, rows, :] = jnp.where(
                    mine, k, jnp.where(spare, bias, 0.0)
                ).astype(BF16)
        return 0

    blocks = rows_all // step
    lax.fori_loop(0, blocks, project, 0)
    start_all(stores[:2])
    ones = jnp.ones((16, step), BF16)

    def score(head, block, part, slot, top):
        rows = pl.ds(pl.multiple_of(block * step, step), step)
        keys = pl.ds(part * step, step)
        scores = dot_nt(ka_ref[head, keys, :], qa_ref[head, rows, :])
        s_ref[slot, keys, :] = scores
        here = jnp.max(scores, axis=0, keepdims=True)
        return here if top is None else jnp.maximum(top, here)

    def body(block, top):
        rows = pl.ds(pl.multiple_of(block * step, step), step)
        outs = []
        for head in range(GROUP_HEADS):
            pair, side = divmod(head, 2)
            slot = head % 2
            following = (head + 1) % GROUP_HEADS
            next_block = block if head + 1 < GROUP_HEADS else jnp.minimum(block + 1, blocks - 1)
            result = jnp.zeros((HEAD_DIM + 16, step), F32)
            next_top = None
            for part in range(blocks):
                keys = pl.ds(part * step, step)
                next_top = score(following, next_block, part, 1 - slot, next_top)
                weights = jnp.exp2(s_ref[slot, keys, :] - top).astype(BF16)
                values = jnp.concatenate(
                    [vt_ref[pair, side * HEAD_DIM : (side + 1) * HEAD_DIM, keys], ones], axis=0
                )
                result += dot_nn(values, weights)
            total = result[HEAD_DIM : HEAD_DIM + 1, :]
            outs.append(result[:HEAD_DIM, :] / total)
            lse_ref[head : head + 1, rows] = top + jnp.log2(total)
            top = next_top
            if side == 1:
                mixed_ref[rows, pair * PAIR : (pair + 1) * PAIR] = (
                    jnp.concatenate(outs[-2:], axis=0).T.astype(BF16)
                )
        return top

    top = None
    for part in range(blocks):
        top = score(0, 0, part, 0, top)
    lax.fori_loop(0, blocks, body, top)
    stores[3].start()
    for copy in stores:
        copy.wait()


def attend(info, source, gain, w, parts, turn, chunk, after=(), step=256):
    rows = source.shape[0]
    width = 2 * w.shape[0]
    first = gain is not None
    stored = [
        ((rows, WIDE), BF16),
        ((rows, WIDE), BF16),
        ((width, 3 * SPAN), BF16),
        ((8, rows), F32),
    ]
    out_shape = [jax.ShapeDtypeStruct(*s) for s in stored]
    out_shape.append(jax.ShapeDtypeStruct((rows, SPAN), BF16))
    scratch = [pltpu.VMEM(*s) for s in stored]
    scratch += [
        pltpu.VMEM((SPAN // PAIR, PAIR, rows), BF16),
        pltpu.VMEM((GROUP_HEADS, rows, PAIR), BF16),
        pltpu.VMEM((GROUP_HEADS, rows, PAIR), BF16),
        pltpu.VMEM((2, rows, step), F32),
    ]
    inputs = [info, source]
    specs = [SCALAR, LOCAL]
    if first:
        out_shape.append(jax.ShapeDtypeStruct((rows, width), BF16))
        scratch.append(pltpu.VMEM((16, WIDE), BF16))
        inputs.append(gain)
        specs.append(LOCAL)
    inputs += [w, *parts, turn]
    specs += [FAR, FAR, FAR, LOCAL]
    kernel = functools.partial(attend_kernel, chunk=chunk, first=first, step=step)
    kernel = skip(kernel, len(inputs), len(after))
    inputs += after
    specs += [FAR] * len(after)
    scratch.append(pltpu.SemaphoreType.DMA((13,)))
    return pl.pallas_call(
        kernel,
        out_shape=tuple(out_shape),
        in_specs=specs,
        out_specs=tuple([STORED] * 4 + [LOCAL] * (len(out_shape) - 4)),
        scratch_shapes=scratch,
        compiler_params=pltpu.CompilerParams(vmem_limit_bytes=LIMITS["attend"] << 20),
        cost_estimate=cost("attend"),
        name=f"attend_{chunk}",
    )(*inputs)


def middle_kernel(
    info_ref, tok_ref, mix0_ref, mix1_ref, mix2_ref, cot_ref, gain_ref,
    wo_ref, wi_ref, wd_ref, *refs, step,
):
    parts, refs = refs[:6], refs[6:]
    (out_ref, dx_far_ref, dxl_ref, dm_ref, h_ref, act_ref, du_ref,
     dx_ref, fo_ref, fi_ref, fd_ref, row_ref, sems) = refs
    rows_all, width = tok_ref.shape
    own = wo_ref.shape[0]
    down = wd_ref.shape[0]
    half = width // 2
    hidden = fd_ref.shape[0]
    valid = info_ref[0]
    group = info_ref[1]
    core = info_ref[2]

    def at(start, size):
        return pl.ds(pl.multiple_of(start, size), size)

    copies = [
        pltpu.make_async_copy(wo_ref, fo_ref.at[at(group * own, own)], sems.at[0]),
        pltpu.make_async_copy(wi_ref, fi_ref.at[at(group * own, own)], sems.at[1]),
        pltpu.make_async_copy(wd_ref, fd_ref.at[at(group * down, down)], sems.at[2]),
        pltpu.make_async_copy(parts[0].at[pl.ds(own + down, 16)], row_ref, sems.at[3]),
    ]
    sub = own // 2
    second = info_ref[3]
    for i, side in enumerate((core, 1 - core)):
        base = 4 + 8 * i
        part = parts[i]
        copies.append(
            pltpu.make_async_copy(
                part.at[pl.ds(0, own)],
                fo_ref.at[at((1 - group) * own, own), at(side * half, half)],
                sems.at[base],
            )
        )
        copies.append(
            pltpu.make_async_copy(
                part.at[pl.ds(own, down)],
                fd_ref.at[at((1 - group) * down, down), at(side * half, half)],
                sems.at[base + 1],
            )
        )
        for k, which in enumerate((second, 1 - second)):
            part = parts[2 + 2 * k + i]
            for j in range(3):
                copies.append(
                    pltpu.make_async_copy(
                        part.at[pl.ds(j * sub, sub)],
                        fi_ref.at[
                            at((1 - group) * own + which * sub, sub), at(side * 3 * half + j * half, half)
                        ],
                        sems.at[base + 2 + 3 * k + j],
                    )
                )
    start_all(copies)
    for copy in copies:
        copy.wait()
    gain_own = gain_ref[...].astype(F32)
    gain_away = row_ref[0:1, :].astype(F32)
    gain = jnp.where(
        group == 0,
        jnp.concatenate([gain_own, gain_away], axis=1),
        jnp.concatenate([gain_away, gain_own], axis=1),
    )

    def body(block, _):
        rows = pl.ds(pl.multiple_of(block * step, step), step)
        mixed = jnp.concatenate([mix0_ref[rows, :], mix1_ref[rows, :], mix2_ref[rows, :]], axis=1)
        x1 = tok_ref[rows, :].astype(F32) + dot_nn(mixed, fo_ref[...])
        center = x1 - jnp.mean(x1, axis=1, keepdims=True)
        rate = lax.rsqrt(jnp.mean(center * center, axis=1, keepdims=True) + norm_eps)
        unit = center * rate
        h2 = (unit * gain).astype(BF16)
        h_ref[rows, :] = h2
        row = lax.broadcasted_iota(jnp.int32, (step, 1), 0) + block * step
        keep = row < valid
        up = dot_nn(h2, fi_ref[...])
        turned = up[:, :hidden]
        gate = up[:, hidden:]
        curve, bell = erf_exp(turned)
        share = 0.5 * (1.0 + curve)
        bent = turned * share
        act = (bent * gate).astype(BF16)
        act_ref[rows, :] = jnp.where(keep, act, jnp.zeros((), BF16))
        result = x1 + dot_nn(act, fd_ref[...])
        out_ref[rows, :] = jnp.where(keep, result, 0.0).astype(BF16)
        dy = jnp.where(keep, cot_ref[rows, :], jnp.zeros((), BF16))
        d_act = dot_nt(dy, fd_ref[...])
        slope = share + turned * bell * (1.0 / math.sqrt(2.0 * math.pi))
        d_up = jnp.concatenate([d_act * gate * slope, d_act * bent], axis=1).astype(BF16)
        du_ref[rows, :] = d_up
        e = dot_nt(d_up, fi_ref[...]) * gain
        d_x1 = dy.astype(F32) + rate * (
            e
            - jnp.mean(e, axis=1, keepdims=True)
            - unit * jnp.mean(e * unit, axis=1, keepdims=True)
        )
        dx_ref[rows, :] = d_x1
        pltpu.make_async_copy(dx_ref.at[rows], dx_far_ref.at[rows], sems.at[20]).start()
        low = d_x1.astype(BF16)
        dxl_ref[rows, :] = low
        dm_ref[rows, :] = dot_nt(low, fo_ref[...]).astype(BF16)
        return 0

    lax.fori_loop(0, rows_all // step, body, 0)
    pltpu.make_async_copy(dx_ref, dx_far_ref, sems.at[20]).wait()


def middle(info, tokens, mixed, cotangent, gain, w_out, w_in, w_down, parts, step=256):
    rows, width = tokens.shape
    hidden = 2 * w_down.shape[0]
    shapes = [
        ((rows, width), BF16),
        ((rows, width), F32),
        ((rows, width), BF16),
        ((rows, width), BF16),
        ((rows, width), BF16),
        ((rows, hidden), BF16),
        ((rows, 2 * hidden), BF16),
    ]
    return pl.pallas_call(
        functools.partial(middle_kernel, step=step),
        out_shape=tuple(jax.ShapeDtypeStruct(*s) for s in shapes),
        in_specs=[SCALAR] + [LOCAL] * 6 + [FAR] * 9,
        out_specs=tuple(STORED if i == 1 else LOCAL for i in range(len(shapes))),
        scratch_shapes=[
            pltpu.VMEM(*shapes[1]),
            pltpu.VMEM((width, width), BF16),
            pltpu.VMEM((width, 2 * hidden), BF16),
            pltpu.VMEM((hidden, width), BF16),
            pltpu.VMEM((16, width // 2), BF16),
            pltpu.SemaphoreType.DMA((21,)),
        ],
        compiler_params=pltpu.CompilerParams(vmem_limit_bytes=LIMITS["middle"] << 20),
        cost_estimate=cost("middle"),
        name="middle",
    )(info, tokens, *mixed, cotangent, gain, w_out, w_in, w_down, *parts)


def early_in_kernel(half_ref, h_ref, du_ref, unit_ref, token_ref):
    token_ref[...] = jnp.zeros_like(token_ref)
    own = h_ref.shape[1] // 2
    side = pl.ds(pl.multiple_of(half_ref[0] * 3 * own, 3 * own), 3 * own)
    for group in range(2):
        whole = dot_tn(h_ref[:, group * own : (group + 1) * own], du_ref[:, side]).astype(BF16)
        for j in range(3):
            unit_ref[group, j * own : (j + 1) * own, :] = whole[:, j * own : (j + 1) * own]


def early_rest_kernel(
    half_ref, act_ref, cot_ref, m0_ref, m1_ref, m2_ref, dx_ref, unit_ref, token_ref
):
    token_ref[...] = jnp.zeros_like(token_ref)
    own = dx_ref.shape[1] // 2
    down = act_ref.shape[1] // 2
    side = pl.ds(pl.multiple_of(half_ref[0] * own, own), own)
    zero = jnp.zeros((unit_ref.shape[1] - own - down, own), BF16)
    mixed = [ref[...] for ref in (m0_ref, m1_ref, m2_ref)]
    low = dx_ref[:, side]
    grad_out = jnp.concatenate([dot_tn(m, low) for m in mixed], axis=0).astype(BF16)
    grad_down = dot_tn(act_ref[...], cot_ref[:, side]).astype(BF16)
    for group in range(2):
        unit_ref[group, :own, :] = grad_out[group * own : (group + 1) * own]
        unit_ref[group, own : own + down, :] = grad_down[group * down : (group + 1) * down]
        unit_ref[group, own + down :, :] = zero


def per_half(kernel, half, inputs, shape, name, after):
    return pl.pallas_call(
        skip(kernel, 1 + len(inputs), len(after)),
        out_shape=(jax.ShapeDtypeStruct(shape, BF16), jax.ShapeDtypeStruct((8, 128), F32)),
        in_specs=[SCALAR] + [LOCAL] * len(inputs) + [FAR] * len(after),
        out_specs=(LOCAL, LOCAL),
        compiler_params=pltpu.CompilerParams(vmem_limit_bytes=LIMITS[name] << 20),
        cost_estimate=cost(name),
        name=name,
    )(half, *inputs, *after)


def early_in(half, h2, d_up, after=()):
    own = h2.shape[1] // 2
    return per_half(early_in_kernel, half, (h2, d_up), (2, 3 * own, own), "early_in", after)


def early_rest(half, act, cotangent, mixed, dx_low, after=()):
    own = dx_low.shape[1] // 2
    filled = -(-(own + act.shape[1] // 2) // 128) * 128
    return per_half(
        early_rest_kernel,
        half,
        (act, cotangent, *mixed, dx_low),
        (2, filled, own),
        "early_rest",
        after,
    )


def late_kernel(half_ref, h_ref, *refs):
    own = h_ref.shape[1] // 2
    unit_ref, token_ref = refs[-2:]
    token_ref[...] = jnp.zeros_like(token_ref)
    for half in range(2):

        @pl.when(half_ref[0] == half)
        def _(half=half):
            for group in range(2):
                left = h_ref[:, group * own : (group + 1) * own]
                for i, d_ref in enumerate(refs[half:-2:2]):
                    unit_ref[group, i * own : (i + 1) * own, :] = dot_tn(left, d_ref[...]).astype(BF16)


def late(half, h1, d_qkv, after=()):
    own = h1.shape[1] // 2
    return per_half(
        late_kernel,
        half,
        (h1, *d_qkv),
        (2, own * len(d_qkv) // 2, WIDE),
        "late",
        after,
    )


def half_of(w_ref, chunk, core):
    sides = []
    for pair in range(2):
        starts = [i * HEADS * HEAD_DIM + chunk * SPAN + pair * PAIR for i in range(3)]
        sides.append(jnp.concatenate([w_ref[:, at : at + PAIR] for at in starts], axis=1))
    return jnp.where(core == 0, sides[0], sides[1])


def pack_first_kernel(info_ref, w_ref, gain_ref, send_ref):
    own = w_ref.shape[0]
    send_ref[:own, :] = half_of(w_ref, 0, info_ref[2])
    send_ref[own:, :] = jnp.broadcast_to(gain_ref[...], (16, send_ref.shape[1]))


def pack_first(info, w_qkv, gain):
    return pl.pallas_call(
        pack_first_kernel,
        out_shape=jax.ShapeDtypeStruct((w_qkv.shape[0] + 16, WIDE), BF16),
        in_specs=[SCALAR, LOCAL, LOCAL],
        out_specs=LOCAL,
        compiler_params=pltpu.CompilerParams(vmem_limit_bytes=8 << 20),
        name="pack_first",
    )(info, w_qkv, gain)


def pack_kernel(info_ref, w_ref, wo_ref, wi_ref, wd_ref, gain_ref, s1_ref, s2_ref, a_ref, b_ref):
    core = info_ref[2]
    own = wo_ref.shape[0]
    down = wd_ref.shape[0]
    half = wo_ref.shape[1] // 2
    s1_ref[...] = half_of(w_ref, 1, core)
    s2_ref[...] = half_of(w_ref, 2, core)

    sub = own // 2

    def part(ref, i, rows=slice(None)):
        left = i * half
        right = ref.shape[1] // 2 + i * half
        return jnp.where(core == 0, ref[rows, left : left + half], ref[rows, right : right + half])

    b_ref[:own, :] = part(wo_ref, 0)
    b_ref[own : own + down, :] = part(wd_ref, 0)
    b_ref[own + down :, :] = jnp.broadcast_to(gain_ref[...], (16, half))
    for j in range(3):
        rows = pl.ds(pl.multiple_of(info_ref[3] * sub, sub), sub)
        a_ref[j * sub : (j + 1) * sub, :] = part(wi_ref, j, rows)


def pack(info, w_qkv, w_out, w_in, w_down, gain):
    own = w_qkv.shape[0]
    wide = WIDE
    return pl.pallas_call(
        pack_kernel,
        out_shape=(
            jax.ShapeDtypeStruct((own, wide), BF16),
            jax.ShapeDtypeStruct((own, wide), BF16),
            jax.ShapeDtypeStruct((own // 2 * 3, wide), BF16),
            jax.ShapeDtypeStruct((own + w_down.shape[0] + 16, wide), BF16),
        ),
        in_specs=[SCALAR] + [LOCAL] * 5,
        out_specs=(LOCAL,) * 4,
        compiler_params=pltpu.CompilerParams(vmem_limit_bytes=12 << 20),
        name="pack",
    )(info, w_qkv, w_out, w_in, w_down, gain)


def halves_kernel(at_ref, mine_ref, in_ref, away_ref, here_ref, *, axis):
    size = here_ref.shape[axis]
    at = at_ref[0]

    def part(ref, index):
        start = pl.multiple_of(index * size, size)
        if axis == 0:
            return ref[pl.ds(start, size)].astype(F32)
        return ref[:, pl.ds(start, size)].astype(F32)

    away_ref[...] = (part(mine_ref, 1 - at) + part(in_ref, 1 - at)).astype(BF16)
    here_ref[...] = (part(mine_ref, at) + part(in_ref, at)).astype(BF16)


def halves(mine, received, at, axis, after=()):
    shape = list(mine.shape)
    shape[axis] //= 2
    out = jax.ShapeDtypeStruct(tuple(shape), BF16)
    return pl.pallas_call(
        skip(functools.partial(halves_kernel, axis=axis), 3, len(after)),
        out_shape=(out, out),
        in_specs=[SCALAR, LOCAL, LOCAL] + [FAR] * len(after),
        out_specs=(LOCAL, LOCAL),
        compiler_params=pltpu.CompilerParams(vmem_limit_bytes=8 << 20),
        cost_estimate=cost("halves"),
        name="halves",
    )(at.astype(jnp.int32)[None], mine, received, *after)


def last_kernel(info_ref, tok_ref, gain_ref, away_ref, *refs, step):
    d_refs, (w0_ref, w1_ref, w2_ref, dx_ref, out_ref, token_ref) = refs[:6], refs[6:]
    token_ref[...] = jnp.zeros_like(token_ref)
    group = info_ref[1]
    gain_own = gain_ref[...].astype(F32)
    gain_away = away_ref[0:1, :].astype(F32)
    gain = jnp.where(
        group == 0,
        jnp.concatenate([gain_own, gain_away], axis=1),
        jnp.concatenate([gain_away, gain_own], axis=1),
    )
    for at in range(0, tok_ref.shape[0], step):
        rows = slice(at, at + step)
        field = tok_ref[rows, :].astype(F32)
        center = field - jnp.mean(field, axis=1, keepdims=True)
        rate = lax.rsqrt(jnp.mean(center * center, axis=1, keepdims=True) + norm_eps)
        unit = center * rate
        e = jnp.zeros(field.shape, F32)
        for chunk, w_ref in enumerate((w0_ref, w1_ref, w2_ref)):
            pairs = [d_refs[2 * chunk + i][rows, :] for i in range(2)]
            e += dot_nt(jnp.concatenate(pairs, axis=1), w_ref[...])
        e *= gain
        out_ref[rows, :] = dx_ref[rows, :] + rate * (
            e
            - jnp.mean(e, axis=1, keepdims=True)
            - unit * jnp.mean(e * unit, axis=1, keepdims=True)
        )


def last(info, tokens, gain, away, d_qkv, full, d_x1, after=(), step=256):
    return pl.pallas_call(
        skip(functools.partial(last_kernel, step=step), 14, len(after)),
        out_shape=(jax.ShapeDtypeStruct(d_x1.shape, F32), jax.ShapeDtypeStruct((8, 128), F32)),
        in_specs=[SCALAR] + [LOCAL] * 13 + [FAR] * len(after),
        out_specs=(LOCAL, LOCAL),
        compiler_params=pltpu.CompilerParams(vmem_limit_bytes=LIMITS["last"] << 20),
        cost_estimate=cost("last"),
        name="last",
    )(info, tokens, gain, away, *d_qkv, *full, d_x1, *after)


def row_of(column):
    return jnp.broadcast_to(column, (column.shape[0], 128)).T[0:1, :]


def spread_early_kernel(
    info_ref, ma_ref, mb_ref, oa_ref, ob_ref, w_ref, gain_ref, in_ref, out_ref, down_ref, dg_ref
):
    core = info_ref[2]
    own = out_ref.shape[0]
    down = down_ref.shape[0]
    half = out_ref.shape[1] // 2

    def part_of(i, mine_ref, other_ref, start, size):
        mine = mine_ref[start : start + size, :].astype(F32)
        other = other_ref[start : start + size, :].astype(F32)
        return jnp.where(core == i, mine, other)

    total = jnp.zeros((own, 1), F32)
    for i in range(2):
        for j in range(3):
            at = (3 * i + j) * half
            part = part_of(i, ma_ref, oa_ref, j * own, own)
            in_ref[:, at : at + half] = part
            total += jnp.sum(part * w_ref[:, at : at + half].astype(F32), axis=1, keepdims=True)
        out_ref[:, i * half : (i + 1) * half] = part_of(i, mb_ref, ob_ref, 0, own)
        down_ref[:, i * half : (i + 1) * half] = part_of(i, mb_ref, ob_ref, own, down)
    dg_ref[...] = (row_of(total) / gain_ref[...].astype(F32))[0]


def spread_early(info, mine, other, w_in, gain, down):
    own = w_in.shape[0]
    return pl.pallas_call(
        spread_early_kernel,
        out_shape=(
            jax.ShapeDtypeStruct(w_in.shape, F32),
            jax.ShapeDtypeStruct((own, 2 * own), F32),
            jax.ShapeDtypeStruct((down, 2 * own), F32),
            jax.ShapeDtypeStruct((own,), F32),
        ),
        in_specs=[SCALAR] + [LOCAL] * 6,
        out_specs=(LOCAL,) * 4,
        compiler_params=pltpu.CompilerParams(vmem_limit_bytes=LIMITS["spread"] << 20),
        cost_estimate=cost("spread"),
        name="spread_early",
    )(info, *mine, *other, w_in, gain)


def spread_late_kernel(info_ref, m01_ref, o01_ref, m2_ref, o2_ref, w_ref, gain_ref, out_ref, dg_ref):
    core = info_ref[2]
    own = w_ref.shape[0]
    total = jnp.zeros((own, 1), F32)
    for chunk in range(3):
        mine_ref, other_ref = (m2_ref, o2_ref) if chunk == 2 else (m01_ref, o01_ref)
        start = own if chunk == 1 else 0
        mine = mine_ref[start : start + own, :].astype(F32)
        other = other_ref[start : start + own, :].astype(F32)
        whole = jnp.concatenate(
            [jnp.where(core == 0, mine, other), jnp.where(core == 0, other, mine)], axis=1
        )
        for i in range(6):
            at = (i % 3) * HEADS * HEAD_DIM + chunk * SPAN + (i // 3) * PAIR
            part = whole[:, i * PAIR : (i + 1) * PAIR]
            out_ref[:, at : at + PAIR] = part
            total += jnp.sum(part * w_ref[:, at : at + PAIR].astype(F32), axis=1, keepdims=True)
    dg_ref[...] = (row_of(total) / gain_ref[...].astype(F32))[0]


def spread_late(info, first, second, w_qkv, gain):
    own = w_qkv.shape[0]
    return pl.pallas_call(
        spread_late_kernel,
        out_shape=(jax.ShapeDtypeStruct(w_qkv.shape, F32), jax.ShapeDtypeStruct((own,), F32)),
        in_specs=[SCALAR] + [LOCAL] * 6,
        out_specs=(LOCAL, LOCAL),
        compiler_params=pltpu.CompilerParams(vmem_limit_bytes=LIMITS["spread"] << 20),
        cost_estimate=cost("spread"),
        name="spread_late",
    )(info, *first, *second, w_qkv, gain)


def pull_kernel(
    info_ref, qkv_ref, mixed_ref, dm_ref, lse_ref, turn_ref, out_ref, token_ref,
    qa_ref, ka_ref, kt_ref, dv_ref, dk_ref, *, pair, step,
):
    length = qkv_ref.shape[0]
    valid = info_ref[0]
    lane = lax.broadcasted_iota(jnp.int32, (step, PAIR), 1)
    one = jnp.ones((), BF16)
    zero = jnp.zeros((), BF16)
    token_ref[...] = jnp.zeros_like(token_ref)
    inner = pair % 2
    for at in range(0, length, step):
        rows = pl.ds(at, step)
        row = lax.broadcasted_iota(jnp.int32, (step, PAIR), 0) + at
        bias = jnp.where(row < valid, 0.0, NEG).astype(BF16)
        q = qkv_ref[rows, :PAIR]
        k = qkv_ref[rows, PAIR : 2 * PAIR]
        kt_ref[:, rows] = k.T
        for side in range(2):
            mine = (lane // HEAD_DIM) == side
            spare = lane == (1 - side) * HEAD_DIM
            qa_ref[side, rows, :] = jnp.where(mine, q, jnp.where(spare, one, zero))
            ka_ref[side, rows, :] = jnp.where(mine, k, jnp.where(spare, bias, zero))
    dv_ref[...] = jnp.zeros_like(dv_ref)
    dk_ref[...] = jnp.zeros_like(dk_ref)
    half_rows = lax.broadcasted_iota(jnp.int32, (8, PAIR), 0)
    half_lane = lax.broadcasted_iota(jnp.int32, (8, PAIR), 1)
    chooser = jnp.where(half_lane // HEAD_DIM == half_rows, 1.0, 0.0).astype(BF16)

    def body(block, _):
        rows = pl.ds(pl.multiple_of(block * step, step), step)
        dm = dm_ref[rows, pair * PAIR : (pair + 1) * PAIR]
        product = dm.astype(F32) * mixed_ref[rows, inner * PAIR : (inner + 1) * PAIR].astype(F32)
        high = product.astype(BF16)
        low = (product - high.astype(F32)).astype(BF16)
        delta = dot_nt(chooser, high) + dot_nt(chooser, low)
        dmt = dm.T
        qt = qkv_ref[rows, :PAIR].T
        outs = []
        for side in range(2):
            head = 2 * inner + side
            part = slice(side * HEAD_DIM, (side + 1) * HEAD_DIM)
            dms = jnp.where((lane // HEAD_DIM) == side, dm, zero)
            scores = dot_nt(ka_ref[side], qa_ref[side, rows, :])
            weights = jnp.exp2(scores - lse_ref[head : head + 1, rows])
            d_weights = dot_nt(qkv_ref[:, 2 * PAIR :], dms)
            d_scores = (weights * (d_weights - delta[side : side + 1, :])).astype(BF16)
            dv_ref[part, :] += dot_nt(dmt[part, :], weights.astype(BF16))
            dk_ref[part, :] += dot_nt(qt[part, :], d_scores)
            outs.append(dot_nn(kt_ref[part, :], d_scores))
        dq = jnp.concatenate(outs, axis=0).T * (1.0 / math.sqrt(HEAD_DIM))
        dq = dq * turn_ref[rows, :PAIR] - swap_halves(dq) * turn_ref[rows, PAIR:]
        out_ref[rows, :PAIR] = dq.astype(BF16)
        return 0

    lax.fori_loop(0, length // step, body, 0)
    for at in range(0, length, step):
        rows = pl.ds(at, step)
        dk = dk_ref[:, rows].T * LN2
        dk = dk * turn_ref[rows, :PAIR] - swap_halves(dk) * turn_ref[rows, PAIR:]
        out_ref[rows, PAIR : 2 * PAIR] = dk.astype(BF16)
        out_ref[rows, 2 * PAIR :] = dv_ref[:, rows].T.astype(BF16)


def pull(info, qkv, mixed, d_mixed, lse, turn, pair, after=(), step=256):
    rows = qkv.shape[0]
    return pl.pallas_call(
        skip(functools.partial(pull_kernel, pair=pair, step=step), 6, len(after)),
        out_shape=(jax.ShapeDtypeStruct((rows, WIDE), BF16), jax.ShapeDtypeStruct((8, 128), F32)),
        in_specs=[SCALAR] + [LOCAL] * 5 + [FAR] * len(after),
        out_specs=(LOCAL, LOCAL),
        scratch_shapes=[
            pltpu.VMEM((2, rows, PAIR), BF16),
            pltpu.VMEM((2, rows, PAIR), BF16),
            pltpu.VMEM((PAIR, rows), BF16),
            pltpu.VMEM((PAIR, rows), F32),
            pltpu.VMEM((PAIR, rows), F32),
        ],
        compiler_params=pltpu.CompilerParams(vmem_limit_bytes=LIMITS["pull"] << 20),
        cost_estimate=cost("pull"),
        name=f"pull_{pair}",
    )(info, qkv, mixed, d_mixed, lse, turn, *after)


def both_kernel(left_ref, right_ref, out_ref):
    out_ref[...] = (left_ref[...].astype(F32) + right_ref[...].astype(F32)).astype(BF16)


def both(left, right, after=()):
    return pl.pallas_call(
        skip(both_kernel, 2, len(after)),
        out_shape=jax.ShapeDtypeStruct(left.shape, BF16),
        in_specs=[LOCAL, LOCAL] + [FAR] * len(after),
        out_specs=LOCAL,
        compiler_params=pltpu.CompilerParams(vmem_limit_bytes=8 << 20),
        cost_estimate=cost("halves"),
        name="both",
    )(left, right, *after)


def swap_replica(field, bit):
    count = lax.axis_size("replica")
    return lax.ppermute(field, "replica", [(i, i ^ bit) for i in range(count)])


def swap_group(field):
    return lax.ppermute(field, "group", [(0, 1), (1, 0)])


def pick(field, index, axis):
    size = field.shape[axis] // 2
    return lax.dynamic_slice_in_dim(field, index * size, size, axis)


def in_order(mine, other, index, axis):
    return jnp.where(
        index == 0,
        jnp.concatenate([mine, other], axis=axis),
        jnp.concatenate([other, mine], axis=axis),
    )


def add_low(left, right):
    return (left.astype(F32) + right.astype(F32)).astype(BF16)


def hold(value, *others):
    return lax.optimization_barrier((value, others))[0]


def further_bits():
    bits = [4, 12]
    bit = 16
    while bit < lax.axis_size("replica"):
        bits.append(bit)
        bit *= 2
    return bits


def on_device(tokens, lengths, w_qkv, w_out, gain_one, w_in, w_down, gain_two, cotangent):
    rows = tokens.shape[1]
    group = lax.axis_index("group")
    replica = lax.axis_index("replica")
    core = replica % 2
    second = (replica // 2) % 2
    info = jnp.stack([lengths[0], group, core, second]).astype(jnp.int32)
    cos_rows, sin_rows = angle_tables(rows)
    turn = jnp.asarray(np.concatenate([cos_rows, sin_rows], axis=1))

    field = tokens[0]
    cot = cotangent[0]
    qkv, mixed, lse, full = [None] * 6, [None] * 3, [None] * 3, [None] * 3
    far0 = swap_group(pack_first(info, w_qkv, gain_one[None]))
    send1, send2, send_a, send_b = pack(info, w_qkv, w_out, w_in, w_down, gain_two[None])
    far0, send1, send2 = lax.optimization_barrier((far0, send1, send2))
    far1 = swap_group(send1)
    far2 = swap_group(send2)
    qkv[0], qkv[1], full[0], lse[0], mixed[0], h1 = attend(
        info, field, gain_one[None], w_qkv, (far0, swap_replica(far0, 1)), turn, 0
    )
    lse[0], send_a, far1 = lax.optimization_barrier((lse[0], send_a, far1))
    far_a = swap_group(send_a)
    near1 = swap_replica(far1, 1)
    near1, send_b = lax.optimization_barrier((near1, send_b))
    far_b = swap_group(send_b)
    qkv[2], qkv[3], full[1], lse[1], mixed[1] = attend(
        info, h1, None, w_qkv, (far1, near1), turn, 1, (lse[0],)
    )
    lse[1], far_a, far2 = lax.optimization_barrier((lse[1], far_a, far2))
    far_c = swap_replica(far_a, 2)
    near_a = swap_replica(far_a, 1)
    qkv[4], qkv[5], full[2], lse[2], mixed[2] = attend(
        info, h1, None, w_qkv, (far2, swap_replica(far2, 1)), turn, 2, (lse[1],)
    )
    lse[2], far_b, far_c = lax.optimization_barrier((lse[2], far_b, far_c))
    parts_rest = (far_b, swap_replica(far_b, 1), far_a, near_a, far_c, swap_replica(far_c, 1))
    output, d_x1, dx_low, d_mixed, h2, act, d_up = middle(
        info, field, mixed, cot, gain_two[None], w_out, w_in, w_down, parts_rest
    )
    mine = core.astype(jnp.int32)[None]
    theirs = 1 - mine

    def tug(pair, *after):
        return pull(
            info, qkv[pair], mixed[pair // 2], d_mixed, lse[pair // 2], turn, pair, after
        )

    d_qkv = [None] * 6
    a_send, token = early_in(theirs, h2, d_up)
    a_in = swap_replica(a_send, 1)
    b_send, token = early_rest(theirs, act, cot, mixed, dx_low, (token,))
    b_in = swap_replica(b_send, 1)
    a_mine, token = early_in(mine, h2, d_up, (token,))
    a_away, a_here = halves(a_mine, a_in, group, 0)
    a_in = swap_group(a_away)
    b_mine, token = early_rest(mine, act, cot, mixed, dx_low, (a_away,))
    b_away, b_here = halves(b_mine, b_in, second, 1)
    b_in = swap_replica(b_away, 2)

    d_qkv[0], token = tug(0, b_away)
    d_qkv[1], token = tug(1, token)
    a_away, a_here = halves(a_here[0], a_in[0], second, 0, (token,))
    a_in = swap_replica(a_away, 2)
    b_away, b_here = halves(b_here, b_in, group, 0, (a_away,))
    b_in = swap_group(b_away)
    d_qkv[2], token = tug(2, b_away)
    d_qkv[3], token = tug(3, token)
    l_send, token = late(theirs, h1, d_qkv[:4], (token,))
    l_in = swap_replica(l_send, 1)
    early_mine = jnp.concatenate([a_here, b_here[0]], axis=0)
    early_in_sum = jnp.concatenate([a_in, b_in[0]], axis=0)
    bits = further_bits()
    at = (replica // 4 + replica // 8) % 2
    e_away, e_here = halves(early_mine, early_in_sum, at, 0, (token,))
    e_in = swap_replica(e_away, bits[0])
    l_mine, token = late(mine, h1, d_qkv[:4], (e_away,))
    l_away, l_here = halves(l_mine, l_in, group, 0)
    l_in = swap_group(l_away)
    d_qkv[4], token = tug(4, l_away)
    e_sum = both(e_here, e_in, (token,))
    e_in = swap_replica(e_sum, bits[1])
    d_qkv[5], token = tug(5, e_sum)
    m_send, token = late(theirs, h1, d_qkv[4:], (token,))
    m_in = swap_replica(m_send, 1)
    l_away, l_here = halves(l_here[0], l_in[0], second, 0, (token,))
    l_in = swap_replica(l_away, 2)
    m_mine, token = late(mine, h1, d_qkv[4:], (l_away,))
    m_away, m_here = halves(m_mine, m_in, group, 0)
    m_in = swap_group(m_away)
    grad_tokens, token = last(
        info, field, gain_one[None], far0[w_qkv.shape[0] :], d_qkv, full, d_x1, (m_away,)
    )

    def across(total, todo):
        for bit in todo:
            total = add_low(total, swap_replica(total, bit))
        return total

    m_away, m_here = halves(m_here[0], m_in[0], second, 0, (token,))
    m_in = swap_replica(m_away, 2)
    e_sum = across(add_low(e_sum, e_in), bits[2:])
    e_sum = in_order(e_sum, swap_replica(e_sum, bits[0]), at, 0)
    e_other = swap_replica(e_sum, 2)
    l_sum = across(add_low(l_here, l_in), bits)
    m_sum = across(add_low(m_here, m_in), bits)
    cut = a_here.shape[0]
    whole_a = in_order(e_sum[:cut], e_other[:cut], second, 0)
    whole_b = in_order(e_sum[cut:], e_other[cut:], second, 0)
    l_sum = in_order(l_sum, swap_replica(l_sum, 2), second, 0)
    m_sum = in_order(m_sum, swap_replica(m_sum, 2), second, 0)
    grad_in, grad_out, grad_down, grad_two = spread_early(
        info,
        (whole_a, whole_b),
        (swap_replica(whole_a, 1), swap_replica(whole_b, 1)),
        w_in,
        gain_two[None],
        w_down.shape[0],
    )
    grad_qkv, grad_one = spread_late(
        info, (l_sum, swap_replica(l_sum, 1)), (m_sum, swap_replica(m_sum, 1)), w_qkv, gain_one[None]
    )
    return (
        output[None],
        grad_tokens[None],
        grad_qkv,
        grad_out,
        grad_one,
        grad_in,
        grad_down,
        grad_two,
    )


def solution(mesh):
    both = P(("group", "replica"), None, None)
    rows = P("group", None)
    vector = P("group")
    return jax.shard_map(
        on_device,
        mesh=mesh,
        in_specs=(both, P(("group", "replica")), rows, rows, vector, rows, rows, vector, both),
        out_specs=(both, both, rows, rows, vector, rows, rows, vector),
        check_vma=False,
    )
```

```python
import functools
import math

import jax
import jax.numpy as jnp
import numpy as np
from jax import lax
from jax.experimental import pallas as pl
from jax.experimental.pallas import tpu as pltpu
from jax.sharding import PartitionSpec as P

HEADS = 12
HEAD_DIM = 64
theta_base = 160000.0
norm_eps = 1e-05
LOG2E = 1.4426950408889634
LN2 = 0.6931471805599453
F32 = jnp.float32
BF16 = jnp.bfloat16
PAIR = 2 * HEAD_DIM
GROUP_HEADS = 4
SPAN = GROUP_HEADS * HEAD_DIM
WIDE = 3 * PAIR
NEG = -1e30
LOCAL = pl.BlockSpec(memory_space=pltpu.VMEM)
SCALAR = pl.BlockSpec(memory_space=pltpu.SMEM)
FAR = pl.BlockSpec(memory_space=pl.ANY)
STORED = pl.BlockSpec(memory_space=pltpu.HBM)


def dot_nn(a, b):
    return lax.dot_general(a, b, (((1,), (0,)), ((), ())), preferred_element_type=F32)


def dot_nt(a, b):
    return lax.dot_general(a, b, (((1,), (1,)), ((), ())), preferred_element_type=F32)


def dot_tn(a, b):
    return lax.dot_general(a, b, (((0,), (0,)), ((), ())), preferred_element_type=F32)


def angle_tables(length):
    half = HEAD_DIM // 2
    freq = np.exp(-math.log(theta_base) * 2.0 * np.arange(half, dtype=np.float64) / HEAD_DIM)
    angle = np.arange(length, dtype=np.float64)[:, None] * freq.astype(np.float32).astype(np.float64)[None]
    cosine = np.cos(angle)
    sine = np.sin(angle)
    cos_rows = np.concatenate([cosine] * 4, axis=1).astype(np.float32)
    sin_rows = np.concatenate([-sine, sine, -sine, sine], axis=1).astype(np.float32)
    return cos_rows, sin_rows


def swap_halves(field):
    half = HEAD_DIM // 2
    lane = lax.broadcasted_iota(jnp.int32, field.shape, 1)
    return jnp.where(
        (lane // half) % 2 == 0, pltpu.roll(field, PAIR - half, 1), pltpu.roll(field, half, 1)
    )


def erf_exp(u):
    return lax.erf(u * (1.0 / math.sqrt(2.0))), jnp.exp(-0.5 * u * u)


LIMITS = {"attend": 16, "middle": 24, "early_in": 8, "early_rest": 8, "pull": 12, "late": 6, "last": 12, "spread": 12}
LENGTHS = {"attend": 3, "middle": 28, "early_in": 3, "early_rest": 3, "pull": 5, "late": 2, "last": 8, "spread": 3, "halves": 1}


def cost(name):
    return pl.CostEstimate(flops=LENGTHS[name] * 1_000_000_000, transcendentals=0, bytes_accessed=0)


def skip(kernel, at, count):
    return lambda *refs: kernel(*refs[:at], *refs[at + count :])


def start_all(copies):
    for copy in copies:
        copy.start()


def attend_kernel(*refs, chunk, first, step):
    if first:
        (info_ref, tok_ref, gain_ref, w_ref, mine_ref, other_ref, turn_ref,
         qkva_ref, qkvb_ref, full_ref, lse_ref, mixed_ref, h_ref,
         vt_ref, qa_ref, ka_ref, s_ref, row_ref, sems) = refs
    else:
        (info_ref, h_ref, w_ref, mine_ref, other_ref, turn_ref,
         qkva_ref, qkvb_ref, full_ref, lse_ref, mixed_ref,
         vt_ref, qa_ref, ka_ref, s_ref, sems) = refs
    rows_all = h_ref.shape[0]
    own = w_ref.shape[0]
    valid = info_ref[0]
    group = info_ref[1]
    core = info_ref[2]
    there = pl.ds(pl.multiple_of(group * own, own), own)
    away = pl.ds(pl.multiple_of((1 - group) * own, own), own)
    copies = []
    for pair in range(2):
        for i in range(3):
            copies.append(
                pltpu.make_async_copy(
                    w_ref.at[:, pl.ds(i * HEADS * HEAD_DIM + chunk * SPAN + pair * PAIR, PAIR)],
                    full_ref.at[there, pl.ds(pair * WIDE + i * PAIR, PAIR)],
                    sems.at[3 * pair + i],
                )
            )
    for i, (part, side) in enumerate(((mine_ref, core), (other_ref, 1 - core))):
        copies.append(
            pltpu.make_async_copy(
                part.at[pl.ds(own if chunk == 2 else 0, own)],
                full_ref.at[away, pl.ds(pl.multiple_of(side * WIDE, WIDE), WIDE)],
                sems.at[6 + i],
            )
        )
    if first:
        copies.append(pltpu.make_async_copy(mine_ref.at[pl.ds(own, 16)], row_ref, sems.at[8]))
    start_all(copies)
    if first:
        copies[-1].wait()
        copies = copies[:-1]
        gain_own = gain_ref[...].astype(F32)
        gain_away = row_ref[0:1, :].astype(F32)
        gain = jnp.where(
            group == 0,
            jnp.concatenate([gain_own, gain_away], axis=1),
            jnp.concatenate([gain_away, gain_own], axis=1),
        )

        def normalize(block, _):
            rows = pl.ds(pl.multiple_of(block * step, step), step)
            field = tok_ref[rows, :].astype(F32)
            center = field - jnp.mean(field, axis=1, keepdims=True)
            spread = jnp.mean(center * center, axis=1, keepdims=True)
            h_ref[rows, :] = (center * lax.rsqrt(spread + norm_eps) * gain).astype(BF16)
            return 0

        lax.fori_loop(0, rows_all // step, normalize, 0)
    for copy in copies:
        copy.wait()
    lane = lax.broadcasted_iota(jnp.int32, (step, PAIR), 1)

    def project(block, _):
        rows = pl.ds(pl.multiple_of(block * step, step), step)
        merged = dot_nn(h_ref[rows, :], full_ref[...])
        cosine = turn_ref[rows, :PAIR]
        sine = turn_ref[rows, PAIR:]
        row = lax.broadcasted_iota(jnp.int32, (step, PAIR), 0) + block * step
        bias = jnp.where(row < valid, 0.0, NEG)
        for pair, qkv_ref in enumerate((qkva_ref, qkvb_ref)):
            left = pair * WIDE
            q = merged[:, left : left + PAIR]
            k = merged[:, left + PAIR : left + 2 * PAIR]
            v = merged[:, left + 2 * PAIR : left + WIDE].astype(BF16)
            q = (q * cosine + swap_halves(q) * sine) * (LOG2E / math.sqrt(HEAD_DIM))
            k = k * cosine + swap_halves(k) * sine
            qkv_ref[rows, :PAIR] = q.astype(BF16)
            qkv_ref[rows, PAIR : 2 * PAIR] = k.astype(BF16)
            qkv_ref[rows, 2 * PAIR :] = v
            vt_ref[pair, :, rows] = v.T
            for side in range(2):
                mine = (lane // HEAD_DIM) == side
                spare = lane == (1 - side) * HEAD_DIM
                qa_ref[2 * pair + side, rows, :] = jnp.where(
                    mine, q, jnp.where(spare, 1.0, 0.0)
                ).astype(BF16)
                ka_ref[2 * pair + side, rows, :] = jnp.where(
                    mine, k, jnp.where(spare, bias, 0.0)
                ).astype(BF16)
        return 0

    blocks = rows_all // step
    lax.fori_loop(0, blocks, project, 0)
    ones = jnp.ones((16, step), BF16)

    def score(head, block, part, slot, top):
        rows = pl.ds(pl.multiple_of(block * step, step), step)
        keys = pl.ds(part * step, step)
        scores = dot_nt(ka_ref[head, keys, :], qa_ref[head, rows, :])
        s_ref[slot, keys, :] = scores
        here = jnp.max(scores, axis=0, keepdims=True)
        return here if top is None else jnp.maximum(top, here)

    def body(block, top):
        rows = pl.ds(pl.multiple_of(block * step, step), step)
        outs = []
        for head in range(GROUP_HEADS):
            pair, side = divmod(head, 2)
            slot = head % 2
            following = (head + 1) % GROUP_HEADS
            next_block = block if head + 1 < GROUP_HEADS else jnp.minimum(block + 1, blocks - 1)
            result = jnp.zeros((HEAD_DIM + 16, step), F32)
            next_top = None
            for part in range(blocks):
                keys = pl.ds(part * step, step)
                next_top = score(following, next_block, part, 1 - slot, next_top)
                weights = jnp.exp2(s_ref[slot, keys, :] - top).astype(BF16)
                values = jnp.concatenate(
                    [vt_ref[pair, side * HEAD_DIM : (side + 1) * HEAD_DIM, keys], ones], axis=0
                )
                result += dot_nn(values, weights)
            total = result[HEAD_DIM : HEAD_DIM + 1, :]
            outs.append(result[:HEAD_DIM, :] / total)
            lse_ref[head : head + 1, rows] = top + jnp.log2(total)
            top = next_top
            if side == 1:
                mixed_ref[rows, pair * PAIR : (pair + 1) * PAIR] = (
                    jnp.concatenate(outs[-2:], axis=0).T.astype(BF16)
                )
        return top

    top = None
    for part in range(blocks):
        top = score(0, 0, part, 0, top)
    lax.fori_loop(0, blocks, body, top)


def attend(info, source, gain, w, parts, turn, chunk, after=(), step=256):
    rows = source.shape[0]
    width = 2 * w.shape[0]
    first = gain is not None
    stored = [
        ((rows, WIDE), BF16),
        ((rows, WIDE), BF16),
        ((width, 3 * SPAN), BF16),
        ((8, rows), F32),
    ]
    out_shape = [jax.ShapeDtypeStruct(*s) for s in stored]
    out_shape.append(jax.ShapeDtypeStruct((rows, SPAN), BF16))
    scratch = [
        pltpu.VMEM((SPAN // PAIR, PAIR, rows), BF16),
        pltpu.VMEM((GROUP_HEADS, rows, PAIR), BF16),
        pltpu.VMEM((GROUP_HEADS, rows, PAIR), BF16),
        pltpu.VMEM((2, rows, step), F32),
    ]
    inputs = [info, source]
    specs = [SCALAR, LOCAL]
    if first:
        out_shape.append(jax.ShapeDtypeStruct((rows, width), BF16))
        scratch.append(pltpu.VMEM((16, WIDE), BF16))
        inputs.append(gain)
        specs.append(LOCAL)
    inputs += [w, *parts, turn]
    specs += [FAR, FAR, FAR, LOCAL]
    kernel = functools.partial(attend_kernel, chunk=chunk, first=first, step=step)
    kernel = skip(kernel, len(inputs), len(after))
    inputs += after
    specs += [FAR] * len(after)
    scratch.append(pltpu.SemaphoreType.DMA((9,)))
    return pl.pallas_call(
        kernel,
        out_shape=tuple(out_shape),
        in_specs=specs,
        out_specs=tuple([LOCAL] * len(out_shape)),
        scratch_shapes=scratch,
        compiler_params=pltpu.CompilerParams(vmem_limit_bytes=LIMITS["attend"] << 20),
        cost_estimate=cost("attend"),
        name=f"attend_{chunk}",
    )(*inputs)


def middle_kernel(
    info_ref, tok_ref, mix0_ref, mix1_ref, mix2_ref, cot_ref, gain_ref,
    wo_ref, wi_ref, wd_ref, *refs, step,
):
    parts, refs = refs[:6], refs[6:]
    (out_ref, dx_ref, dxl_ref, dm_ref, h_ref, act_ref, du_ref,
     fo_ref, fi_ref, fd_ref, row_ref, sems) = refs
    rows_all, width = tok_ref.shape
    own = wo_ref.shape[0]
    down = wd_ref.shape[0]
    half = width // 2
    hidden = fd_ref.shape[0]
    valid = info_ref[0]
    group = info_ref[1]
    core = info_ref[2]

    def at(start, size):
        return pl.ds(pl.multiple_of(start, size), size)

    copies = [
        pltpu.make_async_copy(wo_ref, fo_ref.at[at(group * own, own)], sems.at[0]),
        pltpu.make_async_copy(wi_ref, fi_ref.at[at(group * own, own)], sems.at[1]),
        pltpu.make_async_copy(wd_ref, fd_ref.at[at(group * down, down)], sems.at[2]),
        pltpu.make_async_copy(parts[0].at[pl.ds(own + down, 16)], row_ref, sems.at[3]),
    ]
    sub = own // 2
    second = info_ref[3]
    for i, side in enumerate((core, 1 - core)):
        base = 4 + 8 * i
        part = parts[i]
        copies.append(
            pltpu.make_async_copy(
                part.at[pl.ds(0, own)],
                fo_ref.at[at((1 - group) * own, own), at(side * half, half)],
                sems.at[base],
            )
        )
        copies.append(
            pltpu.make_async_copy(
                part.at[pl.ds(own, down)],
                fd_ref.at[at((1 - group) * down, down), at(side * half, half)],
                sems.at[base + 1],
            )
        )
        for k, which in enumerate((second, 1 - second)):
            part = parts[2 + 2 * k + i]
            for j in range(3):
                copies.append(
                    pltpu.make_async_copy(
                        part.at[pl.ds(j * sub, sub)],
                        fi_ref.at[
                            at((1 - group) * own + which * sub, sub), at(side * 3 * half + j * half, half)
                        ],
                        sems.at[base + 2 + 3 * k + j],
                    )
                )
    start_all(copies)
    for copy in copies:
        copy.wait()
    gain_own = gain_ref[...].astype(F32)
    gain_away = row_ref[0:1, :].astype(F32)
    gain = jnp.where(
        group == 0,
        jnp.concatenate([gain_own, gain_away], axis=1),
        jnp.concatenate([gain_away, gain_own], axis=1),
    )

    def body(block, _):
        rows = pl.ds(pl.multiple_of(block * step, step), step)
        mixed = jnp.concatenate([mix0_ref[rows, :], mix1_ref[rows, :], mix2_ref[rows, :]], axis=1)
        x1 = tok_ref[rows, :].astype(F32) + dot_nn(mixed, fo_ref[...])
        center = x1 - jnp.mean(x1, axis=1, keepdims=True)
        rate = lax.rsqrt(jnp.mean(center * center, axis=1, keepdims=True) + norm_eps)
        unit = center * rate
        h2 = (unit * gain).astype(BF16)
        h_ref[rows, :] = h2
        row = lax.broadcasted_iota(jnp.int32, (step, 1), 0) + block * step
        keep = row < valid
        up = dot_nn(h2, fi_ref[...])
        turned = up[:, :hidden]
        gate = up[:, hidden:]
        curve, bell = erf_exp(turned)
        share = 0.5 * (1.0 + curve)
        bent = turned * share
        act = (bent * gate).astype(BF16)
        act_ref[rows, :] = jnp.where(keep, act, jnp.zeros((), BF16))
        result = x1 + dot_nn(act, fd_ref[...])
        out_ref[rows, :] = jnp.where(keep, result, 0.0).astype(BF16)
        dy = jnp.where(keep, cot_ref[rows, :], jnp.zeros((), BF16))
        d_act = dot_nt(dy, fd_ref[...])
        slope = share + turned * bell * (1.0 / math.sqrt(2.0 * math.pi))
        d_up = jnp.concatenate([d_act * gate * slope, d_act * bent], axis=1).astype(BF16)
        du_ref[rows, :] = d_up
        e = dot_nt(d_up, fi_ref[...]) * gain
        d_x1 = dy.astype(F32) + rate * (
            e
            - jnp.mean(e, axis=1, keepdims=True)
            - unit * jnp.mean(e * unit, axis=1, keepdims=True)
        )
        dx_ref[rows, :] = d_x1
        low = d_x1.astype(BF16)
        dxl_ref[rows, :] = low
        dm_ref[rows, :] = dot_nt(low, fo_ref[...]).astype(BF16)
        return 0

    lax.fori_loop(0, rows_all // step, body, 0)


def middle(info, tokens, mixed, cotangent, gain, w_out, w_in, w_down, parts, step=256):
    rows, width = tokens.shape
    hidden = 2 * w_down.shape[0]
    shapes = [
        ((rows, width), BF16),
        ((rows, width), F32),
        ((rows, width), BF16),
        ((rows, width), BF16),
        ((rows, width), BF16),
        ((rows, hidden), BF16),
        ((rows, 2 * hidden), BF16),
    ]
    return pl.pallas_call(
        functools.partial(middle_kernel, step=step),
        out_shape=tuple(jax.ShapeDtypeStruct(*s) for s in shapes),
        in_specs=[SCALAR] + [LOCAL] * 6 + [FAR] * 9,
        out_specs=tuple([LOCAL] * len(shapes)),
        scratch_shapes=[
            pltpu.VMEM((width, width), BF16),
            pltpu.VMEM((width, 2 * hidden), BF16),
            pltpu.VMEM((hidden, width), BF16),
            pltpu.VMEM((16, width // 2), BF16),
            pltpu.SemaphoreType.DMA((20,)),
        ],
        compiler_params=pltpu.CompilerParams(vmem_limit_bytes=LIMITS["middle"] << 20),
        cost_estimate=cost("middle"),
        name="middle",
    )(info, tokens, *mixed, cotangent, gain, w_out, w_in, w_down, *parts)


def early_in_kernel(half_ref, h_ref, du_ref, unit_ref, token_ref):
    token_ref[...] = jnp.zeros_like(token_ref)
    own = h_ref.shape[1] // 2
    side = pl.ds(pl.multiple_of(half_ref[0] * 3 * own, 3 * own), 3 * own)
    for group in range(2):
        whole = dot_tn(h_ref[:, group * own : (group + 1) * own], du_ref[:, side]).astype(BF16)
        for j in range(3):
            unit_ref[group, j * own : (j + 1) * own, :] = whole[:, j * own : (j + 1) * own]


def early_rest_kernel(
    half_ref, act_ref, cot_ref, m0_ref, m1_ref, m2_ref, dx_ref, unit_ref, token_ref
):
    token_ref[...] = jnp.zeros_like(token_ref)
    own = dx_ref.shape[1] // 2
    down = act_ref.shape[1] // 2
    side = pl.ds(pl.multiple_of(half_ref[0] * own, own), own)
    zero = jnp.zeros((unit_ref.shape[1] - own - down, own), BF16)
    mixed = [ref[...] for ref in (m0_ref, m1_ref, m2_ref)]
    low = dx_ref[:, side]
    grad_out = jnp.concatenate([dot_tn(m, low) for m in mixed], axis=0).astype(BF16)
    grad_down = dot_tn(act_ref[...], cot_ref[:, side]).astype(BF16)
    for group in range(2):
        unit_ref[group, :own, :] = grad_out[group * own : (group + 1) * own]
        unit_ref[group, own : own + down, :] = grad_down[group * down : (group + 1) * down]
        unit_ref[group, own + down :, :] = zero


def per_half(kernel, half, inputs, shape, name, after):
    return pl.pallas_call(
        skip(kernel, 1 + len(inputs), len(after)),
        out_shape=(jax.ShapeDtypeStruct(shape, BF16), jax.ShapeDtypeStruct((8, 128), F32)),
        in_specs=[SCALAR] + [LOCAL] * len(inputs) + [FAR] * len(after),
        out_specs=(LOCAL, LOCAL),
        compiler_params=pltpu.CompilerParams(vmem_limit_bytes=LIMITS[name] << 20),
        cost_estimate=cost(name),
        name=name,
    )(half, *inputs, *after)


def early_in(half, h2, d_up, after=()):
    own = h2.shape[1] // 2
    return per_half(early_in_kernel, half, (h2, d_up), (2, 3 * own, own), "early_in", after)


def early_rest(half, act, cotangent, mixed, dx_low, after=()):
    own = dx_low.shape[1] // 2
    filled = -(-(own + act.shape[1] // 2) // 128) * 128
    return per_half(
        early_rest_kernel,
        half,
        (act, cotangent, *mixed, dx_low),
        (2, filled, own),
        "early_rest",
        after,
    )


def late_kernel(half_ref, h_ref, *refs):
    own = h_ref.shape[1] // 2
    unit_ref, token_ref = refs[-2:]
    token_ref[...] = jnp.zeros_like(token_ref)
    pairs = [
        jnp.where(half_ref[0] == 0, first[...], second[...])
        for first, second in zip(refs[:-2:2], refs[1:-2:2])
    ]
    for group in range(2):
        left = h_ref[:, group * own : (group + 1) * own]
        for i, pair in enumerate(pairs):
            unit_ref[group, i * own : (i + 1) * own, :] = dot_tn(left, pair).astype(BF16)


def late(half, h1, d_qkv, after=()):
    own = h1.shape[1] // 2
    return per_half(
        late_kernel,
        half,
        (h1, *d_qkv),
        (2, own * len(d_qkv) // 2, WIDE),
        "late",
        after,
    )


def half_of(w_ref, chunk, core):
    sides = []
    for pair in range(2):
        starts = [i * HEADS * HEAD_DIM + chunk * SPAN + pair * PAIR for i in range(3)]
        sides.append(jnp.concatenate([w_ref[:, at : at + PAIR] for at in starts], axis=1))
    return jnp.where(core == 0, sides[0], sides[1])


def pack_first_kernel(info_ref, w_ref, gain_ref, send_ref):
    own = w_ref.shape[0]
    send_ref[:own, :] = half_of(w_ref, 0, info_ref[2])
    send_ref[own:, :] = jnp.broadcast_to(gain_ref[...], (16, send_ref.shape[1]))


def pack_first(info, w_qkv, gain):
    return pl.pallas_call(
        pack_first_kernel,
        out_shape=jax.ShapeDtypeStruct((w_qkv.shape[0] + 16, WIDE), BF16),
        in_specs=[SCALAR, LOCAL, LOCAL],
        out_specs=LOCAL,
        compiler_params=pltpu.CompilerParams(vmem_limit_bytes=8 << 20),
        name="pack_first",
    )(info, w_qkv, gain)


def pack_kernel(info_ref, w_ref, wo_ref, wi_ref, wd_ref, gain_ref, s_ref, a_ref, b_ref):
    core = info_ref[2]
    own = wo_ref.shape[0]
    down = wd_ref.shape[0]
    half = wo_ref.shape[1] // 2
    s_ref[:own, :] = half_of(w_ref, 1, core)
    s_ref[own:, :] = half_of(w_ref, 2, core)

    sub = own // 2

    def part(ref, i, rows=slice(None)):
        left = i * half
        right = ref.shape[1] // 2 + i * half
        return jnp.where(core == 0, ref[rows, left : left + half], ref[rows, right : right + half])

    b_ref[:own, :] = part(wo_ref, 0)
    b_ref[own : own + down, :] = part(wd_ref, 0)
    b_ref[own + down :, :] = jnp.broadcast_to(gain_ref[...], (16, half))
    for j in range(3):
        rows = pl.ds(pl.multiple_of(info_ref[3] * sub, sub), sub)
        a_ref[j * sub : (j + 1) * sub, :] = part(wi_ref, j, rows)


def pack(info, w_qkv, w_out, w_in, w_down, gain):
    own = w_qkv.shape[0]
    wide = WIDE
    return pl.pallas_call(
        pack_kernel,
        out_shape=(
            jax.ShapeDtypeStruct((2 * own, wide), BF16),
            jax.ShapeDtypeStruct((own // 2 * 3, wide), BF16),
            jax.ShapeDtypeStruct((own + w_down.shape[0] + 16, wide), BF16),
        ),
        in_specs=[SCALAR] + [LOCAL] * 5,
        out_specs=(LOCAL,) * 3,
        compiler_params=pltpu.CompilerParams(vmem_limit_bytes=12 << 20),
        name="pack",
    )(info, w_qkv, w_out, w_in, w_down, gain)


def halves_kernel(at_ref, mine_ref, in_ref, away_ref, here_ref, *, axis):
    size = here_ref.shape[axis]
    at = at_ref[0]

    def part(ref, index):
        start = pl.multiple_of(index * size, size)
        if axis == 0:
            return ref[pl.ds(start, size)].astype(F32)
        return ref[:, pl.ds(start, size)].astype(F32)

    away_ref[...] = (part(mine_ref, 1 - at) + part(in_ref, 1 - at)).astype(BF16)
    here_ref[...] = (part(mine_ref, at) + part(in_ref, at)).astype(BF16)


def halves(mine, received, at, axis, after=()):
    shape = list(mine.shape)
    shape[axis] //= 2
    out = jax.ShapeDtypeStruct(tuple(shape), BF16)
    return pl.pallas_call(
        skip(functools.partial(halves_kernel, axis=axis), 3, len(after)),
        out_shape=(out, out),
        in_specs=[SCALAR, LOCAL, LOCAL] + [FAR] * len(after),
        out_specs=(LOCAL, LOCAL),
        compiler_params=pltpu.CompilerParams(vmem_limit_bytes=8 << 20),
        cost_estimate=cost("halves"),
        name="halves",
    )(at.astype(jnp.int32)[None], mine, received, *after)


def last_kernel(info_ref, tok_ref, gain_ref, away_ref, *refs, step):
    d_refs, (w0_ref, w1_ref, w2_ref, dx_ref, out_ref, token_ref) = refs[:6], refs[6:]
    token_ref[...] = jnp.zeros_like(token_ref)
    group = info_ref[1]
    gain_own = gain_ref[...].astype(F32)
    gain_away = away_ref[0:1, :].astype(F32)
    gain = jnp.where(
        group == 0,
        jnp.concatenate([gain_own, gain_away], axis=1),
        jnp.concatenate([gain_away, gain_own], axis=1),
    )

    def body(block, _):
        rows = pl.ds(pl.multiple_of(block * step, step), step)
        field = tok_ref[rows, :].astype(F32)
        center = field - jnp.mean(field, axis=1, keepdims=True)
        rate = lax.rsqrt(jnp.mean(center * center, axis=1, keepdims=True) + norm_eps)
        unit = center * rate
        e = jnp.zeros(field.shape, F32)
        for chunk, w_ref in enumerate((w0_ref, w1_ref, w2_ref)):
            pairs = [d_refs[2 * chunk + i][rows, :] for i in range(2)]
            e += dot_nt(jnp.concatenate(pairs, axis=1), w_ref[...])
        e *= gain
        out_ref[rows, :] = dx_ref[rows, :] + rate * (
            e
            - jnp.mean(e, axis=1, keepdims=True)
            - unit * jnp.mean(e * unit, axis=1, keepdims=True)
        )
        return 0

    lax.fori_loop(0, tok_ref.shape[0] // step, body, 0)


def last(info, tokens, gain, away, d_qkv, full, d_x1, after=(), step=256):
    return pl.pallas_call(
        skip(functools.partial(last_kernel, step=step), 14, len(after)),
        out_shape=(jax.ShapeDtypeStruct(d_x1.shape, F32), jax.ShapeDtypeStruct((8, 128), F32)),
        in_specs=[SCALAR] + [LOCAL] * 13 + [FAR] * len(after),
        out_specs=(LOCAL, LOCAL),
        compiler_params=pltpu.CompilerParams(vmem_limit_bytes=LIMITS["last"] << 20),
        cost_estimate=cost("last"),
        name="last",
    )(info, tokens, gain, away, *d_qkv, *full, d_x1, *after)


def row_of(column):
    return jnp.broadcast_to(column, (column.shape[0], 128)).T[0:1, :]


def spread_early_kernel(
    info_ref, ma_ref, mb_ref, oa_ref, ob_ref, w_ref, gain_ref, in_ref, out_ref, down_ref, dg_ref
):
    core = info_ref[2]
    own = out_ref.shape[0]
    down = down_ref.shape[0]
    half = out_ref.shape[1] // 2

    def part_of(i, mine_ref, other_ref, start, size):
        mine = mine_ref[start : start + size, :].astype(F32)
        other = other_ref[start : start + size, :].astype(F32)
        return jnp.where(core == i, mine, other)

    total = jnp.zeros((own, 1), F32)
    for i in range(2):
        for j in range(3):
            at = (3 * i + j) * half
            part = part_of(i, ma_ref, oa_ref, j * own, own)
            in_ref[:, at : at + half] = part
            total += jnp.sum(part * w_ref[:, at : at + half].astype(F32), axis=1, keepdims=True)
        out_ref[:, i * half : (i + 1) * half] = part_of(i, mb_ref, ob_ref, 0, own)
        down_ref[:, i * half : (i + 1) * half] = part_of(i, mb_ref, ob_ref, own, down)
    dg_ref[...] = (row_of(total) / gain_ref[...].astype(F32))[0]


def spread_early(info, mine, other, w_in, gain, down):
    own = w_in.shape[0]
    return pl.pallas_call(
        spread_early_kernel,
        out_shape=(
            jax.ShapeDtypeStruct(w_in.shape, F32),
            jax.ShapeDtypeStruct((own, 2 * own), F32),
            jax.ShapeDtypeStruct((down, 2 * own), F32),
            jax.ShapeDtypeStruct((own,), F32),
        ),
        in_specs=[SCALAR] + [LOCAL] * 6,
        out_specs=(LOCAL,) * 4,
        compiler_params=pltpu.CompilerParams(vmem_limit_bytes=LIMITS["spread"] << 20),
        cost_estimate=cost("spread"),
        name="spread_early",
    )(info, *mine, *other, w_in, gain)


def spread_late_kernel(info_ref, m01_ref, o01_ref, m2_ref, o2_ref, w_ref, gain_ref, out_ref, dg_ref):
    core = info_ref[2]
    own = w_ref.shape[0]
    total = jnp.zeros((own, 1), F32)
    for chunk in range(3):
        mine_ref, other_ref = (m2_ref, o2_ref) if chunk == 2 else (m01_ref, o01_ref)
        start = own if chunk == 1 else 0
        mine = mine_ref[start : start + own, :].astype(F32)
        other = other_ref[start : start + own, :].astype(F32)
        whole = jnp.concatenate(
            [jnp.where(core == 0, mine, other), jnp.where(core == 0, other, mine)], axis=1
        )
        for i in range(6):
            at = (i % 3) * HEADS * HEAD_DIM + chunk * SPAN + (i // 3) * PAIR
            part = whole[:, i * PAIR : (i + 1) * PAIR]
            out_ref[:, at : at + PAIR] = part
            total += jnp.sum(part * w_ref[:, at : at + PAIR].astype(F32), axis=1, keepdims=True)
    dg_ref[...] = (row_of(total) / gain_ref[...].astype(F32))[0]


def spread_late(info, first, second, w_qkv, gain):
    own = w_qkv.shape[0]
    return pl.pallas_call(
        spread_late_kernel,
        out_shape=(jax.ShapeDtypeStruct(w_qkv.shape, F32), jax.ShapeDtypeStruct((own,), F32)),
        in_specs=[SCALAR] + [LOCAL] * 6,
        out_specs=(LOCAL, LOCAL),
        compiler_params=pltpu.CompilerParams(vmem_limit_bytes=LIMITS["spread"] << 20),
        cost_estimate=cost("spread"),
        name="spread_late",
    )(info, *first, *second, w_qkv, gain)


def pull_kernel(
    info_ref, qkv_ref, mixed_ref, dm_ref, lse_ref, turn_ref, out_ref, token_ref,
    qa_ref, ka_ref, kt_ref, dv_ref, dk_ref, *, pair, step,
):
    length = qkv_ref.shape[0]
    valid = info_ref[0]
    lane = lax.broadcasted_iota(jnp.int32, (step, PAIR), 1)
    one = jnp.ones((), BF16)
    zero = jnp.zeros((), BF16)
    token_ref[...] = jnp.zeros_like(token_ref)
    inner = pair % 2
    for at in range(0, length, step):
        rows = pl.ds(at, step)
        row = lax.broadcasted_iota(jnp.int32, (step, PAIR), 0) + at
        bias = jnp.where(row < valid, 0.0, NEG).astype(BF16)
        q = qkv_ref[rows, :PAIR]
        k = qkv_ref[rows, PAIR : 2 * PAIR]
        kt_ref[:, rows] = k.T
        for side in range(2):
            mine = (lane // HEAD_DIM) == side
            spare = lane == (1 - side) * HEAD_DIM
            qa_ref[side, rows, :] = jnp.where(mine, q, jnp.where(spare, one, zero))
            ka_ref[side, rows, :] = jnp.where(mine, k, jnp.where(spare, bias, zero))
    dv_ref[...] = jnp.zeros_like(dv_ref)
    dk_ref[...] = jnp.zeros_like(dk_ref)
    half_rows = lax.broadcasted_iota(jnp.int32, (8, PAIR), 0)
    half_lane = lax.broadcasted_iota(jnp.int32, (8, PAIR), 1)
    chooser = jnp.where(half_lane // HEAD_DIM == half_rows, 1.0, 0.0).astype(BF16)

    def body(block, _):
        rows = pl.ds(pl.multiple_of(block * step, step), step)
        dm = dm_ref[rows, pair * PAIR : (pair + 1) * PAIR]
        product = dm.astype(F32) * mixed_ref[rows, inner * PAIR : (inner + 1) * PAIR].astype(F32)
        high = product.astype(BF16)
        low = (product - high.astype(F32)).astype(BF16)
        delta = dot_nt(chooser, high) + dot_nt(chooser, low)
        dmt = dm.T
        qt = qkv_ref[rows, :PAIR].T
        outs = []
        for side in range(2):
            head = 2 * inner + side
            part = slice(side * HEAD_DIM, (side + 1) * HEAD_DIM)
            dms = jnp.where((lane // HEAD_DIM) == side, dm, zero)
            scores = dot_nt(ka_ref[side], qa_ref[side, rows, :])
            weights = jnp.exp2(scores - lse_ref[head : head + 1, rows])
            d_weights = dot_nt(qkv_ref[:, 2 * PAIR :], dms)
            d_scores = (weights * (d_weights - delta[side : side + 1, :])).astype(BF16)
            dv_ref[part, :] += dot_nt(dmt[part, :], weights.astype(BF16))
            dk_ref[part, :] += dot_nt(qt[part, :], d_scores)
            outs.append(dot_nn(kt_ref[part, :], d_scores))
        dq = jnp.concatenate(outs, axis=0).T * (1.0 / math.sqrt(HEAD_DIM))
        dq = dq * turn_ref[rows, :PAIR] - swap_halves(dq) * turn_ref[rows, PAIR:]
        out_ref[rows, :PAIR] = dq.astype(BF16)
        return 0

    lax.fori_loop(0, length // step, body, 0)
    for at in range(0, length, step):
        rows = pl.ds(at, step)
        dk = dk_ref[:, rows].T * LN2
        dk = dk * turn_ref[rows, :PAIR] - swap_halves(dk) * turn_ref[rows, PAIR:]
        out_ref[rows, PAIR : 2 * PAIR] = dk.astype(BF16)
        out_ref[rows, 2 * PAIR :] = dv_ref[:, rows].T.astype(BF16)


def pull(info, qkv, mixed, d_mixed, lse, turn, pair, after=(), step=256):
    rows = qkv.shape[0]
    return pl.pallas_call(
        skip(functools.partial(pull_kernel, pair=pair, step=step), 6, len(after)),
        out_shape=(jax.ShapeDtypeStruct((rows, WIDE), BF16), jax.ShapeDtypeStruct((8, 128), F32)),
        in_specs=[SCALAR] + [LOCAL] * 5 + [FAR] * len(after),
        out_specs=(LOCAL, LOCAL),
        scratch_shapes=[
            pltpu.VMEM((2, rows, PAIR), BF16),
            pltpu.VMEM((2, rows, PAIR), BF16),
            pltpu.VMEM((PAIR, rows), BF16),
            pltpu.VMEM((PAIR, rows), F32),
            pltpu.VMEM((PAIR, rows), F32),
        ],
        compiler_params=pltpu.CompilerParams(vmem_limit_bytes=LIMITS["pull"] << 20),
        cost_estimate=cost("pull"),
        name=f"pull_{pair}",
    )(info, qkv, mixed, d_mixed, lse, turn, *after)


def both_kernel(left_ref, right_ref, out_ref):
    out_ref[...] = (left_ref[...].astype(F32) + right_ref[...].astype(F32)).astype(BF16)


def both(left, right, after=()):
    return pl.pallas_call(
        skip(both_kernel, 2, len(after)),
        out_shape=jax.ShapeDtypeStruct(left.shape, BF16),
        in_specs=[LOCAL, LOCAL] + [FAR] * len(after),
        out_specs=LOCAL,
        compiler_params=pltpu.CompilerParams(vmem_limit_bytes=8 << 20),
        cost_estimate=cost("halves"),
        name="both",
    )(left, right, *after)


def swap_replica(field, bit):
    count = lax.axis_size("replica")
    return lax.ppermute(field, "replica", [(i, i ^ bit) for i in range(count)])


def swap_group(field):
    return lax.ppermute(field, "group", [(0, 1), (1, 0)])


def pick(field, index, axis):
    size = field.shape[axis] // 2
    return lax.dynamic_slice_in_dim(field, index * size, size, axis)


def in_order(mine, other, index, axis):
    return jnp.where(
        index == 0,
        jnp.concatenate([mine, other], axis=axis),
        jnp.concatenate([other, mine], axis=axis),
    )


def add_low(left, right):
    return (left.astype(F32) + right.astype(F32)).astype(BF16)


def hold(value, *others):
    return lax.optimization_barrier((value, others))[0]


def further_bits():
    bits = [4, 12]
    bit = 16
    while bit < lax.axis_size("replica"):
        bits.append(bit)
        bit *= 2
    return bits


def on_device(tokens, lengths, w_qkv, w_out, gain_one, w_in, w_down, gain_two, cotangent):
    rows = tokens.shape[1]
    group = lax.axis_index("group")
    replica = lax.axis_index("replica")
    core = replica % 2
    second = (replica // 2) % 2
    info = jnp.stack([lengths[0], group, core, second]).astype(jnp.int32)
    cos_rows, sin_rows = angle_tables(rows)
    turn = jnp.asarray(np.concatenate([cos_rows, sin_rows], axis=1))

    field = tokens[0]
    cot = cotangent[0]
    qkv, mixed, lse, full = [None] * 6, [None] * 3, [None] * 3, [None] * 3
    far0 = swap_group(pack_first(info, w_qkv, gain_one[None]))
    send, send_a, send_b = pack(info, w_qkv, w_out, w_in, w_down, gain_two[None])
    far0, send = lax.optimization_barrier((far0, send))
    far1 = swap_group(send)
    qkv[0], qkv[1], full[0], lse[0], mixed[0], h1 = attend(
        info, field, gain_one[None], w_qkv, (far0, swap_replica(far0, 1)), turn, 0
    )
    lse[0], send_a, far1 = lax.optimization_barrier((lse[0], send_a, far1))
    far_a = swap_group(send_a)
    near1 = swap_replica(far1, 1)
    near1, send_b = lax.optimization_barrier((near1, send_b))
    far_b = swap_group(send_b)
    qkv[2], qkv[3], full[1], lse[1], mixed[1] = attend(
        info, h1, None, w_qkv, (far1, near1), turn, 1, (lse[0],)
    )
    lse[1], far_a = lax.optimization_barrier((lse[1], far_a))
    far_c = swap_replica(far_a, 2)
    near_a = swap_replica(far_a, 1)
    qkv[4], qkv[5], full[2], lse[2], mixed[2] = attend(
        info, h1, None, w_qkv, (far1, near1), turn, 2, (lse[1],)
    )
    lse[2], far_b, far_c = lax.optimization_barrier((lse[2], far_b, far_c))
    parts_rest = (far_b, swap_replica(far_b, 1), far_a, near_a, far_c, swap_replica(far_c, 1))
    output, d_x1, dx_low, d_mixed, h2, act, d_up = middle(
        info, field, mixed, cot, gain_two[None], w_out, w_in, w_down, parts_rest
    )
    mine = core.astype(jnp.int32)[None]
    theirs = 1 - mine

    def tug(pair, *after):
        return pull(
            info, qkv[pair], mixed[pair // 2], d_mixed, lse[pair // 2], turn, pair, after
        )

    d_qkv = [None] * 6
    a_send, token = early_in(theirs, h2, d_up)
    a_in = swap_replica(a_send, 1)
    b_send, token = early_rest(theirs, act, cot, mixed, dx_low, (token,))
    b_in = swap_replica(b_send, 1)
    a_mine, token = early_in(mine, h2, d_up, (token,))
    a_away, a_here = halves(a_mine, a_in, group, 0)
    a_in = swap_group(a_away)
    b_mine, token = early_rest(mine, act, cot, mixed, dx_low, (a_away,))
    b_away, b_here = halves(b_mine, b_in, second, 1)
    b_in = swap_replica(b_away, 2)

    d_qkv[0], token = tug(0, b_away)
    d_qkv[1], token = tug(1, token)
    a_away, a_here = halves(a_here[0], a_in[0], second, 0, (token,))
    a_in = swap_replica(a_away, 2)
    b_away, b_here = halves(b_here, b_in, group, 0, (a_away,))
    b_in = swap_group(b_away)
    d_qkv[2], token = tug(2, b_away)
    d_qkv[3], token = tug(3, token)
    early_mine = jnp.concatenate([a_here, b_here[0]], axis=0)
    early_in_sum = jnp.concatenate([a_in, b_in[0]], axis=0)
    bits = further_bits()
    at = (replica // 4 + replica // 8) % 2
    l_send, token = late(theirs, h1, d_qkv[:4], (token,))
    l_in = swap_replica(l_send, 1)
    l_mine, token = late(mine, h1, d_qkv[:4], (token,))
    l_away, l_here = halves(l_mine, l_in, group, 0)
    l_in = swap_group(l_away)
    token = l_away
    e_away, e_here = halves(early_mine, early_in_sum, at, 0, (token,))
    e_in = swap_replica(e_away, bits[0])
    token = e_away
    d_qkv[4], token = tug(4, token)
    e_sum = both(e_here, e_in, (token,))
    e_in = swap_replica(e_sum, bits[1])
    token = e_sum
    d_qkv[5], token = tug(5, token)
    m_send, token = late(theirs, h1, d_qkv[4:], (token,))
    m_in = swap_replica(m_send, 1)
    l_away, l_here = halves(l_here[0], l_in[0], second, 0, (token,))
    l_in = swap_replica(l_away, 2)
    token = l_away
    m_mine, token = late(mine, h1, d_qkv[4:], (token,))
    m_away, m_here = halves(m_mine, m_in, group, 0)
    m_in = swap_group(m_away)
    token = m_away

    def across(total, todo):
        for bit in todo:
            total = add_low(total, swap_replica(total, bit))
        return total

    grad_tokens, token = last(
        info, field, gain_one[None], far0[w_qkv.shape[0] :], d_qkv, full, d_x1, (token,)
    )
    m_away, m_here = halves(m_here[0], m_in[0], second, 0, (token,))
    m_in = swap_replica(m_away, 2)
    e_sum = across(add_low(e_sum, e_in), bits[2:])
    e_back = swap_replica(e_sum, bits[0])
    e_sum = in_order(e_sum, e_back, at, 0)
    e_other = swap_replica(e_sum, 2)
    l_sum = across(add_low(l_here, l_in), bits)
    m_sum = across(add_low(m_here, m_in), bits)
    cut = a_here.shape[0]
    whole_a = in_order(e_sum[:cut], e_other[:cut], second, 0)
    whole_b = in_order(e_sum[cut:], e_other[cut:], second, 0)
    l_sum = in_order(l_sum, swap_replica(l_sum, 2), second, 0)
    m_sum = in_order(m_sum, swap_replica(m_sum, 2), second, 0)
    grad_in, grad_out, grad_down, grad_two = spread_early(
        info,
        (whole_a, whole_b),
        (swap_replica(whole_a, 1), swap_replica(whole_b, 1)),
        w_in,
        gain_two[None],
        w_down.shape[0],
    )
    grad_qkv, grad_one = spread_late(
        info, (l_sum, swap_replica(l_sum, 1)), (m_sum, swap_replica(m_sum, 1)), w_qkv, gain_one[None]
    )
    return (
        output[None],
        grad_tokens[None],
        grad_qkv,
        grad_out,
        grad_one,
        grad_in,
        grad_down,
        grad_two,
    )


def solution(mesh):
    both = P(("group", "replica"), None, None)
    rows = P("group", None)
    vector = P("group")
    return jax.shard_map(
        on_device,
        mesh=mesh,
        in_specs=(both, P(("group", "replica")), rows, rows, vector, rows, rows, vector, both),
        out_specs=(both, both, rows, rows, vector, rows, rows, vector),
        check_vma=False,
    )
```

```python
import functools
import math

import jax
import jax.numpy as jnp
import numpy as np
from jax import lax
from jax.experimental import pallas as pl
from jax.experimental.pallas import tpu as pltpu
from jax.sharding import PartitionSpec as P

HEADS = 12
HEAD_DIM = 64
theta_base = 160000.0
norm_eps = 1e-05
LOG2E = 1.4426950408889634
LN2 = 0.6931471805599453
F32 = jnp.float32
BF16 = jnp.bfloat16
PAIR = 2 * HEAD_DIM
GROUP_HEADS = 4
SPAN = GROUP_HEADS * HEAD_DIM
WIDE = 3 * PAIR
NEG = -1e30
LOCAL = pl.BlockSpec(memory_space=pltpu.VMEM)
SCALAR = pl.BlockSpec(memory_space=pltpu.SMEM)
FAR = pl.BlockSpec(memory_space=pl.ANY)
STORED = pl.BlockSpec(memory_space=pltpu.HBM)


def dot_nn(a, b):
    return lax.dot_general(a, b, (((1,), (0,)), ((), ())), preferred_element_type=F32)


def dot_nt(a, b):
    return lax.dot_general(a, b, (((1,), (1,)), ((), ())), preferred_element_type=F32)


def dot_tn(a, b):
    return lax.dot_general(a, b, (((0,), (0,)), ((), ())), preferred_element_type=F32)


def angle_tables(length):
    half = HEAD_DIM // 2
    freq = np.exp(-math.log(theta_base) * 2.0 * np.arange(half, dtype=np.float64) / HEAD_DIM)
    angle = np.arange(length, dtype=np.float64)[:, None] * freq.astype(np.float32).astype(np.float64)[None]
    cosine = np.cos(angle)
    sine = np.sin(angle)
    cos_rows = np.concatenate([cosine] * 4, axis=1).astype(np.float32)
    sin_rows = np.concatenate([-sine, sine, -sine, sine], axis=1).astype(np.float32)
    return cos_rows, sin_rows


def swap_halves(field):
    half = HEAD_DIM // 2
    lane = lax.broadcasted_iota(jnp.int32, field.shape, 1)
    return jnp.where(
        (lane // half) % 2 == 0, pltpu.roll(field, PAIR - half, 1), pltpu.roll(field, half, 1)
    )


def erf_exp(u):
    return lax.erf(u * (1.0 / math.sqrt(2.0))), jnp.exp(-0.5 * u * u)


LIMITS = {"attend": 16, "middle": 24, "early_in": 8, "early_rest": 8, "pull": 12, "late": 6, "last": 12, "spread": 12}
LENGTHS = {"attend": 3, "middle": 28, "early_in": 3, "early_rest": 3, "pull": 5, "late": 2, "last": 8, "spread": 3, "halves": 1}


def cost(name):
    return pl.CostEstimate(flops=LENGTHS[name] * 1_000_000_000, transcendentals=0, bytes_accessed=0)


def skip(kernel, at, count):
    return lambda *refs: kernel(*refs[:at], *refs[at + count :])


def start_all(copies):
    for copy in copies:
        copy.start()


def attend_kernel(*refs, chunk, first, step):
    if first:
        (info_ref, tok_ref, gain_ref, w_ref, mine_ref, other_ref, turn_ref,
         qkva_ref, qkvb_ref, full_ref, lse_ref, mixed_ref, h_ref,
         vt_ref, qa_ref, ka_ref, s_ref, row_ref, sems) = refs
    else:
        (info_ref, h_ref, w_ref, mine_ref, other_ref, turn_ref,
         qkva_ref, qkvb_ref, full_ref, lse_ref, mixed_ref,
         vt_ref, qa_ref, ka_ref, s_ref, sems) = refs
    rows_all = h_ref.shape[0]
    own = w_ref.shape[0]
    valid = info_ref[0]
    group = info_ref[1]
    core = info_ref[2]
    there = pl.ds(pl.multiple_of(group * own, own), own)
    away = pl.ds(pl.multiple_of((1 - group) * own, own), own)
    copies = []
    for pair in range(2):
        for i in range(3):
            copies.append(
                pltpu.make_async_copy(
                    w_ref.at[:, pl.ds(i * HEADS * HEAD_DIM + chunk * SPAN + pair * PAIR, PAIR)],
                    full_ref.at[there, pl.ds(pair * WIDE + i * PAIR, PAIR)],
                    sems.at[3 * pair + i],
                )
            )
    for i, (part, side) in enumerate(((mine_ref, core), (other_ref, 1 - core))):
        copies.append(
            pltpu.make_async_copy(
                part.at[pl.ds(own if chunk == 2 else 0, own)],
                full_ref.at[away, pl.ds(pl.multiple_of(side * WIDE, WIDE), WIDE)],
                sems.at[6 + i],
            )
        )
    if first:
        copies.append(pltpu.make_async_copy(mine_ref.at[pl.ds(own, 16)], row_ref, sems.at[8]))
    start_all(copies)
    if first:
        copies[-1].wait()
        copies = copies[:-1]
        gain_own = gain_ref[...].astype(F32)
        gain_away = row_ref[0:1, :].astype(F32)
        gain = jnp.where(
            group == 0,
            jnp.concatenate([gain_own, gain_away], axis=1),
            jnp.concatenate([gain_away, gain_own], axis=1),
        )

        def normalize(block, _):
            rows = pl.ds(pl.multiple_of(block * step, step), step)
            field = tok_ref[rows, :].astype(F32)
            center = field - jnp.mean(field, axis=1, keepdims=True)
            spread = jnp.mean(center * center, axis=1, keepdims=True)
            h_ref[rows, :] = (center * lax.rsqrt(spread + norm_eps) * gain).astype(BF16)
            return 0

        lax.fori_loop(0, rows_all // step, normalize, 0)
    for copy in copies:
        copy.wait()
    lane = lax.broadcasted_iota(jnp.int32, (step, PAIR), 1)

    def project(block, _):
        rows = pl.ds(pl.multiple_of(block * step, step), step)
        merged = dot_nn(h_ref[rows, :], full_ref[...])
        cosine = turn_ref[rows, :PAIR]
        sine = turn_ref[rows, PAIR:]
        row = lax.broadcasted_iota(jnp.int32, (step, PAIR), 0) + block * step
        bias = jnp.where(row < valid, 0.0, NEG)
        for pair, qkv_ref in enumerate((qkva_ref, qkvb_ref)):
            left = pair * WIDE
            q = merged[:, left : left + PAIR]
            k = merged[:, left + PAIR : left + 2 * PAIR]
            v = merged[:, left + 2 * PAIR : left + WIDE].astype(BF16)
            q = (q * cosine + swap_halves(q) * sine) * (LOG2E / math.sqrt(HEAD_DIM))
            k = k * cosine + swap_halves(k) * sine
            qkv_ref[rows, :PAIR] = q.astype(BF16)
            qkv_ref[rows, PAIR : 2 * PAIR] = k.astype(BF16)
            qkv_ref[rows, 2 * PAIR :] = v
            vt_ref[pair, :, rows] = v.T
            for side in range(2):
                mine = (lane // HEAD_DIM) == side
                spare = lane == (1 - side) * HEAD_DIM
                qa_ref[2 * pair + side, rows, :] = jnp.where(
                    mine, q, jnp.where(spare, 1.0, 0.0)
                ).astype(BF16)
                ka_ref[2 * pair + side, rows, :] = jnp.where(
                    mine, k, jnp.where(spare, bias, 0.0)
                ).astype(BF16)
        return 0

    blocks = rows_all // step
    lax.fori_loop(0, blocks, project, 0)
    ones = jnp.ones((16, step), BF16)

    def score(head, block, part, slot, top):
        rows = pl.ds(pl.multiple_of(block * step, step), step)
        keys = pl.ds(part * step, step)
        scores = dot_nt(ka_ref[head, keys, :], qa_ref[head, rows, :])
        s_ref[slot, keys, :] = scores
        here = jnp.max(scores, axis=0, keepdims=True)
        return here if top is None else jnp.maximum(top, here)

    def body(block, top):
        rows = pl.ds(pl.multiple_of(block * step, step), step)
        outs = []
        for head in range(GROUP_HEADS):
            pair, side = divmod(head, 2)
            slot = head % 2
            following = (head + 1) % GROUP_HEADS
            next_block = block if head + 1 < GROUP_HEADS else jnp.minimum(block + 1, blocks - 1)
            result = jnp.zeros((HEAD_DIM + 16, step), F32)
            next_top = None
            for part in range(blocks):
                keys = pl.ds(part * step, step)
                next_top = score(following, next_block, part, 1 - slot, next_top)
                weights = jnp.exp2(s_ref[slot, keys, :] - top).astype(BF16)
                values = jnp.concatenate(
                    [vt_ref[pair, side * HEAD_DIM : (side + 1) * HEAD_DIM, keys], ones], axis=0
                )
                result += dot_nn(values, weights)
            total = result[HEAD_DIM : HEAD_DIM + 1, :]
            outs.append(result[:HEAD_DIM, :] / total)
            lse_ref[head : head + 1, rows] = top + jnp.log2(total)
            top = next_top
            if side == 1:
                mixed_ref[rows, pair * PAIR : (pair + 1) * PAIR] = (
                    jnp.concatenate(outs[-2:], axis=0).T.astype(BF16)
                )
        return top

    top = None
    for part in range(blocks):
        top = score(0, 0, part, 0, top)
    lax.fori_loop(0, blocks, body, top)


def attend(info, source, gain, w, parts, turn, chunk, after=(), step=256):
    rows = source.shape[0]
    width = 2 * w.shape[0]
    first = gain is not None
    stored = [
        ((rows, WIDE), BF16),
        ((rows, WIDE), BF16),
        ((width, 3 * SPAN), BF16),
        ((8, rows), F32),
    ]
    out_shape = [jax.ShapeDtypeStruct(*s) for s in stored]
    out_shape.append(jax.ShapeDtypeStruct((rows, SPAN), BF16))
    scratch = [
        pltpu.VMEM((SPAN // PAIR, PAIR, rows), BF16),
        pltpu.VMEM((GROUP_HEADS, rows, PAIR), BF16),
        pltpu.VMEM((GROUP_HEADS, rows, PAIR), BF16),
        pltpu.VMEM((2, rows, step), F32),
    ]
    inputs = [info, source]
    specs = [SCALAR, LOCAL]
    if first:
        out_shape.append(jax.ShapeDtypeStruct((rows, width), BF16))
        scratch.append(pltpu.VMEM((16, WIDE), BF16))
        inputs.append(gain)
        specs.append(LOCAL)
    inputs += [w, *parts, turn]
    specs += [FAR, FAR, FAR, LOCAL]
    kernel = functools.partial(attend_kernel, chunk=chunk, first=first, step=step)
    kernel = skip(kernel, len(inputs), len(after))
    inputs += after
    specs += [FAR] * len(after)
    scratch.append(pltpu.SemaphoreType.DMA((9,)))
    return pl.pallas_call(
        kernel,
        out_shape=tuple(out_shape),
        in_specs=specs,
        out_specs=tuple([LOCAL] * len(out_shape)),
        scratch_shapes=scratch,
        compiler_params=pltpu.CompilerParams(vmem_limit_bytes=LIMITS["attend"] << 20),
        cost_estimate=cost("attend"),
        name=f"attend_{chunk}",
    )(*inputs)


def middle_kernel(
    info_ref, tok_ref, mix0_ref, mix1_ref, mix2_ref, cot_ref, gain_ref,
    wo_ref, wi_ref, wd_ref, *refs, step,
):
    parts, refs = refs[:6], refs[6:]
    (out_ref, dx_ref, dxl_ref, dm_ref, h_ref, act_ref, du_ref,
     fo_ref, fi_ref, fd_ref, row_ref, sems) = refs
    rows_all, width = tok_ref.shape
    own = wo_ref.shape[0]
    down = wd_ref.shape[0]
    half = width // 2
    hidden = fd_ref.shape[0]
    valid = info_ref[0]
    group = info_ref[1]
    core = info_ref[2]

    def at(start, size):
        return pl.ds(pl.multiple_of(start, size), size)

    copies = [
        pltpu.make_async_copy(wo_ref, fo_ref.at[at(group * own, own)], sems.at[0]),
        pltpu.make_async_copy(wi_ref, fi_ref.at[at(group * own, own)], sems.at[1]),
        pltpu.make_async_copy(wd_ref, fd_ref.at[at(group * down, down)], sems.at[2]),
        pltpu.make_async_copy(parts[0].at[pl.ds(own + down, 16)], row_ref, sems.at[3]),
    ]
    sub = own // 2
    second = info_ref[3]
    for i, side in enumerate((core, 1 - core)):
        base = 4 + 8 * i
        part = parts[i]
        copies.append(
            pltpu.make_async_copy(
                part.at[pl.ds(0, own)],
                fo_ref.at[at((1 - group) * own, own), at(side * half, half)],
                sems.at[base],
            )
        )
        copies.append(
            pltpu.make_async_copy(
                part.at[pl.ds(own, down)],
                fd_ref.at[at((1 - group) * down, down), at(side * half, half)],
                sems.at[base + 1],
            )
        )
        for k, which in enumerate((second, 1 - second)):
            part = parts[2 + 2 * k + i]
            for j in range(3):
                copies.append(
                    pltpu.make_async_copy(
                        part.at[pl.ds(j * sub, sub)],
                        fi_ref.at[
                            at((1 - group) * own + which * sub, sub), at(side * 3 * half + j * half, half)
                        ],
                        sems.at[base + 2 + 3 * k + j],
                    )
                )
    start_all(copies)
    for copy in copies:
        copy.wait()
    gain_own = gain_ref[...].astype(F32)
    gain_away = row_ref[0:1, :].astype(F32)
    gain = jnp.where(
        group == 0,
        jnp.concatenate([gain_own, gain_away], axis=1),
        jnp.concatenate([gain_away, gain_own], axis=1),
    )

    def body(block, _):
        rows = pl.ds(pl.multiple_of(block * step, step), step)
        mixed = jnp.concatenate([mix0_ref[rows, :], mix1_ref[rows, :], mix2_ref[rows, :]], axis=1)
        x1 = tok_ref[rows, :].astype(F32) + dot_nn(mixed, fo_ref[...])
        center = x1 - jnp.mean(x1, axis=1, keepdims=True)
        rate = lax.rsqrt(jnp.mean(center * center, axis=1, keepdims=True) + norm_eps)
        unit = center * rate
        h2 = (unit * gain).astype(BF16)
        h_ref[rows, :] = h2
        row = lax.broadcasted_iota(jnp.int32, (step, 1), 0) + block * step
        keep = row < valid
        up = dot_nn(h2, fi_ref[...])
        turned = up[:, :hidden]
        gate = up[:, hidden:]
        curve, bell = erf_exp(turned)
        share = 0.5 * (1.0 + curve)
        bent = turned * share
        act = (bent * gate).astype(BF16)
        act_ref[rows, :] = jnp.where(keep, act, jnp.zeros((), BF16))
        result = x1 + dot_nn(act, fd_ref[...])
        out_ref[rows, :] = jnp.where(keep, result, 0.0).astype(BF16)
        dy = jnp.where(keep, cot_ref[rows, :], jnp.zeros((), BF16))
        d_act = dot_nt(dy, fd_ref[...])
        slope = share + turned * bell * (1.0 / math.sqrt(2.0 * math.pi))
        d_up = jnp.concatenate([d_act * gate * slope, d_act * bent], axis=1).astype(BF16)
        du_ref[rows, :] = d_up
        e = dot_nt(d_up, fi_ref[...]) * gain
        d_x1 = dy.astype(F32) + rate * (
            e
            - jnp.mean(e, axis=1, keepdims=True)
            - unit * jnp.mean(e * unit, axis=1, keepdims=True)
        )
        dx_ref[rows, :] = d_x1
        low = d_x1.astype(BF16)
        dxl_ref[rows, :] = low
        dm_ref[rows, :] = dot_nt(low, fo_ref[...]).astype(BF16)
        return 0

    lax.fori_loop(0, rows_all // step, body, 0)


def middle(info, tokens, mixed, cotangent, gain, w_out, w_in, w_down, parts, step=256):
    rows, width = tokens.shape
    hidden = 2 * w_down.shape[0]
    shapes = [
        ((rows, width), BF16),
        ((rows, width), F32),
        ((rows, width), BF16),
        ((rows, width), BF16),
        ((rows, width), BF16),
        ((rows, hidden), BF16),
        ((rows, 2 * hidden), BF16),
    ]
    return pl.pallas_call(
        functools.partial(middle_kernel, step=step),
        out_shape=tuple(jax.ShapeDtypeStruct(*s) for s in shapes),
        in_specs=[SCALAR] + [LOCAL] * 6 + [FAR] * 9,
        out_specs=tuple([LOCAL] * len(shapes)),
        scratch_shapes=[
            pltpu.VMEM((width, width), BF16),
            pltpu.VMEM((width, 2 * hidden), BF16),
            pltpu.VMEM((hidden, width), BF16),
            pltpu.VMEM((16, width // 2), BF16),
            pltpu.SemaphoreType.DMA((20,)),
        ],
        compiler_params=pltpu.CompilerParams(vmem_limit_bytes=LIMITS["middle"] << 20),
        cost_estimate=cost("middle"),
        name="middle",
    )(info, tokens, *mixed, cotangent, gain, w_out, w_in, w_down, *parts)


def early_in_kernel(half_ref, h_ref, du_ref, unit_ref, token_ref):
    token_ref[...] = jnp.zeros_like(token_ref)
    own = h_ref.shape[1] // 2
    side = pl.ds(pl.multiple_of(half_ref[0] * 3 * own, 3 * own), 3 * own)
    for group in range(2):
        whole = dot_tn(h_ref[:, group * own : (group + 1) * own], du_ref[:, side]).astype(BF16)
        for j in range(3):
            unit_ref[group, j * own : (j + 1) * own, :] = whole[:, j * own : (j + 1) * own]


def early_rest_kernel(
    half_ref, act_ref, cot_ref, m0_ref, m1_ref, m2_ref, dx_ref, unit_ref, token_ref
):
    token_ref[...] = jnp.zeros_like(token_ref)
    own = dx_ref.shape[1] // 2
    down = act_ref.shape[1] // 2
    side = pl.ds(pl.multiple_of(half_ref[0] * own, own), own)
    zero = jnp.zeros((unit_ref.shape[1] - own - down, own), BF16)
    mixed = [ref[...] for ref in (m0_ref, m1_ref, m2_ref)]
    low = dx_ref[:, side]
    grad_out = jnp.concatenate([dot_tn(m, low) for m in mixed], axis=0).astype(BF16)
    grad_down = dot_tn(act_ref[...], cot_ref[:, side]).astype(BF16)
    for group in range(2):
        unit_ref[group, :own, :] = grad_out[group * own : (group + 1) * own]
        unit_ref[group, own : own + down, :] = grad_down[group * down : (group + 1) * down]
        unit_ref[group, own + down :, :] = zero


def per_half(kernel, half, inputs, shape, name, after):
    return pl.pallas_call(
        skip(kernel, 1 + len(inputs), len(after)),
        out_shape=(jax.ShapeDtypeStruct(shape, BF16), jax.ShapeDtypeStruct((8, 128), F32)),
        in_specs=[SCALAR] + [LOCAL] * len(inputs) + [FAR] * len(after),
        out_specs=(LOCAL, LOCAL),
        compiler_params=pltpu.CompilerParams(vmem_limit_bytes=LIMITS[name] << 20),
        cost_estimate=cost(name),
        name=name,
    )(half, *inputs, *after)


def early_in(half, h2, d_up, after=()):
    own = h2.shape[1] // 2
    return per_half(early_in_kernel, half, (h2, d_up), (2, 3 * own, own), "early_in", after)


def early_rest(half, act, cotangent, mixed, dx_low, after=()):
    own = dx_low.shape[1] // 2
    filled = -(-(own + act.shape[1] // 2) // 128) * 128
    return per_half(
        early_rest_kernel,
        half,
        (act, cotangent, *mixed, dx_low),
        (2, filled, own),
        "early_rest",
        after,
    )


def late_kernel(half_ref, h_ref, *refs):
    own = h_ref.shape[1] // 2
    unit_ref, token_ref = refs[-2:]
    token_ref[...] = jnp.zeros_like(token_ref)
    pairs = [
        jnp.where(half_ref[0] == 0, first[...], second[...])
        for first, second in zip(refs[:-2:2], refs[1:-2:2])
    ]
    for group in range(2):
        left = h_ref[:, group * own : (group + 1) * own]
        for i, pair in enumerate(pairs):
            unit_ref[group, i * own : (i + 1) * own, :] = dot_tn(left, pair).astype(BF16)


def late(half, h1, d_qkv, after=()):
    own = h1.shape[1] // 2
    return per_half(
        late_kernel,
        half,
        (h1, *d_qkv),
        (2, own * len(d_qkv) // 2, WIDE),
        "late",
        after,
    )


def half_of(w_ref, chunk, core):
    sides = []
    for pair in range(2):
        starts = [i * HEADS * HEAD_DIM + chunk * SPAN + pair * PAIR for i in range(3)]
        sides.append(jnp.concatenate([w_ref[:, at : at + PAIR] for at in starts], axis=1))
    return jnp.where(core == 0, sides[0], sides[1])


def pack_first_kernel(info_ref, w_ref, gain_ref, send_ref):
    own = w_ref.shape[0]
    send_ref[:own, :] = half_of(w_ref, 0, info_ref[2])
    send_ref[own:, :] = jnp.broadcast_to(gain_ref[...], (16, send_ref.shape[1]))


def pack_first(info, w_qkv, gain):
    return pl.pallas_call(
        pack_first_kernel,
        out_shape=jax.ShapeDtypeStruct((w_qkv.shape[0] + 16, WIDE), BF16),
        in_specs=[SCALAR, LOCAL, LOCAL],
        out_specs=LOCAL,
        compiler_params=pltpu.CompilerParams(vmem_limit_bytes=8 << 20),
        name="pack_first",
    )(info, w_qkv, gain)


def pack_kernel(info_ref, w_ref, wo_ref, wi_ref, wd_ref, gain_ref, s_ref, a_ref, b_ref):
    core = info_ref[2]
    own = wo_ref.shape[0]
    down = wd_ref.shape[0]
    half = wo_ref.shape[1] // 2
    s_ref[:own, :] = half_of(w_ref, 1, core)
    s_ref[own:, :] = half_of(w_ref, 2, core)

    sub = own // 2

    def part(ref, i, rows=slice(None)):
        left = i * half
        right = ref.shape[1] // 2 + i * half
        return jnp.where(core == 0, ref[rows, left : left + half], ref[rows, right : right + half])

    b_ref[:own, :] = part(wo_ref, 0)
    b_ref[own : own + down, :] = part(wd_ref, 0)
    b_ref[own + down :, :] = jnp.broadcast_to(gain_ref[...], (16, half))
    for j in range(3):
        rows = pl.ds(pl.multiple_of(info_ref[3] * sub, sub), sub)
        a_ref[j * sub : (j + 1) * sub, :] = part(wi_ref, j, rows)


def pack(info, w_qkv, w_out, w_in, w_down, gain):
    own = w_qkv.shape[0]
    wide = WIDE
    return pl.pallas_call(
        pack_kernel,
        out_shape=(
            jax.ShapeDtypeStruct((2 * own, wide), BF16),
            jax.ShapeDtypeStruct((own // 2 * 3, wide), BF16),
            jax.ShapeDtypeStruct((own + w_down.shape[0] + 16, wide), BF16),
        ),
        in_specs=[SCALAR] + [LOCAL] * 5,
        out_specs=(LOCAL,) * 3,
        compiler_params=pltpu.CompilerParams(vmem_limit_bytes=12 << 20),
        name="pack",
    )(info, w_qkv, w_out, w_in, w_down, gain)


def halves_kernel(at_ref, mine_ref, in_ref, away_ref, here_ref, *, axis):
    size = here_ref.shape[axis]
    at = at_ref[0]

    def part(ref, index):
        start = pl.multiple_of(index * size, size)
        if axis == 0:
            return ref[pl.ds(start, size)].astype(F32)
        return ref[:, pl.ds(start, size)].astype(F32)

    away_ref[...] = (part(mine_ref, 1 - at) + part(in_ref, 1 - at)).astype(BF16)
    here_ref[...] = (part(mine_ref, at) + part(in_ref, at)).astype(BF16)


def halves(mine, received, at, axis, after=()):
    shape = list(mine.shape)
    shape[axis] //= 2
    out = jax.ShapeDtypeStruct(tuple(shape), BF16)
    return pl.pallas_call(
        skip(functools.partial(halves_kernel, axis=axis), 3, len(after)),
        out_shape=(out, out),
        in_specs=[SCALAR, LOCAL, LOCAL] + [FAR] * len(after),
        out_specs=(LOCAL, LOCAL),
        compiler_params=pltpu.CompilerParams(vmem_limit_bytes=8 << 20),
        cost_estimate=cost("halves"),
        name="halves",
    )(at.astype(jnp.int32)[None], mine, received, *after)


def last_kernel(info_ref, tok_ref, gain_ref, away_ref, *refs, step):
    d_refs, (w0_ref, w1_ref, w2_ref, dx_ref, out_ref, token_ref) = refs[:6], refs[6:]
    token_ref[...] = jnp.zeros_like(token_ref)
    group = info_ref[1]
    gain_own = gain_ref[...].astype(F32)
    gain_away = away_ref[0:1, :].astype(F32)
    gain = jnp.where(
        group == 0,
        jnp.concatenate([gain_own, gain_away], axis=1),
        jnp.concatenate([gain_away, gain_own], axis=1),
    )

    def body(block, _):
        rows = pl.ds(pl.multiple_of(block * step, step), step)
        field = tok_ref[rows, :].astype(F32)
        center = field - jnp.mean(field, axis=1, keepdims=True)
        rate = lax.rsqrt(jnp.mean(center * center, axis=1, keepdims=True) + norm_eps)
        unit = center * rate
        e = jnp.zeros(field.shape, F32)
        for chunk, w_ref in enumerate((w0_ref, w1_ref, w2_ref)):
            pairs = [d_refs[2 * chunk + i][rows, :] for i in range(2)]
            e += dot_nt(jnp.concatenate(pairs, axis=1), w_ref[...])
        e *= gain
        out_ref[rows, :] = dx_ref[rows, :] + rate * (
            e
            - jnp.mean(e, axis=1, keepdims=True)
            - unit * jnp.mean(e * unit, axis=1, keepdims=True)
        )
        return 0

    lax.fori_loop(0, tok_ref.shape[0] // step, body, 0)


def last(info, tokens, gain, away, d_qkv, full, d_x1, after=(), step=256):
    return pl.pallas_call(
        skip(functools.partial(last_kernel, step=step), 14, len(after)),
        out_shape=(jax.ShapeDtypeStruct(d_x1.shape, F32), jax.ShapeDtypeStruct((8, 128), F32)),
        in_specs=[SCALAR] + [LOCAL] * 13 + [FAR] * len(after),
        out_specs=(LOCAL, LOCAL),
        compiler_params=pltpu.CompilerParams(vmem_limit_bytes=LIMITS["last"] << 20),
        cost_estimate=cost("last"),
        name="last",
    )(info, tokens, gain, away, *d_qkv, *full, d_x1, *after)


def row_of(column):
    return jnp.broadcast_to(column, (column.shape[0], 128)).T[0:1, :]


def in_place(core, second, refs):
    mine, across, other, other_across = (ref[...] for ref in refs)
    own = (jnp.where(second == 0, mine, across), jnp.where(second == 0, across, mine))
    far = (jnp.where(second == 0, other, other_across), jnp.where(second == 0, other_across, other))
    return [
        [jnp.where(core == i, a, b) for a, b in zip(own, far)] for i in range(2)
    ]


def spread_early_kernel(info_ref, *refs):
    parts, (w_ref, gain_ref, in_ref, out_ref, down_ref, dg_ref) = refs[:4], refs[4:]
    own = out_ref.shape[0]
    down = down_ref.shape[0]
    half = out_ref.shape[1] // 2
    cut = 3 * own // 2
    total = jnp.zeros((own, 1), F32)
    for i, (low, high) in enumerate(in_place(info_ref[2], info_ref[3], parts)):
        whole = jnp.concatenate([low[:cut], high[:cut]], axis=0)
        for j in range(3):
            at = (3 * i + j) * half
            part = whole[j * own : (j + 1) * own].astype(F32)
            in_ref[:, at : at + half] = part
            total += jnp.sum(part * w_ref[:, at : at + half].astype(F32), axis=1, keepdims=True)
        rest = jnp.concatenate([low[cut:], high[cut:]], axis=0)
        out_ref[:, i * half : (i + 1) * half] = rest[:own].astype(F32)
        down_ref[:, i * half : (i + 1) * half] = rest[own : own + down].astype(F32)
    dg_ref[...] = (row_of(total) / gain_ref[...].astype(F32))[0]


def spread_early(info, parts, w_in, gain, down):
    own = w_in.shape[0]
    return pl.pallas_call(
        spread_early_kernel,
        out_shape=(
            jax.ShapeDtypeStruct(w_in.shape, F32),
            jax.ShapeDtypeStruct((own, 2 * own), F32),
            jax.ShapeDtypeStruct((down, 2 * own), F32),
            jax.ShapeDtypeStruct((own,), F32),
        ),
        in_specs=[SCALAR] + [LOCAL] * 6,
        out_specs=(LOCAL,) * 4,
        compiler_params=pltpu.CompilerParams(vmem_limit_bytes=LIMITS["spread"] << 20),
        cost_estimate=cost("spread"),
        name="spread_early",
    )(info, *parts, w_in, gain)


def spread_late_kernel(info_ref, *refs):
    first, second, (w_ref, gain_ref, out_ref, dg_ref) = refs[:4], refs[4:6], refs[6:]
    core = info_ref[2]
    own = w_ref.shape[0]
    total = jnp.zeros((own, 1), F32)
    early = [jnp.concatenate(sides, axis=0) for sides in in_place(core, info_ref[4], first)]
    mine, other = (ref[...] for ref in second)
    final = [jnp.where(core == 0, mine, other), jnp.where(core == 0, other, mine)]
    for chunk in range(3):
        start = own if chunk == 1 else 0
        for side, whole in enumerate(final if chunk == 2 else early):
            for i in range(3):
                at = i * HEADS * HEAD_DIM + chunk * SPAN + side * PAIR
                part = whole[start : start + own, i * PAIR : (i + 1) * PAIR].astype(F32)
                out_ref[:, at : at + PAIR] = part
                total += jnp.sum(part * w_ref[:, at : at + PAIR].astype(F32), axis=1, keepdims=True)
    dg_ref[...] = (row_of(total) / gain_ref[...].astype(F32))[0]


def spread_late(info, first, second, w_qkv, gain, after=()):
    own = w_qkv.shape[0]
    return pl.pallas_call(
        skip(spread_late_kernel, 9, len(after)),
        out_shape=(jax.ShapeDtypeStruct(w_qkv.shape, F32), jax.ShapeDtypeStruct((own,), F32)),
        in_specs=[SCALAR] + [LOCAL] * 8 + [FAR] * len(after),
        out_specs=(LOCAL, LOCAL),
        compiler_params=pltpu.CompilerParams(vmem_limit_bytes=LIMITS["spread"] << 20),
        cost_estimate=cost("spread"),
        name="spread_late",
    )(info, *first, *second, w_qkv, gain, *after)


def pull_kernel(
    info_ref, qkv_ref, mixed_ref, dm_ref, lse_ref, turn_ref, out_ref, token_ref,
    qa_ref, ka_ref, kt_ref, dv_ref, dk_ref, *, pair, step,
):
    length = qkv_ref.shape[0]
    valid = info_ref[0]
    lane = lax.broadcasted_iota(jnp.int32, (step, PAIR), 1)
    one = jnp.ones((), BF16)
    zero = jnp.zeros((), BF16)
    token_ref[...] = jnp.zeros_like(token_ref)
    inner = pair % 2
    for at in range(0, length, step):
        rows = pl.ds(at, step)
        row = lax.broadcasted_iota(jnp.int32, (step, PAIR), 0) + at
        bias = jnp.where(row < valid, 0.0, NEG).astype(BF16)
        q = qkv_ref[rows, :PAIR]
        k = qkv_ref[rows, PAIR : 2 * PAIR]
        kt_ref[:, rows] = k.T
        for side in range(2):
            mine = (lane // HEAD_DIM) == side
            spare = lane == (1 - side) * HEAD_DIM
            qa_ref[side, rows, :] = jnp.where(mine, q, jnp.where(spare, one, zero))
            ka_ref[side, rows, :] = jnp.where(mine, k, jnp.where(spare, bias, zero))
    dv_ref[...] = jnp.zeros_like(dv_ref)
    dk_ref[...] = jnp.zeros_like(dk_ref)
    half_rows = lax.broadcasted_iota(jnp.int32, (8, PAIR), 0)
    half_lane = lax.broadcasted_iota(jnp.int32, (8, PAIR), 1)
    chooser = jnp.where(half_lane // HEAD_DIM == half_rows, 1.0, 0.0).astype(BF16)

    def body(block, _):
        rows = pl.ds(pl.multiple_of(block * step, step), step)
        dm = dm_ref[rows, pair * PAIR : (pair + 1) * PAIR]
        product = dm.astype(F32) * mixed_ref[rows, inner * PAIR : (inner + 1) * PAIR].astype(F32)
        high = product.astype(BF16)
        low = (product - high.astype(F32)).astype(BF16)
        delta = dot_nt(chooser, high) + dot_nt(chooser, low)
        dmt = dm.T
        qt = qkv_ref[rows, :PAIR].T
        outs = []
        for side in range(2):
            head = 2 * inner + side
            part = slice(side * HEAD_DIM, (side + 1) * HEAD_DIM)
            dms = jnp.where((lane // HEAD_DIM) == side, dm, zero)
            scores = dot_nt(ka_ref[side], qa_ref[side, rows, :])
            weights = jnp.exp2(scores - lse_ref[head : head + 1, rows])
            d_weights = dot_nt(qkv_ref[:, 2 * PAIR :], dms)
            d_scores = (weights * (d_weights - delta[side : side + 1, :])).astype(BF16)
            dv_ref[part, :] += dot_nt(dmt[part, :], weights.astype(BF16))
            dk_ref[part, :] += dot_nt(qt[part, :], d_scores)
            outs.append(dot_nn(kt_ref[part, :], d_scores))
        dq = jnp.concatenate(outs, axis=0).T * (1.0 / math.sqrt(HEAD_DIM))
        dq = dq * turn_ref[rows, :PAIR] - swap_halves(dq) * turn_ref[rows, PAIR:]
        out_ref[rows, :PAIR] = dq.astype(BF16)
        return 0

    lax.fori_loop(0, length // step, body, 0)
    for at in range(0, length, step):
        rows = pl.ds(at, step)
        dk = dk_ref[:, rows].T * LN2
        dk = dk * turn_ref[rows, :PAIR] - swap_halves(dk) * turn_ref[rows, PAIR:]
        out_ref[rows, PAIR : 2 * PAIR] = dk.astype(BF16)
        out_ref[rows, 2 * PAIR :] = dv_ref[:, rows].T.astype(BF16)


def pull(info, qkv, mixed, d_mixed, lse, turn, pair, after=(), step=256):
    rows = qkv.shape[0]
    return pl.pallas_call(
        skip(functools.partial(pull_kernel, pair=pair, step=step), 6, len(after)),
        out_shape=(jax.ShapeDtypeStruct((rows, WIDE), BF16), jax.ShapeDtypeStruct((8, 128), F32)),
        in_specs=[SCALAR] + [LOCAL] * 5 + [FAR] * len(after),
        out_specs=(LOCAL, LOCAL),
        scratch_shapes=[
            pltpu.VMEM((2, rows, PAIR), BF16),
            pltpu.VMEM((2, rows, PAIR), BF16),
            pltpu.VMEM((PAIR, rows), BF16),
            pltpu.VMEM((PAIR, rows), F32),
            pltpu.VMEM((PAIR, rows), F32),
        ],
        compiler_params=pltpu.CompilerParams(vmem_limit_bytes=LIMITS["pull"] << 20),
        cost_estimate=cost("pull"),
        name=f"pull_{pair}",
    )(info, qkv, mixed, d_mixed, lse, turn, *after)


def both_kernel(left_ref, right_ref, out_ref):
    out_ref[...] = (left_ref[...].astype(F32) + right_ref[...].astype(F32)).astype(BF16)


def both(left, right, after=()):
    return pl.pallas_call(
        skip(both_kernel, 2, len(after)),
        out_shape=jax.ShapeDtypeStruct(left.shape, BF16),
        in_specs=[LOCAL, LOCAL] + [FAR] * len(after),
        out_specs=LOCAL,
        compiler_params=pltpu.CompilerParams(vmem_limit_bytes=8 << 20),
        cost_estimate=cost("halves"),
        name="both",
    )(left, right, *after)


def swap_replica(field, bit):
    count = lax.axis_size("replica")
    return lax.ppermute(field, "replica", [(i, i ^ bit) for i in range(count)])


def swap_group(field):
    return lax.ppermute(field, "group", [(0, 1), (1, 0)])


def pick(field, index, axis):
    size = field.shape[axis] // 2
    return lax.dynamic_slice_in_dim(field, index * size, size, axis)


def in_order(mine, other, index, axis):
    return jnp.where(
        index == 0,
        jnp.concatenate([mine, other], axis=axis),
        jnp.concatenate([other, mine], axis=axis),
    )


def quarters(mine, bit):
    across = swap_replica(mine, bit)
    return mine, across, swap_replica(mine, 1), swap_replica(across, 1)


def add_low(left, right):
    return (left.astype(F32) + right.astype(F32)).astype(BF16)


def hold(value, *others):
    return lax.optimization_barrier((value, others))[0]


def further_bits():
    bits = [4, 12]
    bit = 16
    while bit < lax.axis_size("replica"):
        bits.append(bit)
        bit *= 2
    return bits


def on_device(tokens, lengths, w_qkv, w_out, gain_one, w_in, w_down, gain_two, cotangent):
    rows = tokens.shape[1]
    group = lax.axis_index("group")
    replica = lax.axis_index("replica")
    core = replica % 2
    second = (replica // 2) % 2
    at = (replica // 4 + replica // 8) % 2
    info = jnp.stack([lengths[0], group, core, second, at]).astype(jnp.int32)
    cos_rows, sin_rows = angle_tables(rows)
    turn = jnp.asarray(np.concatenate([cos_rows, sin_rows], axis=1))

    field = tokens[0]
    cot = cotangent[0]
    qkv, mixed, lse, full = [None] * 6, [None] * 3, [None] * 3, [None] * 3
    far0 = swap_group(pack_first(info, w_qkv, gain_one[None]))
    send, send_a, send_b = pack(info, w_qkv, w_out, w_in, w_down, gain_two[None])
    far0, send = lax.optimization_barrier((far0, send))
    far1 = swap_group(send)
    qkv[0], qkv[1], full[0], lse[0], mixed[0], h1 = attend(
        info, field, gain_one[None], w_qkv, (far0, swap_replica(far0, 1)), turn, 0
    )
    lse[0], send_a, far1 = lax.optimization_barrier((lse[0], send_a, far1))
    far_a = swap_group(send_a)
    near1 = swap_replica(far1, 1)
    near1, send_b = lax.optimization_barrier((near1, send_b))
    far_b = swap_group(send_b)
    qkv[2], qkv[3], full[1], lse[1], mixed[1] = attend(
        info, h1, None, w_qkv, (far1, near1), turn, 1, (lse[0],)
    )
    lse[1], far_a = lax.optimization_barrier((lse[1], far_a))
    far_c = swap_replica(far_a, 2)
    near_a = swap_replica(far_a, 1)
    qkv[4], qkv[5], full[2], lse[2], mixed[2] = attend(
        info, h1, None, w_qkv, (far1, near1), turn, 2, (lse[1],)
    )
    lse[2], far_b, far_c = lax.optimization_barrier((lse[2], far_b, far_c))
    parts_rest = (far_b, swap_replica(far_b, 1), far_a, near_a, far_c, swap_replica(far_c, 1))
    output, d_x1, dx_low, d_mixed, h2, act, d_up = middle(
        info, field, mixed, cot, gain_two[None], w_out, w_in, w_down, parts_rest
    )
    mine = core.astype(jnp.int32)[None]
    theirs = 1 - mine

    def tug(pair, *after):
        return pull(
            info, qkv[pair], mixed[pair // 2], d_mixed, lse[pair // 2], turn, pair, after
        )

    d_qkv = [None] * 6
    a_send, token = early_in(theirs, h2, d_up)
    a_in = swap_replica(a_send, 1)
    b_send, token = early_rest(theirs, act, cot, mixed, dx_low, (token,))
    b_in = swap_replica(b_send, 1)
    a_mine, token = early_in(mine, h2, d_up, (token,))
    a_away, a_here = halves(a_mine, a_in, group, 0)
    a_in = swap_group(a_away)
    b_mine, token = early_rest(mine, act, cot, mixed, dx_low, (a_away,))
    b_away, b_here = halves(b_mine, b_in, second, 1)
    b_in = swap_replica(b_away, 2)

    d_qkv[0], token = tug(0, b_away)
    d_qkv[1], token = tug(1, token)
    a_away, a_here = halves(a_here[0], a_in[0], second, 0, (token,))
    a_in = swap_replica(a_away, 2)
    b_away, b_here = halves(b_here, b_in, group, 0, (a_away,))
    b_in = swap_group(b_away)
    d_qkv[2], token = tug(2, b_away)
    d_qkv[3], token = tug(3, token)
    early_mine = jnp.concatenate([a_here, b_here[0]], axis=0)
    early_in_sum = jnp.concatenate([a_in, b_in[0]], axis=0)
    bits = further_bits()
    l_send, token = late(theirs, h1, d_qkv[:4], (token,))
    l_in = swap_replica(l_send, 1)
    l_mine, token = late(mine, h1, d_qkv[:4], (token,))
    l_away, l_here = halves(l_mine, l_in, group, 0)
    l_in = swap_group(l_away)
    token = l_away
    e_away, e_here = halves(early_mine, early_in_sum, at, 0, (token,))
    e_in = swap_replica(e_away, bits[0])
    token = e_away
    d_qkv[4], token = tug(4, token)
    e_sum = both(e_here, e_in, (token,))
    e_in = swap_replica(e_sum, bits[1])
    token = e_sum
    d_qkv[5], token = tug(5, token)
    m_send, token = late(theirs, h1, d_qkv[4:], (token,))
    m_in = swap_replica(m_send, 1)
    l_away, l_here = halves(l_here[0], l_in[0], at, 0, (token,))
    l_in = swap_replica(l_away, bits[0])
    token = l_away
    m_mine, token = late(mine, h1, d_qkv[4:], (token,))
    m_away, m_here = halves(m_mine, m_in, group, 0)
    m_in = swap_group(m_away)
    token = m_away

    def across(total, todo):
        for bit in todo:
            total = add_low(total, swap_replica(total, bit))
        return total

    grad_tokens, token = last(
        info, field, gain_one[None], far0[w_qkv.shape[0] :], d_qkv, full, d_x1, (token,)
    )
    l_sum = add_low(l_here, l_in)
    l_in = swap_replica(l_sum, 2)
    e_sum = across(add_low(e_sum, e_in), bits[2:])
    e_back = swap_replica(e_sum, bits[0])
    m_here, m_in, e_sum, e_back, l_sum, l_in, _ = lax.optimization_barrier(
        (m_here, m_in, e_sum, e_back, l_sum, l_in, token)
    )
    m_sum = across(both(m_here[0], m_in[0], (token,)), bits + [2])
    e_parts = quarters(in_order(e_sum, e_back, at, 0), 2)
    l_parts = quarters(across(add_low(l_sum, l_in), bits[1:]), bits[0])
    m_parts = (m_sum, swap_replica(m_sum, 1))
    grad_in, grad_out, grad_down, grad_two = spread_early(
        info, e_parts, w_in, gain_two[None], w_down.shape[0]
    )
    grad_qkv, grad_one = spread_late(info, l_parts, m_parts, w_qkv, gain_one[None], (grad_two,))
    return (
        output[None],
        grad_tokens[None],
        grad_qkv,
        grad_out,
        grad_one,
        grad_in,
        grad_down,
        grad_two,
    )


def solution(mesh):
    both = P(("group", "replica"), None, None)
    rows = P("group", None)
    vector = P("group")
    return jax.shard_map(
        on_device,
        mesh=mesh,
        in_specs=(both, P(("group", "replica")), rows, rows, vector, rows, rows, vector, both),
        out_specs=(both, both, rows, rows, vector, rows, rows, vector),
        check_vma=False,
    )
```

```python
import functools
import math

import jax
import jax.numpy as jnp
import numpy as np
from jax import lax
from jax.experimental import pallas as pl
from jax.experimental.pallas import tpu as pltpu
from jax.sharding import PartitionSpec as P

HEADS = 12
HEAD_DIM = 64
theta_base = 160000.0
norm_eps = 1e-05
LOG2E = 1.4426950408889634
LN2 = 0.6931471805599453
F32 = jnp.float32
BF16 = jnp.bfloat16
PAIR = 2 * HEAD_DIM
GROUP_HEADS = 4
SPAN = GROUP_HEADS * HEAD_DIM
WIDE = 3 * PAIR
NEG = -1e30
LOCAL = pl.BlockSpec(memory_space=pltpu.VMEM)
SCALAR = pl.BlockSpec(memory_space=pltpu.SMEM)
FAR = pl.BlockSpec(memory_space=pl.ANY)
STORED = pl.BlockSpec(memory_space=pltpu.HBM)


def dot_nn(a, b):
    return lax.dot_general(a, b, (((1,), (0,)), ((), ())), preferred_element_type=F32)


def dot_nt(a, b):
    return lax.dot_general(a, b, (((1,), (1,)), ((), ())), preferred_element_type=F32)


def dot_tn(a, b):
    return lax.dot_general(a, b, (((0,), (0,)), ((), ())), preferred_element_type=F32)


def angle_tables(length):
    half = HEAD_DIM // 2
    freq = np.exp(-math.log(theta_base) * 2.0 * np.arange(half, dtype=np.float64) / HEAD_DIM)
    angle = np.arange(length, dtype=np.float64)[:, None] * freq.astype(np.float32).astype(np.float64)[None]
    cosine = np.cos(angle)
    sine = np.sin(angle)
    cos_rows = np.concatenate([cosine] * 4, axis=1).astype(np.float32)
    sin_rows = np.concatenate([-sine, sine, -sine, sine], axis=1).astype(np.float32)
    return cos_rows, sin_rows


def swap_halves(field):
    half = HEAD_DIM // 2
    lane = lax.broadcasted_iota(jnp.int32, field.shape, 1)
    return jnp.where(
        (lane // half) % 2 == 0, pltpu.roll(field, PAIR - half, 1), pltpu.roll(field, half, 1)
    )


def erf_exp(u):
    return lax.erf(u * (1.0 / math.sqrt(2.0))), jnp.exp(-0.5 * u * u)


LIMITS = {"attend": 16, "middle": 24, "early_in": 8, "early_rest": 8, "pull": 12, "late": 6, "last": 12, "spread": 12}
LENGTHS = {"attend": 3, "middle": 28, "early_in": 3, "early_rest": 3, "pull": 5, "late": 2, "last": 8, "spread": 3, "halves": 1}


def cost(name):
    return pl.CostEstimate(flops=LENGTHS[name] * 500_000_000, transcendentals=0, bytes_accessed=0)


def skip(kernel, at, count):
    return lambda *refs: kernel(*refs[:at], *refs[at + count :])


def start_all(copies):
    for copy in copies:
        copy.start()


def attend_kernel(*refs, chunk, first, step):
    if first:
        (info_ref, tok_ref, gain_ref, w_ref, mine_ref, other_ref, turn_ref,
         qkva_ref, qkvb_ref, full_ref, lse_ref, mixed_ref, h_ref,
         vt_ref, qa_ref, ka_ref, s_ref, row_ref, sems) = refs
    else:
        (info_ref, h_ref, w_ref, mine_ref, other_ref, turn_ref,
         qkva_ref, qkvb_ref, full_ref, lse_ref, mixed_ref,
         vt_ref, qa_ref, ka_ref, s_ref, sems) = refs
    rows_all = h_ref.shape[0]
    own = w_ref.shape[0]
    valid = info_ref[0]
    group = info_ref[1]
    core = info_ref[2]
    there = pl.ds(pl.multiple_of(group * own, own), own)
    away = pl.ds(pl.multiple_of((1 - group) * own, own), own)
    copies = []
    for pair in range(2):
        for i in range(3):
            copies.append(
                pltpu.make_async_copy(
                    w_ref.at[:, pl.ds(i * HEADS * HEAD_DIM + chunk * SPAN + pair * PAIR, PAIR)],
                    full_ref.at[there, pl.ds(pair * WIDE + i * PAIR, PAIR)],
                    sems.at[3 * pair + i],
                )
            )
    for i, (part, side) in enumerate(((mine_ref, core), (other_ref, 1 - core))):
        copies.append(
            pltpu.make_async_copy(
                part.at[pl.ds(own if chunk == 2 else 0, own)],
                full_ref.at[away, pl.ds(pl.multiple_of(side * WIDE, WIDE), WIDE)],
                sems.at[6 + i],
            )
        )
    if first:
        copies.append(pltpu.make_async_copy(mine_ref.at[pl.ds(own, 16)], row_ref, sems.at[8]))
    start_all(copies)
    if first:
        copies[-1].wait()
        copies = copies[:-1]
        gain_own = gain_ref[...].astype(F32)
        gain_away = row_ref[0:1, :].astype(F32)
        gain = jnp.where(
            group == 0,
            jnp.concatenate([gain_own, gain_away], axis=1),
            jnp.concatenate([gain_away, gain_own], axis=1),
        )

        def normalize(block, _):
            rows = pl.ds(pl.multiple_of(block * step, step), step)
            field = tok_ref[rows, :].astype(F32)
            center = field - jnp.mean(field, axis=1, keepdims=True)
            spread = jnp.mean(center * center, axis=1, keepdims=True)
            h_ref[rows, :] = (center * lax.rsqrt(spread + norm_eps) * gain).astype(BF16)
            return 0

        lax.fori_loop(0, rows_all // step, normalize, 0)
    for copy in copies:
        copy.wait()
    lane = lax.broadcasted_iota(jnp.int32, (step, PAIR), 1)

    def project(block, _):
        rows = pl.ds(pl.multiple_of(block * step, step), step)
        merged = dot_nn(h_ref[rows, :], full_ref[...])
        cosine = turn_ref[rows, :PAIR]
        sine = turn_ref[rows, PAIR:]
        row = lax.broadcasted_iota(jnp.int32, (step, PAIR), 0) + block * step
        bias = jnp.where(row < valid, 0.0, NEG)
        for pair, qkv_ref in enumerate((qkva_ref, qkvb_ref)):
            left = pair * WIDE
            q = merged[:, left : left + PAIR]
            k = merged[:, left + PAIR : left + 2 * PAIR]
            v = merged[:, left + 2 * PAIR : left + WIDE].astype(BF16)
            q = (q * cosine + swap_halves(q) * sine) * (LOG2E / math.sqrt(HEAD_DIM))
            k = k * cosine + swap_halves(k) * sine
            qkv_ref[rows, :PAIR] = q.astype(BF16)
            qkv_ref[rows, PAIR : 2 * PAIR] = k.astype(BF16)
            qkv_ref[rows, 2 * PAIR :] = v
            vt_ref[pair, :, rows] = v.T
            for side in range(2):
                mine = (lane // HEAD_DIM) == side
                spare = lane == (1 - side) * HEAD_DIM
                qa_ref[2 * pair + side, rows, :] = jnp.where(
                    mine, q, jnp.where(spare, 1.0, 0.0)
                ).astype(BF16)
                ka_ref[2 * pair + side, rows, :] = jnp.where(
                    mine, k, jnp.where(spare, bias, 0.0)
                ).astype(BF16)
        return 0

    blocks = rows_all // step
    lax.fori_loop(0, blocks, project, 0)
    ones = jnp.ones((16, step), BF16)

    def score(head, block, part, slot, top):
        rows = pl.ds(pl.multiple_of(block * step, step), step)
        keys = pl.ds(part * step, step)
        scores = dot_nt(ka_ref[head, keys, :], qa_ref[head, rows, :])
        s_ref[slot, keys, :] = scores
        here = jnp.max(scores, axis=0, keepdims=True)
        return here if top is None else jnp.maximum(top, here)

    def body(block, top):
        rows = pl.ds(pl.multiple_of(block * step, step), step)
        outs = []
        for head in range(GROUP_HEADS):
            pair, side = divmod(head, 2)
            slot = head % 2
            following = (head + 1) % GROUP_HEADS
            next_block = block if head + 1 < GROUP_HEADS else jnp.minimum(block + 1, blocks - 1)
            result = jnp.zeros((HEAD_DIM + 16, step), F32)
            next_top = None
            for part in range(blocks):
                keys = pl.ds(part * step, step)
                next_top = score(following, next_block, part, 1 - slot, next_top)
                weights = jnp.exp2(s_ref[slot, keys, :] - top).astype(BF16)
                values = jnp.concatenate(
                    [vt_ref[pair, side * HEAD_DIM : (side + 1) * HEAD_DIM, keys], ones], axis=0
                )
                result += dot_nn(values, weights)
            total = result[HEAD_DIM : HEAD_DIM + 1, :]
            outs.append(result[:HEAD_DIM, :] / total)
            lse_ref[head : head + 1, rows] = top + jnp.log2(total)
            top = next_top
            if side == 1:
                mixed_ref[rows, pair * PAIR : (pair + 1) * PAIR] = (
                    jnp.concatenate(outs[-2:], axis=0).T.astype(BF16)
                )
        return top

    top = None
    for part in range(blocks):
        top = score(0, 0, part, 0, top)
    lax.fori_loop(0, blocks, body, top)


def attend(info, source, gain, w, parts, turn, chunk, after=(), step=256):
    rows = source.shape[0]
    width = 2 * w.shape[0]
    first = gain is not None
    stored = [
        ((rows, WIDE), BF16),
        ((rows, WIDE), BF16),
        ((width, 3 * SPAN), BF16),
        ((8, rows), F32),
    ]
    out_shape = [jax.ShapeDtypeStruct(*s) for s in stored]
    out_shape.append(jax.ShapeDtypeStruct((rows, SPAN), BF16))
    scratch = [
        pltpu.VMEM((SPAN // PAIR, PAIR, rows), BF16),
        pltpu.VMEM((GROUP_HEADS, rows, PAIR), BF16),
        pltpu.VMEM((GROUP_HEADS, rows, PAIR), BF16),
        pltpu.VMEM((2, rows, step), F32),
    ]
    inputs = [info, source]
    specs = [SCALAR, LOCAL]
    if first:
        out_shape.append(jax.ShapeDtypeStruct((rows, width), BF16))
        scratch.append(pltpu.VMEM((16, WIDE), BF16))
        inputs.append(gain)
        specs.append(LOCAL)
    inputs += [w, *parts, turn]
    specs += [FAR, FAR, FAR, LOCAL]
    kernel = functools.partial(attend_kernel, chunk=chunk, first=first, step=step)
    kernel = skip(kernel, len(inputs), len(after))
    inputs += after
    specs += [FAR] * len(after)
    scratch.append(pltpu.SemaphoreType.DMA((9,)))
    return pl.pallas_call(
        kernel,
        out_shape=tuple(out_shape),
        in_specs=specs,
        out_specs=tuple([LOCAL] * len(out_shape)),
        scratch_shapes=scratch,
        compiler_params=pltpu.CompilerParams(vmem_limit_bytes=LIMITS["attend"] << 20),
        cost_estimate=cost("attend"),
        name=f"attend_{chunk}",
    )(*inputs)


def middle_kernel(
    info_ref, tok_ref, mix0_ref, mix1_ref, mix2_ref, cot_ref, gain_ref,
    wo_ref, wi_ref, wd_ref, *refs, step,
):
    parts, refs = refs[:6], refs[6:]
    (out_ref, dx_ref, dxl_ref, dm_ref, h_ref, act_ref, du_ref,
     fo_ref, fi_ref, fd_ref, row_ref, sems) = refs
    rows_all, width = tok_ref.shape
    own = wo_ref.shape[0]
    down = wd_ref.shape[0]
    half = width // 2
    hidden = fd_ref.shape[0]
    valid = info_ref[0]
    group = info_ref[1]
    core = info_ref[2]

    def at(start, size):
        return pl.ds(pl.multiple_of(start, size), size)

    copies = [
        pltpu.make_async_copy(wo_ref, fo_ref.at[at(group * own, own)], sems.at[0]),
        pltpu.make_async_copy(wi_ref, fi_ref.at[at(group * own, own)], sems.at[1]),
        pltpu.make_async_copy(wd_ref, fd_ref.at[at(group * down, down)], sems.at[2]),
        pltpu.make_async_copy(parts[0].at[pl.ds(own + down, 16)], row_ref, sems.at[3]),
    ]
    sub = own // 2
    second = info_ref[3]
    for i, side in enumerate((core, 1 - core)):
        base = 4 + 8 * i
        part = parts[i]
        copies.append(
            pltpu.make_async_copy(
                part.at[pl.ds(0, own)],
                fo_ref.at[at((1 - group) * own, own), at(side * half, half)],
                sems.at[base],
            )
        )
        copies.append(
            pltpu.make_async_copy(
                part.at[pl.ds(own, down)],
                fd_ref.at[at((1 - group) * down, down), at(side * half, half)],
                sems.at[base + 1],
            )
        )
        for k, which in enumerate((second, 1 - second)):
            part = parts[2 + 2 * k + i]
            for j in range(3):
                copies.append(
                    pltpu.make_async_copy(
                        part.at[pl.ds(j * sub, sub)],
                        fi_ref.at[
                            at((1 - group) * own + which * sub, sub), at(side * 3 * half + j * half, half)
                        ],
                        sems.at[base + 2 + 3 * k + j],
                    )
                )
    start_all(copies)
    for copy in copies:
        copy.wait()
    gain_own = gain_ref[...].astype(F32)
    gain_away = row_ref[0:1, :].astype(F32)
    gain = jnp.where(
        group == 0,
        jnp.concatenate([gain_own, gain_away], axis=1),
        jnp.concatenate([gain_away, gain_own], axis=1),
    )

    def body(block, _):
        rows = pl.ds(pl.multiple_of(block * step, step), step)
        mixed = jnp.concatenate([mix0_ref[rows, :], mix1_ref[rows, :], mix2_ref[rows, :]], axis=1)
        x1 = tok_ref[rows, :].astype(F32) + dot_nn(mixed, fo_ref[...])
        center = x1 - jnp.mean(x1, axis=1, keepdims=True)
        rate = lax.rsqrt(jnp.mean(center * center, axis=1, keepdims=True) + norm_eps)
        unit = center * rate
        h2 = (unit * gain).astype(BF16)
        h_ref[rows, :] = h2
        row = lax.broadcasted_iota(jnp.int32, (step, 1), 0) + block * step
        keep = row < valid
        up = dot_nn(h2, fi_ref[...])
        turned = up[:, :hidden]
        gate = up[:, hidden:]
        curve, bell = erf_exp(turned)
        share = 0.5 * (1.0 + curve)
        bent = turned * share
        act = (bent * gate).astype(BF16)
        act_ref[rows, :] = jnp.where(keep, act, jnp.zeros((), BF16))
        result = x1 + dot_nn(act, fd_ref[...])
        out_ref[rows, :] = jnp.where(keep, result, 0.0).astype(BF16)
        dy = jnp.where(keep, cot_ref[rows, :], jnp.zeros((), BF16))
        d_act = dot_nt(dy, fd_ref[...])
        slope = share + turned * bell * (1.0 / math.sqrt(2.0 * math.pi))
        d_up = jnp.concatenate([d_act * gate * slope, d_act * bent], axis=1).astype(BF16)
        du_ref[rows, :] = d_up
        e = dot_nt(d_up, fi_ref[...]) * gain
        d_x1 = dy.astype(F32) + rate * (
            e
            - jnp.mean(e, axis=1, keepdims=True)
            - unit * jnp.mean(e * unit, axis=1, keepdims=True)
        )
        dx_ref[rows, :] = d_x1
        low = d_x1.astype(BF16)
        dxl_ref[rows, :] = low
        dm_ref[rows, :] = dot_nt(low, fo_ref[...]).astype(BF16)
        return 0

    lax.fori_loop(0, rows_all // step, body, 0)


def middle(info, tokens, mixed, cotangent, gain, w_out, w_in, w_down, parts, step=256):
    rows, width = tokens.shape
    hidden = 2 * w_down.shape[0]
    shapes = [
        ((rows, width), BF16),
        ((rows, width), F32),
        ((rows, width), BF16),
        ((rows, width), BF16),
        ((rows, width), BF16),
        ((rows, hidden), BF16),
        ((rows, 2 * hidden), BF16),
    ]
    return pl.pallas_call(
        functools.partial(middle_kernel, step=step),
        out_shape=tuple(jax.ShapeDtypeStruct(*s) for s in shapes),
        in_specs=[SCALAR] + [LOCAL] * 6 + [FAR] * 9,
        out_specs=tuple([LOCAL] * len(shapes)),
        scratch_shapes=[
            pltpu.VMEM((width, width), BF16),
            pltpu.VMEM((width, 2 * hidden), BF16),
            pltpu.VMEM((hidden, width), BF16),
            pltpu.VMEM((16, width // 2), BF16),
            pltpu.SemaphoreType.DMA((20,)),
        ],
        compiler_params=pltpu.CompilerParams(vmem_limit_bytes=LIMITS["middle"] << 20),
        cost_estimate=cost("middle"),
        name="middle",
    )(info, tokens, *mixed, cotangent, gain, w_out, w_in, w_down, *parts)


def early_in_kernel(half_ref, h_ref, du_ref, unit_ref, token_ref):
    token_ref[...] = jnp.zeros_like(token_ref)
    own = h_ref.shape[1] // 2
    side = pl.ds(pl.multiple_of(half_ref[0] * 3 * own, 3 * own), 3 * own)
    for group in range(2):
        whole = dot_tn(h_ref[:, group * own : (group + 1) * own], du_ref[:, side]).astype(BF16)
        for j in range(3):
            unit_ref[group, j * own : (j + 1) * own, :] = whole[:, j * own : (j + 1) * own]


def early_rest_kernel(
    half_ref, act_ref, cot_ref, m0_ref, m1_ref, m2_ref, dx_ref, unit_ref, token_ref
):
    token_ref[...] = jnp.zeros_like(token_ref)
    own = dx_ref.shape[1] // 2
    down = act_ref.shape[1] // 2
    side = pl.ds(pl.multiple_of(half_ref[0] * own, own), own)
    zero = jnp.zeros((unit_ref.shape[1] - own - down, own), BF16)
    mixed = [ref[...] for ref in (m0_ref, m1_ref, m2_ref)]
    low = dx_ref[:, side]
    grad_out = jnp.concatenate([dot_tn(m, low) for m in mixed], axis=0).astype(BF16)
    grad_down = dot_tn(act_ref[...], cot_ref[:, side]).astype(BF16)
    for group in range(2):
        unit_ref[group, :own, :] = grad_out[group * own : (group + 1) * own]
        unit_ref[group, own : own + down, :] = grad_down[group * down : (group + 1) * down]
        unit_ref[group, own + down :, :] = zero


def per_half(kernel, half, inputs, shape, name, after):
    return pl.pallas_call(
        skip(kernel, 1 + len(inputs), len(after)),
        out_shape=(jax.ShapeDtypeStruct(shape, BF16), jax.ShapeDtypeStruct((8, 128), F32)),
        in_specs=[SCALAR] + [LOCAL] * len(inputs) + [FAR] * len(after),
        out_specs=(LOCAL, LOCAL),
        compiler_params=pltpu.CompilerParams(vmem_limit_bytes=LIMITS[name] << 20),
        cost_estimate=cost(name),
        name=name,
    )(half, *inputs, *after)


def early_in(half, h2, d_up, after=()):
    own = h2.shape[1] // 2
    return per_half(early_in_kernel, half, (h2, d_up), (2, 3 * own, own), "early_in", after)


def early_rest(half, act, cotangent, mixed, dx_low, after=()):
    own = dx_low.shape[1] // 2
    filled = -(-(own + act.shape[1] // 2) // 128) * 128
    return per_half(
        early_rest_kernel,
        half,
        (act, cotangent, *mixed, dx_low),
        (2, filled, own),
        "early_rest",
        after,
    )


def late_kernel(half_ref, h_ref, *refs):
    own = h_ref.shape[1] // 2
    unit_ref, token_ref = refs[-2:]
    token_ref[...] = jnp.zeros_like(token_ref)
    pairs = [
        jnp.where(half_ref[0] == 0, first[...], second[...])
        for first, second in zip(refs[:-2:2], refs[1:-2:2])
    ]
    for group in range(2):
        left = h_ref[:, group * own : (group + 1) * own]
        for i, pair in enumerate(pairs):
            unit_ref[group, i * own : (i + 1) * own, :] = dot_tn(left, pair).astype(BF16)


def late(half, h1, d_qkv, after=()):
    own = h1.shape[1] // 2
    return per_half(
        late_kernel,
        half,
        (h1, *d_qkv),
        (2, own * len(d_qkv) // 2, WIDE),
        "late",
        after,
    )


def half_of(w_ref, chunk, core):
    sides = []
    for pair in range(2):
        starts = [i * HEADS * HEAD_DIM + chunk * SPAN + pair * PAIR for i in range(3)]
        sides.append(jnp.concatenate([w_ref[:, at : at + PAIR] for at in starts], axis=1))
    return jnp.where(core == 0, sides[0], sides[1])


def pack_first_kernel(info_ref, w_ref, gain_ref, send_ref):
    own = w_ref.shape[0]
    send_ref[:own, :] = half_of(w_ref, 0, info_ref[2])
    send_ref[own:, :] = jnp.broadcast_to(gain_ref[...], (16, send_ref.shape[1]))


def pack_first(info, w_qkv, gain):
    return pl.pallas_call(
        pack_first_kernel,
        out_shape=jax.ShapeDtypeStruct((w_qkv.shape[0] + 16, WIDE), BF16),
        in_specs=[SCALAR, LOCAL, LOCAL],
        out_specs=LOCAL,
        compiler_params=pltpu.CompilerParams(vmem_limit_bytes=8 << 20),
        name="pack_first",
    )(info, w_qkv, gain)


def pack_kernel(info_ref, w_ref, wo_ref, wi_ref, wd_ref, gain_ref, s_ref, a_ref, b_ref):
    core = info_ref[2]
    own = wo_ref.shape[0]
    down = wd_ref.shape[0]
    half = wo_ref.shape[1] // 2
    s_ref[:own, :] = half_of(w_ref, 1, core)
    s_ref[own:, :] = half_of(w_ref, 2, core)

    sub = own // 2

    def part(ref, i, rows=slice(None)):
        left = i * half
        right = ref.shape[1] // 2 + i * half
        return jnp.where(core == 0, ref[rows, left : left + half], ref[rows, right : right + half])

    b_ref[:own, :] = part(wo_ref, 0)
    b_ref[own : own + down, :] = part(wd_ref, 0)
    b_ref[own + down :, :] = jnp.broadcast_to(gain_ref[...], (16, half))
    for j in range(3):
        rows = pl.ds(pl.multiple_of(info_ref[3] * sub, sub), sub)
        a_ref[j * sub : (j + 1) * sub, :] = part(wi_ref, j, rows)


def pack(info, w_qkv, w_out, w_in, w_down, gain):
    own = w_qkv.shape[0]
    wide = WIDE
    return pl.pallas_call(
        pack_kernel,
        out_shape=(
            jax.ShapeDtypeStruct((2 * own, wide), BF16),
            jax.ShapeDtypeStruct((own // 2 * 3, wide), BF16),
            jax.ShapeDtypeStruct((own + w_down.shape[0] + 16, wide), BF16),
        ),
        in_specs=[SCALAR] + [LOCAL] * 5,
        out_specs=(LOCAL,) * 3,
        compiler_params=pltpu.CompilerParams(vmem_limit_bytes=12 << 20),
        name="pack",
    )(info, w_qkv, w_out, w_in, w_down, gain)


def halves_kernel(at_ref, mine_ref, in_ref, away_ref, here_ref, *, axis):
    size = here_ref.shape[axis]
    at = at_ref[0]

    def part(ref, index):
        start = pl.multiple_of(index * size, size)
        if axis == 0:
            return ref[pl.ds(start, size)].astype(F32)
        return ref[:, pl.ds(start, size)].astype(F32)

    away_ref[...] = (part(mine_ref, 1 - at) + part(in_ref, 1 - at)).astype(BF16)
    here_ref[...] = (part(mine_ref, at) + part(in_ref, at)).astype(BF16)


def halves(mine, received, at, axis, after=()):
    shape = list(mine.shape)
    shape[axis] //= 2
    out = jax.ShapeDtypeStruct(tuple(shape), BF16)
    return pl.pallas_call(
        skip(functools.partial(halves_kernel, axis=axis), 3, len(after)),
        out_shape=(out, out),
        in_specs=[SCALAR, LOCAL, LOCAL] + [FAR] * len(after),
        out_specs=(LOCAL, LOCAL),
        compiler_params=pltpu.CompilerParams(vmem_limit_bytes=8 << 20),
        cost_estimate=cost("halves"),
        name="halves",
    )(at.astype(jnp.int32)[None], mine, received, *after)


def last_kernel(info_ref, tok_ref, gain_ref, away_ref, *refs, step):
    d_refs, (w0_ref, w1_ref, w2_ref, dx_ref, out_ref, token_ref) = refs[:6], refs[6:]
    token_ref[...] = jnp.zeros_like(token_ref)
    group = info_ref[1]
    gain_own = gain_ref[...].astype(F32)
    gain_away = away_ref[0:1, :].astype(F32)
    gain = jnp.where(
        group == 0,
        jnp.concatenate([gain_own, gain_away], axis=1),
        jnp.concatenate([gain_away, gain_own], axis=1),
    )

    def body(block, _):
        rows = pl.ds(pl.multiple_of(block * step, step), step)
        field = tok_ref[rows, :].astype(F32)
        center = field - jnp.mean(field, axis=1, keepdims=True)
        rate = lax.rsqrt(jnp.mean(center * center, axis=1, keepdims=True) + norm_eps)
        unit = center * rate
        e = jnp.zeros(field.shape, F32)
        for chunk, w_ref in enumerate((w0_ref, w1_ref, w2_ref)):
            pairs = [d_refs[2 * chunk + i][rows, :] for i in range(2)]
            e += dot_nt(jnp.concatenate(pairs, axis=1), w_ref[...])
        e *= gain
        out_ref[rows, :] = dx_ref[rows, :] + rate * (
            e
            - jnp.mean(e, axis=1, keepdims=True)
            - unit * jnp.mean(e * unit, axis=1, keepdims=True)
        )
        return 0

    lax.fori_loop(0, tok_ref.shape[0] // step, body, 0)


def last(info, tokens, gain, away, d_qkv, full, d_x1, after=(), step=256):
    return pl.pallas_call(
        skip(functools.partial(last_kernel, step=step), 14, len(after)),
        out_shape=(jax.ShapeDtypeStruct(d_x1.shape, F32), jax.ShapeDtypeStruct((8, 128), F32)),
        in_specs=[SCALAR] + [LOCAL] * 13 + [FAR] * len(after),
        out_specs=(LOCAL, LOCAL),
        compiler_params=pltpu.CompilerParams(vmem_limit_bytes=LIMITS["last"] << 20),
        cost_estimate=cost("last"),
        name="last",
    )(info, tokens, gain, away, *d_qkv, *full, d_x1, *after)


def row_of(column):
    return jnp.broadcast_to(column, (column.shape[0], 128)).T[0:1, :]


def in_place(core, second, refs):
    mine, across, other, other_across = (ref[...] for ref in refs)
    own = (jnp.where(second == 0, mine, across), jnp.where(second == 0, across, mine))
    far = (jnp.where(second == 0, other, other_across), jnp.where(second == 0, other_across, other))
    return [
        [jnp.where(core == i, a, b) for a, b in zip(own, far)] for i in range(2)
    ]


def spread_early_kernel(info_ref, *refs):
    parts, (w_ref, gain_ref, in_ref, out_ref, down_ref, dg_ref) = refs[:4], refs[4:]
    own = out_ref.shape[0]
    down = down_ref.shape[0]
    half = out_ref.shape[1] // 2
    cut = 3 * own // 2
    total = jnp.zeros((own, 1), F32)
    for i, (low, high) in enumerate(in_place(info_ref[2], info_ref[3], parts)):
        whole = jnp.concatenate([low[:cut], high[:cut]], axis=0)
        for j in range(3):
            at = (3 * i + j) * half
            part = whole[j * own : (j + 1) * own].astype(F32)
            in_ref[:, at : at + half] = part
            total += jnp.sum(part * w_ref[:, at : at + half].astype(F32), axis=1, keepdims=True)
        rest = jnp.concatenate([low[cut:], high[cut:]], axis=0)
        out_ref[:, i * half : (i + 1) * half] = rest[:own].astype(F32)
        down_ref[:, i * half : (i + 1) * half] = rest[own : own + down].astype(F32)
    dg_ref[...] = (row_of(total) / gain_ref[...].astype(F32))[0]


def spread_early(info, parts, w_in, gain, down):
    own = w_in.shape[0]
    return pl.pallas_call(
        spread_early_kernel,
        out_shape=(
            jax.ShapeDtypeStruct(w_in.shape, F32),
            jax.ShapeDtypeStruct((own, 2 * own), F32),
            jax.ShapeDtypeStruct((down, 2 * own), F32),
            jax.ShapeDtypeStruct((own,), F32),
        ),
        in_specs=[SCALAR] + [LOCAL] * 6,
        out_specs=(LOCAL,) * 4,
        compiler_params=pltpu.CompilerParams(vmem_limit_bytes=LIMITS["spread"] << 20),
        cost_estimate=cost("spread"),
        name="spread_early",
    )(info, *parts, w_in, gain)


def spread_late_kernel(info_ref, *refs):
    first, second, (w_ref, gain_ref, out_ref, dg_ref) = refs[:4], refs[4:6], refs[6:]
    core = info_ref[2]
    own = w_ref.shape[0]
    total = jnp.zeros((own, 1), F32)
    early = [jnp.concatenate(sides, axis=0) for sides in in_place(core, info_ref[4], first)]
    mine, other = (ref[...] for ref in second)
    final = [jnp.where(core == 0, mine, other), jnp.where(core == 0, other, mine)]
    for chunk in range(3):
        start = own if chunk == 1 else 0
        for side, whole in enumerate(final if chunk == 2 else early):
            for i in range(3):
                at = i * HEADS * HEAD_DIM + chunk * SPAN + side * PAIR
                part = whole[start : start + own, i * PAIR : (i + 1) * PAIR].astype(F32)
                out_ref[:, at : at + PAIR] = part
                total += jnp.sum(part * w_ref[:, at : at + PAIR].astype(F32), axis=1, keepdims=True)
    dg_ref[...] = (row_of(total) / gain_ref[...].astype(F32))[0]


def spread_late(info, first, second, w_qkv, gain, after=()):
    own = w_qkv.shape[0]
    return pl.pallas_call(
        skip(spread_late_kernel, 9, len(after)),
        out_shape=(jax.ShapeDtypeStruct(w_qkv.shape, F32), jax.ShapeDtypeStruct((own,), F32)),
        in_specs=[SCALAR] + [LOCAL] * 8 + [FAR] * len(after),
        out_specs=(LOCAL, LOCAL),
        compiler_params=pltpu.CompilerParams(vmem_limit_bytes=LIMITS["spread"] << 20),
        cost_estimate=cost("spread"),
        name="spread_late",
    )(info, *first, *second, w_qkv, gain, *after)


def pull_kernel(
    info_ref, qkv_ref, mixed_ref, dm_ref, lse_ref, turn_ref, out_ref, token_ref,
    qa_ref, ka_ref, kt_ref, dv_ref, dk_ref, *, pair, step,
):
    length = qkv_ref.shape[0]
    valid = info_ref[0]
    lane = lax.broadcasted_iota(jnp.int32, (step, PAIR), 1)
    one = jnp.ones((), BF16)
    zero = jnp.zeros((), BF16)
    token_ref[...] = jnp.zeros_like(token_ref)
    inner = pair % 2
    for at in range(0, length, step):
        rows = pl.ds(at, step)
        row = lax.broadcasted_iota(jnp.int32, (step, PAIR), 0) + at
        bias = jnp.where(row < valid, 0.0, NEG).astype(BF16)
        q = qkv_ref[rows, :PAIR]
        k = qkv_ref[rows, PAIR : 2 * PAIR]
        kt_ref[:, rows] = k.T
        for side in range(2):
            mine = (lane // HEAD_DIM) == side
            spare = lane == (1 - side) * HEAD_DIM
            qa_ref[side, rows, :] = jnp.where(mine, q, jnp.where(spare, one, zero))
            ka_ref[side, rows, :] = jnp.where(mine, k, jnp.where(spare, bias, zero))
    dv_ref[...] = jnp.zeros_like(dv_ref)
    dk_ref[...] = jnp.zeros_like(dk_ref)
    half_rows = lax.broadcasted_iota(jnp.int32, (8, PAIR), 0)
    half_lane = lax.broadcasted_iota(jnp.int32, (8, PAIR), 1)
    chooser = jnp.where(half_lane // HEAD_DIM == half_rows, 1.0, 0.0).astype(BF16)

    def body(block, _):
        rows = pl.ds(pl.multiple_of(block * step, step), step)
        dm = dm_ref[rows, pair * PAIR : (pair + 1) * PAIR]
        product = dm.astype(F32) * mixed_ref[rows, inner * PAIR : (inner + 1) * PAIR].astype(F32)
        high = product.astype(BF16)
        low = (product - high.astype(F32)).astype(BF16)
        delta = dot_nt(chooser, high) + dot_nt(chooser, low)
        dmt = dm.T
        qt = qkv_ref[rows, :PAIR].T
        outs = []
        for side in range(2):
            head = 2 * inner + side
            part = slice(side * HEAD_DIM, (side + 1) * HEAD_DIM)
            dms = jnp.where((lane // HEAD_DIM) == side, dm, zero)
            scores = dot_nt(ka_ref[side], qa_ref[side, rows, :])
            weights = jnp.exp2(scores - lse_ref[head : head + 1, rows])
            d_weights = dot_nt(qkv_ref[:, 2 * PAIR :], dms)
            d_scores = (weights * (d_weights - delta[side : side + 1, :])).astype(BF16)
            dv_ref[part, :] += dot_nt(dmt[part, :], weights.astype(BF16))
            dk_ref[part, :] += dot_nt(qt[part, :], d_scores)
            outs.append(dot_nn(kt_ref[part, :], d_scores))
        dq = jnp.concatenate(outs, axis=0).T * (1.0 / math.sqrt(HEAD_DIM))
        dq = dq * turn_ref[rows, :PAIR] - swap_halves(dq) * turn_ref[rows, PAIR:]
        out_ref[rows, :PAIR] = dq.astype(BF16)
        return 0

    lax.fori_loop(0, length // step, body, 0)
    for at in range(0, length, step):
        rows = pl.ds(at, step)
        dk = dk_ref[:, rows].T * LN2
        dk = dk * turn_ref[rows, :PAIR] - swap_halves(dk) * turn_ref[rows, PAIR:]
        out_ref[rows, PAIR : 2 * PAIR] = dk.astype(BF16)
        out_ref[rows, 2 * PAIR :] = dv_ref[:, rows].T.astype(BF16)


def pull(info, qkv, mixed, d_mixed, lse, turn, pair, after=(), step=256):
    rows = qkv.shape[0]
    return pl.pallas_call(
        skip(functools.partial(pull_kernel, pair=pair, step=step), 6, len(after)),
        out_shape=(jax.ShapeDtypeStruct((rows, WIDE), BF16), jax.ShapeDtypeStruct((8, 128), F32)),
        in_specs=[SCALAR] + [LOCAL] * 5 + [FAR] * len(after),
        out_specs=(LOCAL, LOCAL),
        scratch_shapes=[
            pltpu.VMEM((2, rows, PAIR), BF16),
            pltpu.VMEM((2, rows, PAIR), BF16),
            pltpu.VMEM((PAIR, rows), BF16),
            pltpu.VMEM((PAIR, rows), F32),
            pltpu.VMEM((PAIR, rows), F32),
        ],
        compiler_params=pltpu.CompilerParams(vmem_limit_bytes=LIMITS["pull"] << 20),
        cost_estimate=cost("pull"),
        name=f"pull_{pair}",
    )(info, qkv, mixed, d_mixed, lse, turn, *after)


def both_kernel(left_ref, right_ref, out_ref):
    out_ref[...] = (left_ref[...].astype(F32) + right_ref[...].astype(F32)).astype(BF16)


def both(left, right, after=()):
    return pl.pallas_call(
        skip(both_kernel, 2, len(after)),
        out_shape=jax.ShapeDtypeStruct(left.shape, BF16),
        in_specs=[LOCAL, LOCAL] + [FAR] * len(after),
        out_specs=LOCAL,
        compiler_params=pltpu.CompilerParams(vmem_limit_bytes=8 << 20),
        cost_estimate=cost("halves"),
        name="both",
    )(left, right, *after)


def swap_replica(field, bit):
    count = lax.axis_size("replica")
    return lax.ppermute(field, "replica", [(i, i ^ bit) for i in range(count)])


def swap_group(field):
    return lax.ppermute(field, "group", [(0, 1), (1, 0)])


def pick(field, index, axis):
    size = field.shape[axis] // 2
    return lax.dynamic_slice_in_dim(field, index * size, size, axis)


def in_order(mine, other, index, axis):
    return jnp.where(
        index == 0,
        jnp.concatenate([mine, other], axis=axis),
        jnp.concatenate([other, mine], axis=axis),
    )


def quarters(mine, bit):
    across = swap_replica(mine, bit)
    return mine, across, swap_replica(mine, 1), swap_replica(across, 1)


def add_low(left, right):
    return (left.astype(F32) + right.astype(F32)).astype(BF16)


def hold(value, *others):
    return lax.optimization_barrier((value, others))[0]


def further_bits():
    bits = [4, 12]
    bit = 16
    while bit < lax.axis_size("replica"):
        bits.append(bit)
        bit *= 2
    return bits


def on_device(tokens, lengths, w_qkv, w_out, gain_one, w_in, w_down, gain_two, cotangent):
    rows = tokens.shape[1]
    group = lax.axis_index("group")
    replica = lax.axis_index("replica")
    core = replica % 2
    second = (replica // 2) % 2
    at = (replica // 4 + replica // 8) % 2
    info = jnp.stack([lengths[0], group, core, second, at]).astype(jnp.int32)
    cos_rows, sin_rows = angle_tables(rows)
    turn = jnp.asarray(np.concatenate([cos_rows, sin_rows], axis=1))

    field = tokens[0]
    cot = cotangent[0]
    qkv, mixed, lse, full = [None] * 6, [None] * 3, [None] * 3, [None] * 3
    far0 = swap_group(pack_first(info, w_qkv, gain_one[None]))
    send, send_a, send_b = pack(info, w_qkv, w_out, w_in, w_down, gain_two[None])
    far0, send = lax.optimization_barrier((far0, send))
    far1 = swap_group(send)
    qkv[0], qkv[1], full[0], lse[0], mixed[0], h1 = attend(
        info, field, gain_one[None], w_qkv, (far0, swap_replica(far0, 1)), turn, 0
    )
    lse[0], send_a, far1 = lax.optimization_barrier((lse[0], send_a, far1))
    far_a = swap_group(send_a)
    near1 = swap_replica(far1, 1)
    near1, send_b = lax.optimization_barrier((near1, send_b))
    far_b = swap_group(send_b)
    qkv[2], qkv[3], full[1], lse[1], mixed[1] = attend(
        info, h1, None, w_qkv, (far1, near1), turn, 1, (lse[0],)
    )
    lse[1], far_a = lax.optimization_barrier((lse[1], far_a))
    far_c = swap_replica(far_a, 2)
    near_a = swap_replica(far_a, 1)
    qkv[4], qkv[5], full[2], lse[2], mixed[2] = attend(
        info, h1, None, w_qkv, (far1, near1), turn, 2, (lse[1],)
    )
    lse[2], far_b, far_c = lax.optimization_barrier((lse[2], far_b, far_c))
    parts_rest = (far_b, swap_replica(far_b, 1), far_a, near_a, far_c, swap_replica(far_c, 1))
    output, d_x1, dx_low, d_mixed, h2, act, d_up = middle(
        info, field, mixed, cot, gain_two[None], w_out, w_in, w_down, parts_rest
    )
    mine = core.astype(jnp.int32)[None]
    theirs = 1 - mine

    def tug(pair, *after):
        return pull(
            info, qkv[pair], mixed[pair // 2], d_mixed, lse[pair // 2], turn, pair, after
        )

    d_qkv = [None] * 6
    a_send, token = early_in(theirs, h2, d_up)
    a_in = swap_replica(a_send, 1)
    b_send, token = early_rest(theirs, act, cot, mixed, dx_low, (token,))
    b_in = swap_replica(b_send, 1)
    a_mine, token = early_in(mine, h2, d_up, (token,))
    a_away, a_here = halves(a_mine, a_in, group, 0)
    a_in = swap_group(a_away)
    b_mine, token = early_rest(mine, act, cot, mixed, dx_low, (a_away,))
    b_away, b_here = halves(b_mine, b_in, second, 1)
    b_in = swap_replica(b_away, 2)

    d_qkv[0], token = tug(0, b_away)
    d_qkv[1], token = tug(1, token)
    a_away, a_here = halves(a_here[0], a_in[0], second, 0, (token,))
    a_in = swap_replica(a_away, 2)
    b_away, b_here = halves(b_here, b_in, group, 0, (a_away,))
    b_in = swap_group(b_away)
    d_qkv[2], token = tug(2, b_away)
    d_qkv[3], token = tug(3, token)
    early_mine = jnp.concatenate([a_here, b_here[0]], axis=0)
    early_in_sum = jnp.concatenate([a_in, b_in[0]], axis=0)
    bits = further_bits()
    l_send, token = late(theirs, h1, d_qkv[:4], (token,))
    l_in = swap_replica(l_send, 1)
    l_mine, token = late(mine, h1, d_qkv[:4], (token,))
    l_away, l_here = halves(l_mine, l_in, group, 0)
    l_in = swap_group(l_away)
    token = l_away
    e_away, e_here = halves(early_mine, early_in_sum, at, 0, (token,))
    e_in = swap_replica(e_away, bits[0])
    token = e_away
    d_qkv[4], token = tug(4, token)
    e_sum = both(e_here, e_in, (token,))
    e_in = swap_replica(e_sum, bits[1])
    token = e_sum
    d_qkv[5], token = tug(5, token)
    m_send, token = late(theirs, h1, d_qkv[4:], (token,))
    m_in = swap_replica(m_send, 1)
    l_away, l_here = halves(l_here[0], l_in[0], at, 0, (token,))
    l_in = swap_replica(l_away, bits[0])
    token = l_away
    m_mine, token = late(mine, h1, d_qkv[4:], (token,))
    m_away, m_here = halves(m_mine, m_in, group, 0)
    m_in = swap_group(m_away)
    token = m_away

    def across(total, todo):
        for bit in todo:
            total = add_low(total, swap_replica(total, bit))
        return total

    grad_tokens, token = last(
        info, field, gain_one[None], far0[w_qkv.shape[0] :], d_qkv, full, d_x1, (token,)
    )
    l_sum = add_low(l_here, l_in)
    l_in = swap_replica(l_sum, 2)
    e_sum = across(add_low(e_sum, e_in), bits[2:])
    e_back = swap_replica(e_sum, bits[0])
    m_here, m_in, e_sum, e_back, l_sum, l_in, _ = lax.optimization_barrier(
        (m_here, m_in, e_sum, e_back, l_sum, l_in, token)
    )
    m_sum = across(both(m_here[0], m_in[0], (token,)), bits + [2])
    e_parts = quarters(in_order(e_sum, e_back, at, 0), 2)
    l_parts = quarters(across(add_low(l_sum, l_in), bits[1:]), bits[0])
    m_parts = (m_sum, swap_replica(m_sum, 1))
    grad_in, grad_out, grad_down, grad_two = spread_early(
        info, e_parts, w_in, gain_two[None], w_down.shape[0]
    )
    grad_qkv, grad_one = spread_late(info, l_parts, m_parts, w_qkv, gain_one[None], (grad_two,))
    return (
        output[None],
        grad_tokens[None],
        grad_qkv,
        grad_out,
        grad_one,
        grad_in,
        grad_down,
        grad_two,
    )


def solution(mesh):
    both = P(("group", "replica"), None, None)
    rows = P("group", None)
    vector = P("group")
    return jax.shard_map(
        on_device,
        mesh=mesh,
        in_specs=(both, P(("group", "replica")), rows, rows, vector, rows, rows, vector, both),
        out_specs=(both, both, rows, rows, vector, rows, rows, vector),
        check_vma=False,
    )
```
